32 devices in a mesh: cp: 8 (over z, y), sp: 4 (over x, core).
Axes of the slice: x: 2, y: 2, z: 4, core: 2. Of those that a mesh axis runs over, the one named last changes fastest.
Arguments:
- tokens: bfloat16 [16, 2, 128, 768], P('cp', None, 'sp'), may hold values from -6 to 6
- out_grad: bfloat16 [16, 2, 128, 768], P('cp', None, 'sp'), may hold values from -6 to 6
- time_table: float32 [64, 768], replicated, may hold values from -6 to 6
- time_index: int32 [2, 8], replicated, may hold values from 0 to 63
- span_order: int32 [16], replicated, may hold values from 0 to 15, each once
- block_ids: int32 [2, 2048], replicated, may hold values from 0 to 7, never falling along the last dimension, each value on 1 to 384 neighbouring positions
- w_ada: bfloat16 [768, 4608], P('cp'), may hold values from -0.21875 to 0.21875
- b_ada: bfloat16 [4608], P('cp'), may hold values from -3 to 3
- w_qkv: bfloat16 [768, 2304], P('cp'), may hold values from -0.21875 to 0.21875
- w_out: bfloat16 [768, 768], P('cp'), may hold values from -0.875 to 0.875
- w_up: bfloat16 [768, 3072], P('cp'), may hold values from -0.21875 to 0.21875
- w_down: bfloat16 [3072, 768], P('cp'), may hold values from -0.109375 to 0.109375
Outputs:
- block_out: bfloat16 [16, 2, 128, 768], P('cp', None, 'sp')
- grad_tokens: float32 [16, 2, 128, 768], P('cp', None, 'sp')
- grad_w_ada: float32 [768, 4608], P('cp')
- grad_b_ada: float32 [4608], P('cp')
- grad_w_qkv: float32 [768, 2304], P('cp')
- grad_w_out: float32 [768, 768], P('cp')
- grad_w_up: float32 [768, 3072], P('cp')
- grad_w_down: float32 [3072, 768], P('cp')
The draws below stay inside these ranges and needn't reach their ends.
Inputs may be any that keep to these rules, and one draw needn't show every extreme that they name: `span_order`: a permutation of the 16 spans of a sequence; slot s lies on index s // 2 of cp. `block_ids`: never falling along a sequence; all 8 blocks occur, each with 1 to 384 tokens.
All inputs are finite; a program needn't handle non-finite values.
Results may differ from the reference program's by a relative error of at most 0.038.
Values may be sent and summed in bfloat16 or wider, within the bound.
No kernel may reach another device: no remote copies, remote signals or barrier semaphores. Data moves between devices by JAX's collectives and lax.ppermute only.
A program may use at most 192 MiB of HBM per device.

```python
import math
from functools import partial
import jax
import jax.numpy as jnp
import numpy as np
from jax import lax

D = 768
HD = 64
FF = 3072
SPAN = 128
SEQS = 2
NTIME = 64
SLOTS = 16
LEN = 2048
NBLK = 8
BLOCK_MOST = 384


def place_ends(array, own_key, low, largest):
    dims = array.shape
    place = [jax.random.randint(jax.random.fold_in(own_key, axis), (), 0, dims[axis]) for axis in range(len(dims))]
    array = array.at[tuple(place)].set(low)
    longest = dims.index(max(dims))
    place[longest] = (place[longest] + 1) % dims[longest]
    return array.at[tuple(place)].set(largest)


def levels(own_key, shape, cuts, low, largest):
    loudness, own = 1.0, jax.random.fold_in(own_key, 6)
    for axis_at, shards_of in cuts:
        draws = jnp.exp(jax.random.uniform(jax.random.fold_in(own, axis_at), (shards_of,), jnp.float32, low / len(cuts), largest / len(cuts)))
        loudness = loudness * jnp.repeat(draws, shape[axis_at] // shards_of).reshape([-1 if axis == axis_at else 1 for axis in range(len(shape))])
    return loudness


def length_profile(count, total, most, slope):
    weights = [(1 << 20) // math.isqrt(grade ** slope) + 1 for grade in range(2, count + 1)]
    surplus, given = total - most - (count - 1), [1] * (count - 1)
    while surplus > 0:
        free = [i for i in range(count - 1) if given[i] < most]
        pool, remaining = sum([weights[i] for i in free]), surplus
        for i in free:
            extra = min(most - given[i], max(1, remaining * weights[i] // pool), surplus)
            given[i] = given[i] + extra
            surplus = surplus - extra
    return np.array([most] + given)


def uneven_parts(key, count, total, bound, lean):
    if count == 2:
        one = jax.random.randint(key, (), max(1, total - bound), min(bound, total - 1) + 1)
        return jnp.stack([one, total - one])
    tallies = jnp.asarray(length_profile(count, total, bound, lean), jnp.int32)
    pairs = (count - 1) // 2
    donor, sink = tallies[1:1 + 2 * pairs:2], tallies[2:2 + 2 * pairs:2]
    margin = jnp.minimum(donor - 1, bound - sink)
    moved = jax.random.randint(jax.random.fold_in(key, 1), (pairs,), 0, 1 << 20) % (margin + 1)
    tallies = tallies.at[1:1 + 2 * pairs:2].set(donor - moved).at[2:2 + 2 * pairs:2].set(sink + moved)
    return tallies[jax.random.permutation(jax.random.fold_in(key, 2), count)]


def gaussian(rng, shape, scale, bound, pieces=(), kind=jnp.bfloat16):
    level = levels(rng, shape, pieces, -0.22, 0.18) if pieces else 1.0
    values = jax.random.normal(rng, shape, jnp.float32) * scale * level
    return jnp.minimum(jnp.maximum(values, -bound), bound).astype(kind)


def setup_inputs(seed: int = 0) -> dict:
    streams_of = jax.random.split(jax.random.key(seed), 13)
    tokens = gaussian(streams_of[0], (SLOTS, SEQS, SPAN, D), 1.0, 6.0, ((0, 8), (2, 4)))
    out_grad = gaussian(streams_of[1], (SLOTS, SEQS, SPAN, D), 1.0, 6.0, ((0, 8), (2, 4)))
    time_table = gaussian(streams_of[2], (NTIME, D), 1.0, 6.0, (), jnp.float32)
    time_index = place_ends(jax.random.randint(streams_of[3], (SEQS, NBLK), 0, NTIME), jax.random.fold_in(streams_of[3], 1), 0, NTIME - 1).astype(jnp.int32)
    span_order = jax.random.permutation(streams_of[4], SLOTS).astype(jnp.int32)
    block_ids = jax.vmap(lambda own: jnp.searchsorted(jnp.cumsum(uneven_parts(own, NBLK, LEN, BLOCK_MOST, 1)), jnp.arange(LEN), side="right"))(jax.random.split(streams_of[5], SEQS)).reshape((SEQS, LEN)).astype(jnp.int32)
    w_ada = gaussian(streams_of[6], (D, 6 * D), D ** -0.5, 0.21875, ((0, 8),))
    b_ada = gaussian(streams_of[7], (6 * D,), 0.5, 3.0, ((0, 8),))
    w_qkv = gaussian(streams_of[8], (D, 3 * D), D ** -0.5, 0.21875, ((0, 8),))
    w_out = gaussian(streams_of[9], (D, D), (D // 16) ** -0.5, 0.875, ((0, 8),))
    w_up = gaussian(streams_of[10], (D, FF), D ** -0.5, 0.21875, ((0, 8),))
    w_down = gaussian(streams_of[11], (FF, D), FF ** -0.5, 0.109375, ((0, 8),))
    return dict(tokens=tokens, out_grad=out_grad, time_table=time_table, time_index=time_index, span_order=span_order, block_ids=block_ids, w_ada=w_ada, b_ada=b_ada, w_qkv=w_qkv, w_out=w_out, w_up=w_up, w_down=w_down)


@jax.custom_vjp
def low(v):
    return lax.optimization_barrier(v.astype(jnp.bfloat16)).astype(jnp.float32)

@jax.custom_vjp
def low_back(v):
    return v

def low_keep(v):
    return (low(v), None)

def low_pass(kept, grad):
    return (grad,)

def back_keep(v):
    return (v, None)

def back_low(kept, grad):
    return (low(grad),)
low.defvjp(low_keep, low_pass)
low_back.defvjp(back_keep, back_low)
epsilon = 1e-06
masked_value = -1e+30

def matmul(left, right):
    return jnp.dot(left, right, precision=lax.Precision.HIGHEST, preferred_element_type=jnp.float32)

def layer_norm(values):
    center = values - lax.optimization_barrier(jnp.mean(values, axis=-1, keepdims=True))
    scale_inv = lax.rsqrt(lax.optimization_barrier(jnp.mean(center * center, axis=-1, keepdims=True)) + epsilon)
    return center * scale_inv

def gelu_tanh(values):
    return 0.5 * values * (1.0 + jnp.tanh(0.7978845608028654 * (values + 0.044715 * values * values * values)))

def rotary_tables(positions, head_width):
    half_width = head_width // 2
    frequency = jnp.exp(-math.log(10000.0) * 2.0 * jnp.arange(half_width, dtype=jnp.float32) / head_width)
    angles = positions.astype(jnp.float32)[..., None] * frequency
    return (jnp.cos(angles), jnp.sin(angles))

def rotate(values, cosine, sine, head_width):
    full_shape = values.shape
    halves = values.reshape(full_shape[:-1] + (full_shape[-1] // head_width, 2, head_width // 2))
    front_half = halves[..., 0, :]
    back_half = halves[..., 1, :]
    turned = jnp.stack([front_half * cosine - back_half * sine, back_half * cosine + front_half * sine], axis=-2)
    return turned.reshape(full_shape)

def attend_rows(query_rows, query_ids, key_rows, value_rows, key_ids, scale):
    scores = low_back(jnp.einsum('qhd,khd->hqk', query_rows, key_rows, precision=lax.Precision.HIGHEST) * scale)
    allowed = key_ids[None, None, :] <= query_ids[None, :, None]
    masked = jnp.where(allowed, scores, masked_value)
    row_peak = lax.optimization_barrier(jnp.max(masked, axis=-1, keepdims=True))
    exponent = jnp.where(allowed, jnp.exp(masked - row_peak), 0.0)
    probability = exponent / lax.optimization_barrier(jnp.sum(exponent, axis=-1, keepdims=True))
    return jnp.einsum('hqk,khd->qhd', low(probability), value_rows, precision=lax.Precision.HIGHEST)

def attend_sequence(query_seq, key_seq, value_seq, ids_seq, scale):
    length = query_seq.shape[0]
    block_rows = min(512, length)
    checked = jax.checkpoint(partial(attend_rows, scale=scale))
    query_blocks = query_seq.reshape((length // block_rows, block_rows) + query_seq.shape[1:])
    id_blocks = ids_seq.reshape(length // block_rows, block_rows)
    results = lax.map(lambda pair: checked(pair[0], pair[1], key_seq, value_seq, ids_seq), (query_blocks, id_blocks))
    return results.reshape(query_seq.shape)

def reference(tokens, out_grad, time_table, time_index, span_order, block_ids, w_ada, b_ada, w_qkv, w_out, w_up, w_down):
    slot_total, seq_count, span_rows, width = tokens.shape
    positions = (span_order[:, None] * span_rows + jnp.arange(span_rows, dtype=jnp.int32)[None, :]).astype(jnp.int32)
    seq_blocks = jnp.take(block_ids, positions.reshape(-1), axis=1)
    token_blocks = seq_blocks.reshape(seq_count, slot_total, span_rows).transpose(1, 0, 2)
    time_rows = time_index[jnp.arange(seq_count, dtype=jnp.int32)[None, :, None], token_blocks]
    embed = time_table.astype(jnp.float32)[time_rows].reshape(-1, width)
    cosine, sine = rotary_tables(positions, HD)
    cosine = cosine[:, None, :, None, :]
    sine = sine[:, None, :, None, :]
    scale = 1.0 / math.sqrt(HD)

    def seq_view(block):
        return block.transpose(1, 0, 2, 3).reshape(seq_count, slot_total * span_rows, width // HD, HD)

    def forward(tokens_in, ada_weight, ada_bias, qkv_weight, out_weight, up_weight, down_weight):
        flat = tokens_in.reshape(-1, width)
        cond_low = low(jax.nn.silu(embed))
        modulate = low_back(matmul(cond_low, ada_weight) + ada_bias)
        shift_one, scale_one, gate_one, shift_two, scale_two, gate_two = jnp.split(modulate, 6, axis=1)
        hidden_one = low(layer_norm(flat) * (1.0 + scale_one) + shift_one)
        projected = low_back(matmul(hidden_one, qkv_weight))
        query_rot = low_back(low(rotate(projected[:, :width].reshape(tokens_in.shape), cosine, sine, HD)))
        key_rot = low_back(low(rotate(projected[:, width:2 * width].reshape(tokens_in.shape), cosine, sine, HD)))
        value_low = low_back(low(projected[:, 2 * width:].reshape(tokens_in.shape)))
        attended = lax.map(lambda group: attend_sequence(group[0], group[1], group[2], group[3], scale), (seq_view(query_rot), seq_view(key_rot), seq_view(value_low), seq_blocks))
        attended = attended.reshape(seq_count, slot_total, span_rows, width).transpose(1, 0, 2, 3).reshape(-1, width)
        attn_low = low_back(low(attended))
        branch_one = low_back(matmul(attn_low, out_weight))
        resid_mid = flat + (1.0 + gate_one) * branch_one
        hidden_two = low(layer_norm(resid_mid) * (1.0 + scale_two) + shift_two)
        pre_act = low_back(matmul(hidden_two, up_weight))
        act_low = low(gelu_tanh(pre_act))
        branch_two = low_back(matmul(act_low, down_weight))
        return (resid_mid + (1.0 + gate_two) * branch_two).reshape(tokens_in.shape)
    result, pull = jax.vjp(forward, tokens.astype(jnp.float32), w_ada.astype(jnp.float32), b_ada.astype(jnp.float32), w_qkv.astype(jnp.float32), w_out.astype(jnp.float32), w_up.astype(jnp.float32), w_down.astype(jnp.float32))
    grads = pull(out_grad.astype(jnp.float32))
    return (result.astype(jnp.bfloat16), grads[0], grads[1], grads[2], grads[3], grads[4], grads[5], grads[6])
```

```python
import functools
import math

import jax
import jax.numpy as jnp
from jax import lax
from jax.experimental import pallas as pl
from jax.experimental.pallas import tpu as pltpu
from jax.sharding import PartitionSpec as P

HD = 64
HEADS = 3
GROUP = 3 * HD
EPS = 1e-06
MASKED = -1e30
BF = jnp.bfloat16
F32 = jnp.float32
VM = pl.BlockSpec(memory_space=pltpu.VMEM)
SM = pl.BlockSpec(memory_space=pltpu.SMEM)


def call(kernel, outs, ins, scratch=(), name=None):
    return pl.pallas_call(
        kernel,
        out_shape=[jax.ShapeDtypeStruct(shape, kind) for shape, kind in outs],
        in_specs=[SM] + [VM] * (len(ins) - 1),
        out_specs=[VM] * len(outs),
        scratch_shapes=[pltpu.VMEM(shape, kind) for shape, kind in scratch],
        compiler_params=pltpu.CompilerParams(vmem_limit_bytes=60 * 1024 * 1024),
        name=name,
    )(*ins)


def dot(a, b):
    return lax.dot_general(a, b, (((1,), (0,)), ((), ())), preferred_element_type=F32)


def dot_nt(a, b):
    return lax.dot_general(a, b, (((1,), (1,)), ((), ())), preferred_element_type=F32)


def dot_tn(a, b):
    return lax.dot_general(a, b, (((0,), (0,)), ((), ())), preferred_element_type=F32)


def normalize(x):
    center = x - jnp.mean(x, axis=-1, keepdims=True)
    inv = lax.rsqrt(jnp.mean(center * center, axis=-1, keepdims=True) + EPS)
    return center * inv, inv


def norm_back(m, n, inv):
    return inv * (
        m - jnp.mean(m, axis=-1, keepdims=True) - n * jnp.mean(m * n, axis=-1, keepdims=True)
    )


def onehot(ids_col, count):
    rows = ids_col.shape[0]
    return jnp.where(
        lax.broadcasted_iota(jnp.int32, (rows, count), 1) == ids_col, 1.0, 0.0
    ).astype(BF)


def onehot_t(ids_row, count):
    cols = ids_row.shape[1]
    return jnp.where(
        lax.broadcasted_iota(jnp.int32, (count, cols), 0) == ids_row, 1.0, 0.0
    ).astype(BF)


def turn(x, cosine, sine):
    lane = lax.broadcasted_iota(jnp.int32, cosine.shape, 1) % HD
    parts = []
    for i in range(x.shape[1] // 128):
        piece = x[:, 128 * i : 128 * (i + 1)]
        swapped = jnp.where(
            lane < HD // 2, pltpu.roll(piece, 128 - HD // 2, 1), pltpu.roll(piece, HD // 2, 1)
        )
        parts.append(piece * cosine + swapped * sine)
    return jnp.concatenate(parts, axis=1)


def turn_back(x, cosine, sine):
    lane = lax.broadcasted_iota(jnp.int32, cosine.shape, 1) % HD
    parts = []
    for i in range(x.shape[1] // 128):
        piece = x[:, 128 * i : 128 * (i + 1)]
        other = piece * sine
        swapped = jnp.where(
            lane < HD // 2, pltpu.roll(other, 128 - HD // 2, 1), pltpu.roll(other, HD // 2, 1)
        )
        parts.append(piece * cosine + swapped)
    return jnp.concatenate(parts, axis=1)


def pack_kernel(mod_rows, seqs, fast, sc, tok, cond, w_ada, bias, wq, send):
    width = tok.shape[-1]
    s = sc[1]
    slots, _, rows, _ = tok.shape
    span = slots * rows
    blocks = mod_rows // seqs
    if fast:
        first = dot(cond[...], w_ada[:, : 2 * width]) + bias[:, : 2 * width]
        at = pl.multiple_of((2 + s) * width, 128)
        rest = (dot(cond[...], w_ada[:, pl.ds(at, width)]) + bias[:, pl.ds(at, width)]).astype(BF)
    for i in range(8):
        seq, hg = i % 2, i // 2
        for slot in range(slots):
            send[i, slot * rows : (slot + 1) * rows, :] = tok[slot, seq]
        if fast:
            mine = first[seq * blocks : (seq + 1) * blocks]
            send[i, span : span + 2 * blocks, :] = jnp.concatenate(
                [mine[:, :width], mine[:, width:]], axis=0
            ).astype(BF)
            at = span + 2 * blocks
            send[i, at : at + mod_rows, :] = rest
            at = at + mod_rows
            block = jnp.concatenate(
                [
                    wq[:, t * width + hg * GROUP : t * width + (hg + 1) * GROUP]
                    for t in (0, 1, 2, 2)
                ],
                axis=1,
            )
            send[i, at:, :] = block


def qkv_kernel(blocks, span, fast, n_w, *refs):
    sc, tok, mod_one, ids, cos, sin = refs[:6]
    w_refs = refs[6 : 6 + n_w]
    q_out, kv_out, h_out, n_out, w_out_ref, one_out, rest_out = refs[6 + n_w : 13 + n_w]
    w_scr = refs[13 + n_w]
    width = tok.shape[-1]
    s = sc[1]
    if fast:
        at = span
        one = jnp.zeros((2 * blocks, width), F32)
        rest = jnp.zeros(rest_out.shape, F32)
        for i in range(8):
            one = one + tok[i, at : at + 2 * blocks, :].astype(F32)
            rest = rest + tok[i, at + 2 * blocks : at + 2 * blocks + rest.shape[0], :].astype(F32)
        rest_out[...] = rest.astype(BF)
        first = at + 2 * blocks + rest.shape[0]
        for m in range(4):
            for i in range(8):
                ref = w_refs[0] if m == 0 else w_refs[m]
                rows = tok.shape[1] - first
                off = first if m == 0 else 0
                where = pl.multiple_of(96 * i + rows * (s ^ m), 8)
                w_scr[pl.ds(where, rows), :] = ref[i, off : off + rows, : 3 * GROUP].astype(F32)
        w = w_scr[...].astype(BF)
    else:
        one = mod_one[...].astype(F32)
        rest_out[...] = jnp.zeros(rest_out.shape, BF)
        w = w_refs[0][...]
    one = one.astype(BF)
    one_out[...] = one
    w_out_ref[...] = w
    x = jnp.concatenate([tok[i, :span, :] for i in range(8)], axis=0).astype(F32)
    n, _ = normalize(x)
    sel = onehot(ids[...], blocks)
    shift = dot(sel, one[:blocks])
    scale = dot(sel, one[blocks:])
    h = (n * (1.0 + scale) + shift).astype(BF)
    h_out[...] = h
    n_out[...] = n.astype(BF)
    p = dot(h, w)
    qk = turn(p[:, : 2 * GROUP], cos[...], sin[...])
    q_out[...] = (qk[:, :GROUP].astype(BF).astype(F32) * (1.0 / math.sqrt(HD))).astype(BF)
    kv_out[...] = jnp.concatenate([qk[:, GROUP:], p[:, 2 * GROUP :]], axis=1).astype(BF)


def attend_kernel(sc, q, kv0, kv1, kv2, kv3, kid, qid, o_low, o_full, lse, scores):
    count = q.shape[0]
    part = kv0.shape[0]
    kvs = (kv0, kv1, kv2, kv3)
    step = 512
    n_step = part // step
    for h in range(HEADS):
        qh = q[:, h * HD : (h + 1) * HD]

        def one(m, g, peak):
            rows = slice(0, step) if n_step == 1 else pl.ds(pl.multiple_of(g * step, step), step)
            k = kvs[m][rows, h * HD : (h + 1) * HD]
            st = dot_nt(k, qh)
            st = jnp.where(kid[m, rows, :] <= qid[...], st, MASKED)
            at = m * part + g * step
            where = slice(at, at + step) if n_step == 1 else pl.ds(pl.multiple_of(at, step), step)
            scores[where, :] = st
            return jnp.maximum(peak, jnp.max(st, axis=0, keepdims=True))

        def two(m, g, peak, carry):
            total, acc = carry
            at = m * part + g * step
            where = slice(at, at + step) if n_step == 1 else pl.ds(pl.multiple_of(at, step), step)
            rows = slice(0, step) if n_step == 1 else pl.ds(pl.multiple_of(g * step, step), step)
            p = jnp.exp(scores[where, :] - peak)
            v = kvs[m][rows, GROUP + h * HD : GROUP + (h + 1) * HD]
            return total + jnp.sum(p, axis=0, keepdims=True), acc + dot_tn(v, p.astype(BF))

        peak = jnp.full((1, count), MASKED, F32)
        for m in range(4):
            if n_step == 1:
                peak = one(m, 0, peak)
            else:
                peak = lax.fori_loop(0, n_step, functools.partial(lambda m, g, c: one(m, g, c), m), peak)
        carry = (jnp.zeros((1, count), F32), jnp.zeros((HD, count), F32))
        for m in range(4):
            if n_step == 1:
                carry = two(m, 0, peak, carry)
            else:
                carry = lax.fori_loop(
                    0, n_step, functools.partial(lambda m, pk, g, c: two(m, g, pk, c), m, peak), carry
                )
        total, acc = carry
        o = (acc / total).T
        o_full[:, h * HD : (h + 1) * HD] = o
        o_low[:, h * HD : (h + 1) * HD] = o.astype(BF)
        lse[h : h + 1, :] = peak + jnp.log(total)


def expand_kernel(sc, rest0, rest1, rest2, rest3, ids, grad, mods, dz):
    s = sc[1]
    parts = [r[...] for r in (rest0, rest1, rest2, rest3)]
    for bit in (1, 2):
        parts = [jnp.where((s & bit) != 0, parts[i ^ bit], parts[i]) for i in range(4)]
    sel = onehot(ids[...], parts[0].shape[0])
    for i in range(4):
        mods[i] = dot(sel, parts[i])
    slots, seqs, rows, width = grad.shape
    for seq in range(seqs):
        for slot in range(slots):
            at = (seq * slots + slot) * rows
            g = grad[slot, seq].astype(F32)
            dz[at : at + rows, :] = (g * (1.0 + mods[3, at : at + rows, :])).astype(BF)


def project_kernel(n_w, *refs):
    sc, attn, tok, mods = refs[:4]
    w_refs = refs[4 : 4 + n_w]
    y_out, x_out, n_out, inv_out, h_out, w_out = refs[4 + n_w : 10 + n_w]
    width = tok.shape[-1]
    r = sc[0]
    for k in range(n_w):
        rows = w_refs[k].shape[0] if n_w == 1 else width // n_w
        at = 0 if n_w == 1 else pl.multiple_of(rows * (r ^ k), 16)
        w_out[pl.ds(at, rows), :] = w_refs[k][-rows:, :]
    full = jnp.concatenate(
        [
            jnp.concatenate([attn[2 * hg + seq] for hg in range(4)], axis=1)
            for seq in range(2)
        ],
        axis=0,
    )
    y = dot(full, w_out[...])
    y_out[...] = y
    slots, seqs, rows, _ = tok.shape
    x = jnp.concatenate(
        [tok[slot, seq] for seq in range(seqs) for slot in range(slots)], axis=0
    ).astype(F32)
    x1 = x + (1.0 + mods[0]) * y
    x_out[...] = x1
    n, inv = normalize(x1)
    n_out[...] = n
    inv_out[...] = inv
    h_out[...] = (n * (1.0 + mods[2]) + mods[1]).astype(BF)


def feed_kernel(n_w, *refs):
    sc, h0, h1, h2, h3, d0, d1, d2, d3 = refs[:9]
    w_refs = refs[9 : 9 + n_w]
    z_keep, z_send, dh_keep, dh_send, g_keep, g_send = refs[9 + n_w : 15 + n_w]
    up, down, g_up, g_down = refs[15 + n_w : 19 + n_w]
    r = sc[0]
    width = h0.shape[1]
    rows = width // n_w
    for k in range(n_w):
        at = 0 if n_w == 1 else pl.multiple_of(rows * (r ^ k), 16)
        up[pl.ds(at, rows), :] = w_refs[k][:rows, :]
        down[pl.ds(at, rows), :] = w_refs[k][rows : 2 * rows, :]
    h = jnp.concatenate([h0[...], h1[...], h2[...], h3[...]], axis=0)
    dz = jnp.concatenate([d0[...], d1[...], d2[...], d3[...]], axis=0)
    part = h0.shape[0]
    u = dot(h, up[...])
    square = u * u
    inner = 0.7978845608028654 * (u + 0.044715 * square * u)
    t = jnp.tanh(inner)
    act = (0.5 * u * (1.0 + t)).astype(BF)
    slope = 0.5 * (1.0 + t) + 0.5 * u * (1.0 - t * t) * (
        0.7978845608028654 * (1.0 + 3.0 * 0.044715 * square)
    )
    du = (dot_nt(dz, down[...]) * slope).astype(BF)
    dh = dot_nt(du, up[...]).astype(BF)
    for m in range(4):
        (dh_keep, dh_send)[m % 2][m // 2] = dh[m * part : (m + 1) * part]
    z = dot(act, down[...]).astype(BF)
    for m in range(4):
        (z_keep, z_send)[m % 2][m // 2] = z[m * part : (m + 1) * part]
    g_up[...] = dot_tn(h, du).astype(BF)
    g_down[...] = dot_tn(act, dz).astype(BF)
    if n_w == 1:
        g_keep[0, :rows, :] = g_up[...]
        g_keep[0, rows:, :] = g_down[...]
        g_send[...] = jnp.zeros(g_send.shape, BF)
    else:
        for k in range(n_w):
            at = pl.multiple_of(rows * (r ^ k), 16)
            (g_keep, g_send)[k % 2][k // 2, :rows, :] = g_up[pl.ds(at, rows), :]
            (g_keep, g_send)[k % 2][k // 2, rows:, :] = g_down[pl.ds(at, rows), :]


def middle_kernel(
    n_p, rows_total, sc, dh_keep, dh_recv, dh_far, mods, n_in, inv, y, grad, attn, w, ids_row,
    dx_out, d_out, s_out, g_keep, g_send, g_scr,
):
    r = sc[0]
    dh = (
        dh_keep[0].astype(F32) + dh_recv[0].astype(F32) + dh_far[...].astype(F32)
    )
    slots, seqs, rows, width = grad.shape
    g = jnp.concatenate(
        [grad[slot, seq] for seq in range(seqs) for slot in range(slots)], axis=0
    ).astype(F32)
    n = n_in[...]
    dx = g + norm_back(dh * (1.0 + mods[2]), n, inv[...])
    dx_out[...] = dx
    dy = (dx * (1.0 + mods[0])).astype(BF)
    d = dot_nt(dy, w[...]).astype(BF)
    span = slots * rows
    for seq in range(seqs):
        for hg in range(4):
            d_out[2 * hg + seq] = d[seq * span : (seq + 1) * span, hg * GROUP : (hg + 1) * GROUP]
    sel = onehot_t(ids_row[...], rows_total)
    s_out[0] = dot(sel, (dx * y[...]).astype(BF))
    s_out[1] = dot(sel, dh.astype(BF))
    s_out[2] = dot(sel, (dh * n).astype(BF))
    full = jnp.concatenate(
        [
            jnp.concatenate([attn[2 * hg + seq] for hg in range(4)], axis=1)
            for seq in range(2)
        ],
        axis=0,
    )
    g_scr[...] = dot_tn(full, dy).astype(BF)
    part = width // n_p
    if n_p == 1:
        g_keep[0] = g_scr[...]
        g_send[...] = jnp.zeros(g_send.shape, BF)
    else:
        for k in range(n_p):
            at = pl.multiple_of(part * (r ^ k), 16)
            (g_keep, g_send)[k % 2][k // 2] = g_scr[pl.ds(at, part), :]


def block_kernel(rows_total, sc, z_keep, z_recv, z_far, mods, x1, grad, ids_row, out, s_out):
    z = z_keep[0].astype(F32) + z_recv[0].astype(F32) + z_far[...].astype(F32)
    slots, seqs, rows, width = grad.shape
    g = jnp.concatenate(
        [grad[slot, seq] for seq in range(seqs) for slot in range(slots)], axis=0
    ).astype(F32)
    s_out[...] = dot(onehot_t(ids_row[...], rows_total), (g * z).astype(BF))
    o = (x1[...] + (1.0 + mods[3]) * z).astype(BF)
    for seq in range(seqs):
        for slot in range(slots):
            at = (seq * slots + slot) * rows
            out[slot, seq] = o[at : at + rows]


def attend_back_kernel(
    sc, q, kv0, kv1, kv2, kv3, kid, qid, o_full, lse, do,
    dq_out, keep0, keep1, send0, send1, dq_scr,
):
    count = q.shape[0]
    part = kv0.shape[0]
    kvs = (kv0, kv1, kv2, kv3)
    outs = (keep0, send0, keep1, send1)
    step = 512
    n_step = part // step
    ones = jnp.ones((8, HD), F32)
    for h in range(HEADS):
        lanes = slice(h * HD, (h + 1) * HD)
        qh = q[:, lanes]
        doh = do[:, lanes]
        prod = doh.astype(F32) * o_full[:, lanes]
        delta = lax.dot_general(
            ones, prod, (((1,), (1,)), ((), ())), precision=lax.Precision.HIGHEST,
            preferred_element_type=F32,
        )[:1]
        top = lse[h : h + 1, :]
        dq_scr[...] = jnp.zeros(dq_scr.shape, F32)

        def one(m, g):
            rows = slice(0, step) if n_step == 1 else pl.ds(pl.multiple_of(g * step, step), step)
            k = kvs[m][rows, lanes]
            v = kvs[m][rows, GROUP + h * HD : GROUP + (h + 1) * HD]
            p = jnp.where(kid[m, rows, :] <= qid[...], jnp.exp(dot_nt(k, qh) - top), 0.0)
            ds = (p * (dot_nt(v, doh) - delta)).astype(BF)
            outs[m][rows, lanes] = dot(ds, qh).astype(BF)
            outs[m][rows, GROUP + h * HD : GROUP + (h + 1) * HD] = dot(p.astype(BF), doh).astype(BF)
            dq_scr[...] += dot_tn(k, ds)

        for m in range(4):
            if n_step == 1:
                one(m, 0)
            else:

                def loop(g, c, m=m):
                    one(m, g)
                    return c

                lax.fori_loop(0, n_step, loop, 0)
        dq_out[:, lanes] = dq_scr[...].T * (1.0 / math.sqrt(HD))


def qkv_back_kernel(
    blocks, n_p, seqs, fast, sc, dq, dkv_a, dkv_b, dkv_c, h, n_in, w, one, ids_col, ids_row, cos, sin,
    dh_out, s_out, g_keep, g_send, g_scr,
):
    kv = dkv_a[...].astype(F32)
    if fast:
        kv = kv + dkv_b[...].astype(F32) + dkv_c[...].astype(F32)
    kv = kv.astype(BF).astype(F32)
    q = dq[...].astype(BF).astype(F32)
    qk = turn_back(jnp.concatenate([q, kv[:, :GROUP]], axis=1), cos[...], sin[...])
    d = jnp.concatenate([qk, kv[:, GROUP:]], axis=1).astype(BF)
    dh = dot_nt(d, w[...])
    scale = dot(onehot(ids_col[...], blocks), one[blocks:])
    m = (dh * (1.0 + scale)).astype(BF)
    part = m.shape[0] // 8
    for i in range(8):
        dh_out[i] = m[i * part : (i + 1) * part]
    sel = onehot_t(ids_row[...], blocks)
    shift_sum = dot(sel, dh.astype(BF))
    scale_sum = dot(sel, (dh * n_in[...].astype(F32)).astype(BF))
    seq = sc[2]
    for b in range(seqs):
        s_out[0, b * blocks : (b + 1) * blocks, :] = jnp.where(seq == b, shift_sum, 0.0)
        s_out[1, b * blocks : (b + 1) * blocks, :] = jnp.where(seq == b, scale_sum, 0.0)
    g_scr[...] = dot_tn(h[...], d).astype(BF)
    if fast:
        c = sc[1] & 1
        half = g_keep.shape[1]
        for i in range(8):
            g_keep[i] = g_scr[pl.ds(pl.multiple_of(2 * half * i + half * c, 16), half), :]
            g_send[i] = g_scr[pl.ds(pl.multiple_of(2 * half * i + half * (1 - c), 16), half), :]
    else:
        g_keep[0] = g_scr[...]
        g_send[...] = jnp.zeros(g_send.shape, BF)


def last_kernel(sc, m_in, tok, dx, out):
    slots, seqs, rows, width = tok.shape
    span = slots * rows
    for seq in range(seqs):
        m = m_in[seq].astype(F32)
        for hg in range(1, 4):
            m = m + m_in[2 * hg + seq].astype(F32)
        x = jnp.concatenate([tok[slot, seq] for slot in range(slots)], axis=0).astype(F32)
        n, inv = normalize(x)
        o = dx[seq * span : (seq + 1) * span, :] + norm_back(m, n, inv)
        for slot in range(slots):
            out[slot, seq] = o[slot * rows : (slot + 1) * rows]


def finish_kernel(sc, p0, p1, p2, p3, up, down, outw):
    s = sc[1]
    rows = p0.shape[0] // 3 if p0.shape[0] % 3 == 0 else 0
    width = p0.shape[1]
    parts = [p0, p1, p2, p3]
    outw[...] = p0[2 * rows :, :].astype(F32)
    for m in range(4):
        down[pl.ds(pl.multiple_of(rows * (s ^ m), 8), rows), :] = parts[m][rows : 2 * rows, :].astype(F32)
    ups = [p[:rows, :].astype(F32) for p in parts]
    for bit in (1, 2):
        ups = [jnp.where((s & bit) != 0, ups[i ^ bit], ups[i]) for i in range(4)]
    quarter = up.shape[1] // 4 // (width // rows)
    n_c = up.shape[1] // (4 * quarter)
    for c in range(n_c):
        up[:, 4 * quarter * c : 4 * quarter * (c + 1)] = jnp.concatenate(
            [u[:, quarter * c : quarter * (c + 1)] for u in ups], axis=1
        )


def swap(x, axis, k, size):
    return lax.ppermute(x, axis, [(i, i ^ k) for i in range(size)])


def gather_sp(x):
    far = swap(x, "sp", 2, 4)
    return [x, swap(x, "sp", 1, 4), far, swap(far, "sp", 1, 4)]


def body(
    tokens, out_grad, time_table, time_index, span_order, block_ids,
    w_ada, b_ada, w_qkv, w_out, w_up, w_down,
):
    slots, seqs, rows, width = tokens.shape
    cp = lax.axis_size("cp")
    fast = cp == 8
    groups = cp // 8
    r = lax.axis_index("cp")
    s = lax.axis_index("sp")
    j = r % 8
    group = r // 8
    seq = j % 2
    hg = j // 2
    span = slots * rows
    span_rows = 4 * rows
    blocks = time_index.shape[1]
    mod_rows = seqs * blocks
    part_rows = width // cp
    total_slots = slots * cp
    hidden = w_up.shape[1]
    count = 8 * span
    sc = jnp.stack([r, s, seq]).astype(jnp.int32)
    exchange_groups = None if fast else [[8 * g + i for i in range(8)] for g in range(groups)]

    def all_to_all(x):
        return lax.all_to_all(
            x, "cp", split_axis=0, concat_axis=0, tiled=True, axis_index_groups=exchange_groups
        )

    spans = span_order.astype(jnp.int32)
    pick = (spans[:, None] == jnp.arange(total_slots, dtype=jnp.int32)[None, :]).astype(BF)
    slot_ids = jnp.einsum(
        "ns,bst->bnt",
        pick,
        block_ids.reshape(seqs, total_slots, span_rows).astype(BF),
        preferred_element_type=F32,
    ).astype(jnp.int32)
    slot_ids = slot_ids.reshape(seqs, total_slots, 4, rows)
    own_seq = lax.dynamic_index_in_dim(slot_ids, seq, 0, keepdims=False)
    key_ids = jnp.stack(
        [
            lax.dynamic_index_in_dim(own_seq, s ^ m, 1, keepdims=False).reshape(-1)
            for m in range(4)
        ]
    )
    query_ids = lax.dynamic_slice_in_dim(key_ids[0], group * count, count, 0)
    own_ids = lax.dynamic_slice(
        slot_ids, (0, slots * r, s, 0), (seqs, slots, 1, rows)
    ).reshape(seqs, span)
    token_ids = (own_ids + blocks * jnp.arange(seqs, dtype=jnp.int32)[:, None]).reshape(-1)
    own_spans = lax.dynamic_slice_in_dim(spans, 8 * slots * group, 8 * slots, 0)
    positions = (
        own_spans[:, None] * span_rows + s * rows + jnp.arange(rows, dtype=jnp.int32)[None, :]
    ).reshape(-1)
    lane = jnp.arange(128, dtype=jnp.int32) % HD
    frequency = jnp.exp(
        -math.log(10000.0) * 2.0 * (lane % (HD // 2)).astype(F32) / HD
    )
    angles = positions.astype(F32)[:, None] * frequency[None, :]
    cosine = jnp.cos(angles)
    sine = jnp.where(lane < HD // 2, -1.0, 1.0)[None, :] * jnp.sin(angles)

    pick_time = (
        time_index.reshape(-1)[:, None] == jnp.arange(time_table.shape[0], dtype=jnp.int32)
    ).astype(F32)
    table_part = lax.dynamic_slice_in_dim(time_table, part_rows * r, part_rows, 1)
    cond = jax.nn.silu(
        jnp.dot(pick_time, table_part, precision=lax.Precision.HIGHEST)
    ).astype(BF)
    bias = lax.dynamic_update_slice(
        jnp.zeros((1, 6 * width), F32), b_ada.astype(F32)[None, :], (0, b_ada.shape[0] * r)
    )

    if fast:
        quarter_rows = part_rows // 4
        wq = lax.dynamic_slice(w_qkv, (quarter_rows * s, 0), (quarter_rows, 3 * width))
        extra = 2 * blocks + mod_rows + quarter_rows
    else:
        wq = w_qkv
        extra = 0
    (send,) = call(
        functools.partial(pack_kernel, mod_rows, seqs, fast),
        [((8, span + extra, width), BF)],
        [sc, tokens, cond, w_ada, bias, wq],
        name="pack",
    )
    got = all_to_all(send)
    if fast:
        w_parts = got[:, span + extra - quarter_rows :, :]
        w_list = [got] + gather_sp(w_parts)[1:]
        mod_one = got
    else:
        full_mod = lax.psum(
            jnp.dot(cond, w_ada, preferred_element_type=F32) + bias, "cp"
        )
        first = lax.dynamic_slice_in_dim(full_mod, seq * blocks, blocks, 0)
        mod_one = jnp.concatenate([first[:, :width], first[:, width : 2 * width]], axis=0)
        gathered = lax.all_gather(w_qkv, "cp", axis=0, tiled=True).reshape(width, 3, 4, GROUP)
        w_list = [
            lax.dynamic_index_in_dim(gathered, hg, 2, keepdims=False).reshape(width, 3 * GROUP)
        ]

    inner = hidden // cp // 4
    up_part = lax.dynamic_index_in_dim(
        w_up.reshape(part_rows, cp, 4, inner), s, 2, keepdims=False
    ).reshape(part_rows, cp * inner)
    down_part = lax.dynamic_slice_in_dim(w_down, inner * s, inner, 0)
    shard = jnp.concatenate([up_part, down_part, w_out], axis=0)
    if fast:
        shard, _ = lax.optimization_barrier((shard, got))
        near = [shard] + [swap(shard, "cp", 2 * m, 8) for m in (1, 2, 3)]
        pieces = []
        for m in range(4):
            pieces += [near[m], swap(near[m], "cp", 1, 8)]
        n_w = 8
    else:
        gathered = lax.all_gather(shard, "cp", axis=0, tiled=False)
        pieces = [
            jnp.concatenate(
                [
                    gathered[:, :part_rows].reshape(width, width),
                    gathered[:, part_rows : part_rows + inner].reshape(width, width),
                    gathered[:, part_rows + inner :].reshape(width, width),
                ],
                axis=0,
            )
        ]
        n_w = 1

    mod_kernel_outs = [
        ((count, GROUP), BF),
        ((count, 2 * GROUP), BF),
        ((count, width), BF),
        ((count, width), BF),
        ((width, 3 * GROUP), BF),
        ((2 * blocks, width), BF),
        ((mod_rows, width), BF),
    ]
    q, kv, h_one, n_one, w_heads, one, rest = call(
        functools.partial(qkv_kernel, blocks, span, fast, len(w_list)),
        mod_kernel_outs,
        [sc, got, mod_one, query_ids[:, None], cosine, sine] + w_list,
        scratch=[((width, 3 * GROUP), F32)],
        name="qkv",
    )
    if not fast:
        kv = lax.all_gather(
            kv, "cp", axis=0, tiled=True,
            axis_index_groups=[[8 * g + i for g in range(groups)] for i in range(8)],
        )
    kvs = gather_sp(kv)
    key_col = key_ids[:, :, None]
    query_row = query_ids[None, :]
    attn, attn_full, lse = call(
        attend_kernel,
        [((count, GROUP), BF), ((count, GROUP), F32), ((8, count), F32)],
        [sc, q] + kvs + [key_col, query_row],
        scratch=[((4 * kv.shape[0], count), F32)],
        name="attend",
    )
    if fast:
        rests = gather_sp(rest)
    else:
        tail = full_mod.astype(BF)
        rests = [
            lax.dynamic_slice_in_dim(tail, (2 + (s ^ m)) * width, width, 1) for m in range(4)
        ]
    mods, dz = call(
        expand_kernel,
        [((4, 2 * span, width), F32), ((2 * span, width), BF)],
        [sc] + rests + [token_ids[:, None], out_grad],
        name="expand",
    )
    dzs = gather_sp(dz)
    attn_tok = all_to_all(attn.reshape(8, span, GROUP))
    y, x_mid, n_two, inv_two, h_two, w_out_full = call(
        functools.partial(project_kernel, n_w),
        [
            ((2 * span, width), F32),
            ((2 * span, width), F32),
            ((2 * span, width), F32),
            ((2 * span, 1), F32),
            ((2 * span, width), BF),
            ((width, width), BF),
        ],
        [sc, attn_tok, tokens, mods] + (pieces if fast else [pieces[0][2 * width :]]),
        name="project",
    )
    hs = gather_sp(h_two)
    pair = ((2, 2 * span, width), BF)
    grads = ((max(n_w // 2, 1), 2 * width // n_w, width), BF)
    z_keep, z_send, dh_keep, dh_send, g_keep, g_send = call(
        functools.partial(feed_kernel, n_w),
        [pair, pair, pair, pair, grads, grads],
        [sc] + hs + dzs + pieces,
        scratch=[((width, width), BF)] * 4,
        name="feed",
    )

    def reduce_sp(keep, send):
        near = swap(send, "sp", 1, 4)
        both = (keep[1].astype(F32) + near[1].astype(F32)).astype(BF)
        return keep, near, swap(both, "sp", 2, 4)

    def reduce_cp(keep, send):
        near = swap(send, "cp", 1, 8)
        sums = [(keep[m].astype(F32) + near[m].astype(F32)) for m in range(4)]
        far = [swap(sums[m].astype(BF), "cp", 2 * m, 8) for m in (1, 2, 3)]
        return sums[0] + far[0].astype(F32) + far[1].astype(F32) + far[2].astype(F32)

    dh_parts = reduce_sp(dh_keep, dh_send)
    token_row = token_ids[None, :]
    g_out = ((max(n_w // 2, 1), width // n_w, width), BF)
    dx_mid, d_attn, s_mid, o_keep, o_send = call(
        functools.partial(middle_kernel, n_w, mod_rows),
        [
            ((2 * span, width), F32),
            ((8, span, GROUP), BF),
            ((3, mod_rows, width), F32),
            g_out,
            g_out,
        ],
        [sc] + list(dh_parts)
        + [mods, n_two, inv_two, y, out_grad, attn_tok, w_out_full, token_row],
        scratch=[((width, width), BF)],
        name="middle",
    )
    d_heads = all_to_all(d_attn).reshape(count, GROUP)
    z_parts = reduce_sp(z_keep, z_send)
    block_out, s_gate = call(
        functools.partial(block_kernel, mod_rows),
        [(tokens.shape, BF), ((mod_rows, width), F32)],
        [sc] + list(z_parts) + [mods, x_mid, out_grad, token_row],
        name="block",
    )
    part = kv.shape[0]
    dkv = ((part, 2 * GROUP), BF)
    dq, keep0, keep1, send0, send1 = call(
        attend_back_kernel,
        [((count, GROUP), F32), dkv, dkv, dkv, dkv],
        [sc, q] + kvs + [key_col, query_row, attn_full, lse, d_heads],
        scratch=[((HD, count), F32)],
        name="attend_back",
    )
    near0 = swap(send0, "sp", 1, 4)
    near1 = swap(send1, "sp", 1, 4)
    both = (keep1.astype(F32) + near1.astype(F32)).astype(BF)
    far = swap(both, "sp", 2, 4)
    dkv_list = [keep0, near0, far]
    if not fast:
        summed = keep0.astype(F32) + near0.astype(F32) + far.astype(F32)
        summed = lax.psum_scatter(
            summed, "cp", scatter_dimension=0, tiled=True,
            axis_index_groups=[[8 * g + i for g in range(groups)] for i in range(8)],
        ).astype(BF)
        dkv_list = [summed, summed, summed]
    g_shape = ((8, part_rows // 2, 3 * GROUP), BF) if fast else ((1, width, 3 * GROUP), BF)
    m_one, s_one, q_keep, q_send = call(
        functools.partial(qkv_back_kernel, blocks, n_w, seqs, fast),
        [((8, span, width), BF), ((2, mod_rows, width), F32), g_shape, g_shape],
        [sc, dq] + dkv_list
        + [h_one, n_one, w_heads, one, query_ids[:, None], query_row, cosine, sine],
        scratch=[((width, 3 * GROUP), BF)],
        name="qkv_back",
    )
    m_tok = all_to_all(m_one)
    (grad_in,) = call(
        last_kernel, [(tokens.shape, F32)], [sc, m_tok, tokens, dx_mid], name="last"
    )

    def reduce_all(x):
        if not fast:
            return lax.psum(x, ("cp", "sp"))
        for axis, k, size in (("sp", 1, 4), ("sp", 2, 4), ("cp", 1, 8), ("cp", 2, 8), ("cp", 4, 8)):
            x = x + swap(x, axis, k, size)
        return x

    early = reduce_all(jnp.concatenate([s_mid, s_gate[None]], axis=0))
    late = reduce_all(s_one)
    sums = jnp.concatenate([late, early], axis=0).transpose(1, 0, 2).reshape(mod_rows, 6 * width)
    grad_ada = lax.dot_general(
        cond.astype(F32), sums, (((0,), (0,)), ((), ())), precision=lax.Precision.HIGHEST
    )
    grad_bias = lax.dynamic_slice_in_dim(
        jnp.sum(sums, axis=0), b_ada.shape[0] * r, b_ada.shape[0], 0
    )

    if fast:
        feed = reduce_cp(g_keep, g_send)
        proj = reduce_cp(o_keep, o_send)
        near = swap(q_send, "sp", 1, 4)
        got_q = all_to_all((q_keep.astype(F32) + near.astype(F32)).astype(BF))
        mine = jnp.sum(
            got_q.reshape(4, 2, part_rows // 2, 3 * GROUP).astype(F32), axis=1
        )
        mine = mine.astype(BF)
        mine = (mine.astype(F32) + swap(mine, "sp", 2, 4).astype(F32)).astype(BF)
        other = swap(mine, "sp", 1, 4)
        low = jnp.where(s % 2 == 0, mine, other)
        high = jnp.where(s % 2 == 0, other, mine)
        both = jnp.concatenate([low, high], axis=1)
        grad_qkv = (
            both.reshape(4, part_rows, 3, GROUP).transpose(1, 2, 0, 3).reshape(part_rows, 3 * width)
        ).astype(F32)
        for k in (1, 2):
            proj_low = proj.astype(BF)
            proj = proj_low.astype(F32) + swap(proj_low, "sp", k, 4).astype(F32)
        proj_low = proj
    else:
        feed = jnp.concatenate(
            [
                lax.psum_scatter(g_keep[0, :width].astype(F32), "cp", scatter_dimension=0, tiled=True),
                lax.psum_scatter(g_keep[0, width:].astype(F32), "cp", scatter_dimension=0, tiled=True),
            ],
            axis=0,
        )
        proj = lax.psum_scatter(o_keep[0].astype(F32), "cp", scatter_dimension=0, tiled=True)
        proj_low = lax.psum(proj, "sp")
        own = lax.psum_scatter(q_keep[0].astype(F32), "sp", scatter_dimension=1, tiled=True)
        placed = lax.dynamic_update_slice(
            jnp.zeros((4, width, 3 * GROUP // 4), F32), own[None], (hg, 0, 0)
        )
        placed = lax.psum_scatter(placed, "cp", scatter_dimension=1, tiled=True)
        whole = lax.all_gather(placed, "sp", axis=2, tiled=True)
        grad_qkv = (
            whole.reshape(4, part_rows, 3, GROUP).transpose(1, 2, 0, 3).reshape(part_rows, 3 * width)
        )
    if fast:
        shares = gather_sp(jnp.concatenate([feed, proj_low], axis=0).astype(BF))
        grad_up, grad_down, grad_out = call(
            finish_kernel,
            [
                ((part_rows, hidden), F32),
                ((hidden // cp, width), F32),
                ((part_rows, width), F32),
            ],
            [sc] + shares,
            name="finish",
        )
    else:
        shares = lax.all_gather(feed, "sp", axis=0, tiled=False)
        grad_up = (
            shares[:, :part_rows]
            .reshape(4, part_rows, cp, inner)
            .transpose(1, 2, 0, 3)
            .reshape(part_rows, hidden)
        )
        grad_down = shares[:, part_rows:].reshape(hidden // cp, width)
        grad_out = proj_low
    return (
        block_out, grad_in, grad_ada, grad_bias, grad_qkv, grad_out, grad_up, grad_down,
    )


def solution(mesh):
    rows = P("cp", None, "sp", None)
    shard = P("cp", None)
    return jax.shard_map(
        body,
        mesh=mesh,
        in_specs=(
            rows, rows, P(), P(), P(), P(), shard, P("cp"), shard, shard, shard, shard,
        ),
        out_specs=(rows, rows, shard, P("cp"), shard, shard, shard, shard),
        check_vma=False,
    )
```

```python
import functools
import math

import jax
import jax.numpy as jnp
from jax import lax
from jax.experimental import pallas as pl
from jax.experimental.pallas import tpu as pltpu
from jax.sharding import PartitionSpec as P

HD = 64
HEADS = 3
GROUP = 3 * HD
EPS = 1e-06
MASKED = -1e30
BF = jnp.bfloat16
F32 = jnp.float32
VM = pl.BlockSpec(memory_space=pltpu.VMEM)
SM = pl.BlockSpec(memory_space=pltpu.SMEM)


def call(kernel, outs, ins, scratch=(), name=None):
    return pl.pallas_call(
        kernel,
        out_shape=[jax.ShapeDtypeStruct(shape, kind) for shape, kind in outs],
        in_specs=[SM] + [VM] * (len(ins) - 1),
        out_specs=[VM] * len(outs),
        scratch_shapes=[pltpu.VMEM(shape, kind) for shape, kind in scratch],
        compiler_params=pltpu.CompilerParams(vmem_limit_bytes=60 * 1024 * 1024),
        name=name,
    )(*ins)


def dot(a, b):
    return lax.dot_general(a, b, (((1,), (0,)), ((), ())), preferred_element_type=F32)


def dot_nt(a, b):
    return lax.dot_general(a, b, (((1,), (1,)), ((), ())), preferred_element_type=F32)


def dot_tn(a, b):
    return lax.dot_general(a, b, (((0,), (0,)), ((), ())), preferred_element_type=F32)


def normalize(x):
    center = x - jnp.mean(x, axis=-1, keepdims=True)
    inv = lax.rsqrt(jnp.mean(center * center, axis=-1, keepdims=True) + EPS)
    return center * inv, inv


def norm_back(m, n, inv):
    return inv * (
        m - jnp.mean(m, axis=-1, keepdims=True) - n * jnp.mean(m * n, axis=-1, keepdims=True)
    )


def onehot(ids_col, count):
    rows = ids_col.shape[0]
    return jnp.where(
        lax.broadcasted_iota(jnp.int32, (rows, count), 1) == ids_col, 1.0, 0.0
    ).astype(BF)


def onehot_t(ids_row, count):
    cols = ids_row.shape[1]
    return jnp.where(
        lax.broadcasted_iota(jnp.int32, (count, cols), 0) == ids_row, 1.0, 0.0
    ).astype(BF)


def turn(x, cosine, sine):
    lane = lax.broadcasted_iota(jnp.int32, cosine.shape, 1) % HD
    parts = []
    for i in range(x.shape[1] // 128):
        piece = x[:, 128 * i : 128 * (i + 1)]
        swapped = jnp.where(
            lane < HD // 2, pltpu.roll(piece, 128 - HD // 2, 1), pltpu.roll(piece, HD // 2, 1)
        )
        parts.append(piece * cosine + swapped * sine)
    return jnp.concatenate(parts, axis=1)


def turn_back(x, cosine, sine):
    lane = lax.broadcasted_iota(jnp.int32, cosine.shape, 1) % HD
    parts = []
    for i in range(x.shape[1] // 128):
        piece = x[:, 128 * i : 128 * (i + 1)]
        other = piece * sine
        swapped = jnp.where(
            lane < HD // 2, pltpu.roll(other, 128 - HD // 2, 1), pltpu.roll(other, HD // 2, 1)
        )
        parts.append(piece * cosine + swapped)
    return jnp.concatenate(parts, axis=1)


def pack_kernel(mod_rows, seqs, fast, sc, tok, cond, w_ada, bias, wq, w_up, w_down, send, shard):
    width = tok.shape[-1]
    s = sc[1]
    slots, _, rows, _ = tok.shape
    span = slots * rows
    blocks = mod_rows // seqs
    if fast:
        first = dot(cond[...], w_ada[:, : 2 * width]) + bias[:, : 2 * width]
        at = pl.multiple_of((2 + s) * width, 128)
        rest = (dot(cond[...], w_ada[:, pl.ds(at, width)]) + bias[:, pl.ds(at, width)]).astype(BF)
    for i in range(8):
        seq, hg = i % 2, i // 2
        for slot in range(slots):
            send[i, slot * rows : (slot + 1) * rows, :] = tok[slot, seq]
        if fast:
            mine = first[seq * blocks : (seq + 1) * blocks]
            send[i, span : span + 2 * blocks, :] = jnp.concatenate(
                [mine[:, :width], mine[:, width:]], axis=0
            ).astype(BF)
            at = span + 2 * blocks
            send[i, at : at + mod_rows, :] = rest
            at = at + mod_rows
            block = jnp.concatenate(
                [
                    wq[:, t * width + hg * GROUP : t * width + (hg + 1) * GROUP]
                    for t in (0, 1, 2, 2)
                ],
                axis=1,
            )
            send[i, at:, :] = block
    inner = w_down.shape[0] // 4
    n_c = w_up.shape[1] // (4 * inner)
    rows = w_up.shape[0]
    shard[rows:, :] = w_down[pl.ds(pl.multiple_of(inner * s, 8), inner), :]
    for own in range(4):

        @pl.when(s == own)
        def _(own=own):
            shard[:rows, :] = jnp.concatenate(
                [
                    w_up[:, (4 * c + own) * inner : (4 * c + own + 1) * inner]
                    for c in range(n_c)
                ],
                axis=1,
            )


def qkv_kernel(blocks, span, fast, n_w, *refs):
    sc, tok, mod_one, ids, cos, sin = refs[:6]
    w_refs = refs[6 : 6 + n_w]
    q_out, kv_out, h_out, n_out, w_out_ref, one_out = refs[6 + n_w : 12 + n_w]
    w_scr = refs[12 + n_w]
    width = tok.shape[-1]
    s = sc[1]
    if fast:
        at = span
        one = jnp.zeros((2 * blocks, width), F32)
        for i in range(8):
            one = one + tok[i, at : at + 2 * blocks, :].astype(F32)
        rows = width // 32
        for m in range(4):
            for i in range(8):
                where = pl.multiple_of(4 * rows * i + rows * (s ^ m), 8)
                w_scr[pl.ds(where, rows), :] = w_refs[m][
                    i * rows : (i + 1) * rows, : 3 * GROUP
                ].astype(F32)
        w = w_scr[...].astype(BF)
    else:
        one = mod_one[...].astype(F32)
        w = w_refs[0][...]
    one = one.astype(BF)
    one_out[...] = one
    w_out_ref[...] = w
    x = jnp.concatenate([tok[i, :span, :] for i in range(8)], axis=0).astype(F32)
    n, _ = normalize(x)
    sel = onehot(ids[...], blocks)
    shift = dot(sel, one[:blocks])
    scale = dot(sel, one[blocks:])
    h = (n * (1.0 + scale) + shift).astype(BF)
    h_out[...] = h
    n_out[...] = n.astype(BF)
    p = dot(h, w)
    qk = turn(p[:, : 2 * GROUP], cos[...], sin[...])
    q_out[...] = (qk[:, :GROUP].astype(BF).astype(F32) * (1.0 / math.sqrt(HD))).astype(BF)
    kv_out[...] = jnp.concatenate([qk[:, GROUP:], p[:, 2 * GROUP :]], axis=1).astype(BF)


def attend_kernel(sc, q, kv0, kv1, kv2, kv3, kid, qid, o_low, o_full, lse, scores):
    count = q.shape[0]
    part = kv0.shape[0]
    kvs = (kv0, kv1, kv2, kv3)
    step = 512
    n_step = part // step
    for h in range(HEADS):
        qh = q[:, h * HD : (h + 1) * HD]

        def one(m, g, peak):
            rows = slice(0, step) if n_step == 1 else pl.ds(pl.multiple_of(g * step, step), step)
            k = kvs[m][rows, h * HD : (h + 1) * HD]
            st = dot_nt(k, qh)
            st = jnp.where(kid[m, rows, :] <= qid[...], st, MASKED)
            at = m * part + g * step
            where = slice(at, at + step) if n_step == 1 else pl.ds(pl.multiple_of(at, step), step)
            scores[where, :] = st
            return jnp.maximum(peak, jnp.max(st, axis=0, keepdims=True))

        def two(m, g, peak, carry):
            total, acc = carry
            at = m * part + g * step
            where = slice(at, at + step) if n_step == 1 else pl.ds(pl.multiple_of(at, step), step)
            rows = slice(0, step) if n_step == 1 else pl.ds(pl.multiple_of(g * step, step), step)
            p = jnp.exp(scores[where, :] - peak)
            v = kvs[m][rows, GROUP + h * HD : GROUP + (h + 1) * HD]
            return total + jnp.sum(p, axis=0, keepdims=True), acc + dot_tn(v, p.astype(BF))

        peak = jnp.full((1, count), MASKED, F32)
        for m in range(4):
            if n_step == 1:
                peak = one(m, 0, peak)
            else:
                peak = lax.fori_loop(0, n_step, functools.partial(lambda m, g, c: one(m, g, c), m), peak)
        carry = (jnp.zeros((1, count), F32), jnp.zeros((HD, count), F32))
        for m in range(4):
            if n_step == 1:
                carry = two(m, 0, peak, carry)
            else:
                carry = lax.fori_loop(
                    0, n_step, functools.partial(lambda m, pk, g, c: two(m, g, pk, c), m, peak), carry
                )
        total, acc = carry
        o = (acc / total).T
        o_full[:, h * HD : (h + 1) * HD] = o
        o_low[:, h * HD : (h + 1) * HD] = o.astype(BF)
        lse[h : h + 1, :] = peak + jnp.log(total)


def expand_kernel(sc, rest0, rest1, rest2, rest3, ids, g0, g1, g2, g3, mods, dz):
    s = sc[1]
    parts = [r[...] for r in (rest0, rest1, rest2, rest3)]
    for bit in (1, 2):
        parts = [jnp.where((s & bit) != 0, parts[i ^ bit], parts[i]) for i in range(4)]
    slots, seqs, rows, width = g0.shape
    count = slots * seqs * rows
    rest_low = parts[3]
    for i in range(3):
        mods[i] = dot(onehot(ids[:count, :], rest_low.shape[0]), parts[i])
    gate = dot(onehot(ids[...], rest_low.shape[0]), rest_low)
    mods[3] = gate[:count]
    for m, grad in enumerate((g0, g1, g2, g3)):
        for seq in range(seqs):
            for slot in range(slots):
                at = m * count + (seq * slots + slot) * rows
                g = grad[slot, seq].astype(F32)
                dz[at : at + rows, :] = (g * (1.0 + gate[at : at + rows])).astype(BF)


def project_kernel(n_w, sc, attn, tok, mods, weights, y_out, x_out, n_out, inv_out, h_out, w_out):
    width = tok.shape[-1]
    r = sc[0]
    rows = width // n_w
    for k in range(n_w):
        w_out[rows * k : rows * (k + 1), :] = weights[k, 2 * rows :, :]
    full = jnp.concatenate(
        [
            jnp.concatenate([attn[2 * hg + seq] for hg in range(4)], axis=1)
            for seq in range(2)
        ],
        axis=0,
    )
    y = dot(full, w_out[...])
    y_out[...] = y
    slots, seqs, rows, _ = tok.shape
    x = jnp.concatenate(
        [tok[slot, seq] for seq in range(seqs) for slot in range(slots)], axis=0
    ).astype(F32)
    x1 = x + (1.0 + mods[0]) * y
    x_out[...] = x1
    n, inv = normalize(x1)
    n_out[...] = n
    inv_out[...] = inv
    h_out[...] = (n * (1.0 + mods[2]) + mods[1]).astype(BF)


def feed_kernel(
    n_w, sc, h0, h1, h2, h3, dz_in, weights,
    z_keep, z_send, dh_keep, dh_send, h_all, act_out, du_out, up, down,
):
    width = h0.shape[1]
    rows = width // n_w
    for k in range(n_w):
        up[rows * k : rows * (k + 1), :] = weights[k, :rows, :]
        down[rows * k : rows * (k + 1), :] = weights[k, rows : 2 * rows, :]
    h = jnp.concatenate([h0[...], h1[...], h2[...], h3[...]], axis=0)
    dz = dz_in[...]
    part = h0.shape[0]
    u = dot(h, up[...])
    square = u * u
    inner = 0.7978845608028654 * (u + 0.044715 * square * u)
    t = jnp.tanh(inner)
    act = (0.5 * u * (1.0 + t)).astype(BF)
    slope = 0.5 * (1.0 + t) + 0.5 * u * (1.0 - t * t) * (
        0.7978845608028654 * (1.0 + 3.0 * 0.044715 * square)
    )
    du = (dot_nt(dz, down[...]) * slope).astype(BF)
    dh = dot_nt(du, up[...]).astype(BF)
    for m in range(4):
        (dh_keep, dh_send)[m % 2][m // 2] = dh[m * part : (m + 1) * part]
    z = dot(act, down[...]).astype(BF)
    for m in range(4):
        (z_keep, z_send)[m % 2][m // 2] = z[m * part : (m + 1) * part]
    h_all[...] = h
    act_out[...] = act
    du_out[...] = du


def feed_grad_kernel(n_w, sc, h, dz, act, du, grads):
    rows = h.shape[1] // n_w
    up = dot_tn(h[...], du[...]).astype(BF)
    down = dot_tn(act[...], dz[...]).astype(BF)
    for k in range(n_w):
        grads[k, :rows, :] = up[rows * k : rows * (k + 1)]
        grads[k, rows:, :] = down[rows * k : rows * (k + 1)]


def middle_kernel(
    sc, dh_keep, dh_recv, dh_far, mods, n_in, inv, grad, w, dx_out, dh_out, dy_out, d_out
):
    dh = (
        dh_keep[0].astype(F32) + dh_recv[0].astype(F32) + dh_far[...].astype(F32)
    )
    slots, seqs, rows, width = grad.shape
    g = jnp.concatenate(
        [grad[slot, seq] for seq in range(seqs) for slot in range(slots)], axis=0
    ).astype(F32)
    dx = g + norm_back(dh * (1.0 + mods[2]), n_in[...], inv[...])
    dx_out[...] = dx
    dh_out[...] = dh
    dy = (dx * (1.0 + mods[0])).astype(BF)
    dy_out[...] = dy
    d = dot_nt(dy, w[...]).astype(BF)
    span = slots * rows
    for seq in range(seqs):
        for hg in range(4):
            d_out[2 * hg + seq] = d[seq * span : (seq + 1) * span, hg * GROUP : (hg + 1) * GROUP]


def middle_grad_kernel(
    n_p, rows_total, sc, dx, dh, dy, n_in, y, attn, ids_row, s_out, g_keep, g_send, g_scr
):
    r = sc[0]
    sel = onehot_t(ids_row[...], rows_total)
    s_out[0] = dot(sel, (dx[...] * y[...]).astype(BF))
    s_out[1] = dot(sel, dh[...].astype(BF))
    s_out[2] = dot(sel, (dh[...] * n_in[...]).astype(BF))
    full = jnp.concatenate(
        [
            jnp.concatenate([attn[2 * hg + seq] for hg in range(4)], axis=1)
            for seq in range(2)
        ],
        axis=0,
    )
    g_scr[...] = dot_tn(full, dy[...]).astype(BF)
    part = g_scr.shape[0] // n_p
    if n_p == 1:
        g_keep[0] = g_scr[...]
        g_send[...] = jnp.zeros(g_send.shape, BF)
    else:
        for k in range(n_p):
            at = pl.multiple_of(part * (r ^ k), 16)
            (g_keep, g_send)[k % 2][k // 2] = g_scr[pl.ds(at, part), :]


def block_kernel(rows_total, sc, z_keep, z_recv, z_far, mods, x1, grad, ids_row, out, s_out):
    z = z_keep[0].astype(F32) + z_recv[0].astype(F32) + z_far[...].astype(F32)
    slots, seqs, rows, width = grad.shape
    g = jnp.concatenate(
        [grad[slot, seq] for seq in range(seqs) for slot in range(slots)], axis=0
    ).astype(F32)
    s_out[...] = dot(onehot_t(ids_row[...], rows_total), (g * z).astype(BF))
    o = (x1[...] + (1.0 + mods[3]) * z).astype(BF)
    for seq in range(seqs):
        for slot in range(slots):
            at = (seq * slots + slot) * rows
            out[slot, seq] = o[at : at + rows]


def attend_back_kernel(
    sc, q, kv0, kv1, kv2, kv3, kid, qid, o_full, lse, do,
    dq_out, keep0, keep1, send0, send1, dq_scr,
):
    count = q.shape[0]
    part = kv0.shape[0]
    kvs = (kv0, kv1, kv2, kv3)
    outs = (keep0, send0, keep1, send1)
    step = 512
    n_step = part // step
    ones = jnp.ones((8, HD), F32)
    for h in range(HEADS):
        lanes = slice(h * HD, (h + 1) * HD)
        qh = q[:, lanes]
        doh = do[:, lanes]
        prod = doh.astype(F32) * o_full[:, lanes]
        delta = lax.dot_general(
            ones, prod, (((1,), (1,)), ((), ())), precision=lax.Precision.HIGHEST,
            preferred_element_type=F32,
        )[:1]
        top = lse[h : h + 1, :]
        dq_scr[...] = jnp.zeros(dq_scr.shape, F32)

        def one(m, g):
            rows = slice(0, step) if n_step == 1 else pl.ds(pl.multiple_of(g * step, step), step)
            k = kvs[m][rows, lanes]
            v = kvs[m][rows, GROUP + h * HD : GROUP + (h + 1) * HD]
            p = jnp.where(kid[m, rows, :] <= qid[...], jnp.exp(dot_nt(k, qh) - top), 0.0)
            ds = (p * (dot_nt(v, doh) - delta)).astype(BF)
            outs[m][rows, lanes] = dot(ds, qh).astype(BF)
            outs[m][rows, GROUP + h * HD : GROUP + (h + 1) * HD] = dot(p.astype(BF), doh).astype(BF)
            dq_scr[...] += dot_tn(k, ds)

        for m in range(4):
            if n_step == 1:
                one(m, 0)
            else:

                def loop(g, c, m=m):
                    one(m, g)
                    return c

                lax.fori_loop(0, n_step, loop, 0)
        dq_out[:, lanes] = dq_scr[...].T * (1.0 / math.sqrt(HD))


def qkv_back_kernel(
    blocks, fast, sc, dq, dkv_a, dkv_b, dkv_c, w, one, ids_col, cos, sin, m_out, dh_out, d_out
):
    kv = dkv_a[...].astype(F32)
    if fast:
        kv = kv + dkv_b[...].astype(F32) + dkv_c[...].astype(F32)
    kv = kv.astype(BF).astype(F32)
    q = dq[...].astype(BF).astype(F32)
    qk = turn_back(jnp.concatenate([q, kv[:, :GROUP]], axis=1), cos[...], sin[...])
    d = jnp.concatenate([qk, kv[:, GROUP:]], axis=1).astype(BF)
    d_out[...] = d
    dh = dot_nt(d, w[...])
    dh_out[...] = dh.astype(BF)
    scale = dot(onehot(ids_col[...], blocks), one[blocks:])
    m = (dh * (1.0 + scale)).astype(BF)
    part = m.shape[0] // 8
    for i in range(8):
        m_out[i] = m[i * part : (i + 1) * part]


def qkv_grad_kernel(
    blocks, seqs, fast, sc, d, dh, h, n_in, ids_row, s_out, g_keep, g_send, g_scr
):
    sel = onehot_t(ids_row[...], blocks)
    shift_sum = dot(sel, dh[...])
    scale_sum = dot(sel, (dh[...].astype(F32) * n_in[...].astype(F32)).astype(BF))
    seq = sc[2]
    for b in range(seqs):
        s_out[0, b * blocks : (b + 1) * blocks, :] = jnp.where(seq == b, shift_sum, 0.0)
        s_out[1, b * blocks : (b + 1) * blocks, :] = jnp.where(seq == b, scale_sum, 0.0)
    g_scr[...] = dot_tn(h[...], d[...]).astype(BF)
    if fast:
        c = sc[1] & 1
        half = g_keep.shape[1]
        for i in range(8):
            g_keep[i] = g_scr[pl.ds(pl.multiple_of(2 * half * i + half * c, 16), half), :]
            g_send[i] = g_scr[pl.ds(pl.multiple_of(2 * half * i + half * (1 - c), 16), half), :]
    else:
        g_keep[0] = g_scr[...]
        g_send[...] = jnp.zeros(g_send.shape, BF)


def last_kernel(sc, m_in, tok, dx, out):
    slots, seqs, rows, width = tok.shape
    span = slots * rows
    for seq in range(seqs):
        m = m_in[seq].astype(F32)
        for hg in range(1, 4):
            m = m + m_in[2 * hg + seq].astype(F32)
        x = jnp.concatenate([tok[slot, seq] for slot in range(slots)], axis=0).astype(F32)
        n, inv = normalize(x)
        o = dx[seq * span : (seq + 1) * span, :] + norm_back(m, n, inv)
        for slot in range(slots):
            out[slot, seq] = o[slot * rows : (slot + 1) * rows]


def finish_kernel(sc, p0, p1, p2, p3, up, down, outw):
    s = sc[1]
    rows = p0.shape[0] // 3 if p0.shape[0] % 3 == 0 else 0
    width = p0.shape[1]
    parts = [p0, p1, p2, p3]
    outw[...] = p0[2 * rows :, :].astype(F32)
    for m in range(4):
        down[pl.ds(pl.multiple_of(rows * (s ^ m), 8), rows), :] = parts[m][rows : 2 * rows, :].astype(F32)
    ups = [p[:rows, :].astype(F32) for p in parts]
    for bit in (1, 2):
        ups = [jnp.where((s & bit) != 0, ups[i ^ bit], ups[i]) for i in range(4)]
    quarter = up.shape[1] // 4 // (width // rows)
    n_c = up.shape[1] // (4 * quarter)
    for c in range(n_c):
        up[:, 4 * quarter * c : 4 * quarter * (c + 1)] = jnp.concatenate(
            [u[:, quarter * c : quarter * (c + 1)] for u in ups], axis=1
        )


def swap(x, axis, k, size):
    return lax.ppermute(x, axis, [(i, i ^ k) for i in range(size)])


def after(x, *others):
    return lax.optimization_barrier((x,) + others)[0]


def gather_sp(x):
    far = swap(x, "sp", 2, 4)
    return [x, swap(x, "sp", 1, 4), far, swap(far, "sp", 1, 4)]


def body(
    tokens, out_grad, time_table, time_index, span_order, block_ids,
    w_ada, b_ada, w_qkv, w_out, w_up, w_down,
):
    slots, seqs, rows, width = tokens.shape
    cp = lax.axis_size("cp")
    fast = cp == 8
    groups = cp // 8
    r = lax.axis_index("cp")
    s = lax.axis_index("sp")
    j = r % 8
    group = r // 8
    seq = j % 2
    hg = j // 2
    span = slots * rows
    span_rows = 4 * rows
    blocks = time_index.shape[1]
    mod_rows = seqs * blocks
    part_rows = width // cp
    total_slots = slots * cp
    hidden = w_up.shape[1]
    count = 8 * span
    sc = jnp.stack([r, s, seq]).astype(jnp.int32)
    exchange_groups = None if fast else [[8 * g + i for i in range(8)] for g in range(groups)]

    def all_to_all(x):
        return lax.all_to_all(
            x, "cp", split_axis=0, concat_axis=0, tiled=True, axis_index_groups=exchange_groups
        )

    spans = span_order.astype(jnp.int32)
    pick = (spans[:, None] == jnp.arange(total_slots, dtype=jnp.int32)[None, :]).astype(BF)
    slot_ids = jnp.einsum(
        "ns,bst->bnt",
        pick,
        block_ids.reshape(seqs, total_slots, span_rows).astype(BF),
        preferred_element_type=F32,
    ).astype(jnp.int32)
    slot_ids = slot_ids.reshape(seqs, total_slots, 4, rows)
    own_seq = lax.dynamic_index_in_dim(slot_ids, seq, 0, keepdims=False)
    key_ids = jnp.stack(
        [
            lax.dynamic_index_in_dim(own_seq, s ^ m, 1, keepdims=False).reshape(-1)
            for m in range(4)
        ]
    )
    query_ids = lax.dynamic_slice_in_dim(key_ids[0], group * count, count, 0)
    here = lax.dynamic_slice_in_dim(slot_ids, slots * r, slots, 1)
    all_ids = jnp.concatenate(
        [
            (
                lax.dynamic_index_in_dim(here, s ^ m, 2, keepdims=False).reshape(seqs, span)
                + blocks * jnp.arange(seqs, dtype=jnp.int32)[:, None]
            ).reshape(-1)
            for m in range(4)
        ]
    )
    token_ids = all_ids[: seqs * span]
    own_spans = lax.dynamic_slice_in_dim(spans, 8 * slots * group, 8 * slots, 0)
    positions = (
        own_spans[:, None] * span_rows + s * rows + jnp.arange(rows, dtype=jnp.int32)[None, :]
    ).reshape(-1)
    lane = jnp.arange(128, dtype=jnp.int32) % HD
    frequency = jnp.exp(
        -math.log(10000.0) * 2.0 * (lane % (HD // 2)).astype(F32) / HD
    )
    angles = positions.astype(F32)[:, None] * frequency[None, :]
    cosine = jnp.cos(angles)
    sine = jnp.where(lane < HD // 2, -1.0, 1.0)[None, :] * jnp.sin(angles)

    pick_time = (
        time_index.reshape(-1)[:, None] == jnp.arange(time_table.shape[0], dtype=jnp.int32)
    ).astype(F32)
    table_part = lax.dynamic_slice_in_dim(time_table, part_rows * r, part_rows, 1)
    cond = jax.nn.silu(
        jnp.dot(pick_time, table_part, precision=lax.Precision.HIGHEST)
    ).astype(BF)
    bias = lax.dynamic_update_slice(
        jnp.zeros((1, 6 * width), F32), b_ada.astype(F32)[None, :], (0, b_ada.shape[0] * r)
    )

    if fast:
        quarter_rows = part_rows // 4
        wq = lax.dynamic_slice(w_qkv, (quarter_rows * s, 0), (quarter_rows, 3 * width))
        extra = 2 * blocks + mod_rows + quarter_rows
    else:
        wq = w_qkv
        extra = 0
    inner = hidden // cp // 4
    if fast:
        send, shard = call(
            functools.partial(pack_kernel, mod_rows, seqs, fast),
            [((8, span + extra, width), BF), ((part_rows + inner, width), BF)],
            [sc, tokens, cond, w_ada, bias, wq, w_up, w_down],
            name="pack",
        )
    else:
        send = jnp.broadcast_to(
            tokens.transpose(1, 0, 2, 3).reshape(1, seqs, span, width), (4, seqs, span, width)
        ).reshape(8, span, width)
        up_part = lax.dynamic_index_in_dim(
            w_up.reshape(part_rows, cp, 4, inner), s, 2, keepdims=False
        ).reshape(part_rows, cp * inner)
        down_part = lax.dynamic_slice_in_dim(w_down, inner * s, inner, 0)
        shard = jnp.concatenate([up_part, down_part], axis=0)
    grad_parts = gather_sp(out_grad)
    got = after(all_to_all(send), *grad_parts)
    if fast:
        w_own = got[:, span + extra - quarter_rows :, :].reshape(8 * quarter_rows, width)
        rest_own = jnp.sum(
            got[:, span + 2 * blocks : span + 2 * blocks + mod_rows, :].astype(F32), axis=0
        ).astype(BF)
        both = gather_sp(jnp.concatenate([w_own, rest_own], axis=0))
        w_list = both
        rests = [x[8 * quarter_rows :] for x in both]
        mod_one = got
    else:
        full_mod = lax.psum(
            jnp.dot(cond, w_ada, preferred_element_type=F32) + bias, "cp"
        )
        first = lax.dynamic_slice_in_dim(full_mod, seq * blocks, blocks, 0)
        mod_one = jnp.concatenate([first[:, :width], first[:, width : 2 * width]], axis=0)
        gathered = lax.all_gather(w_qkv, "cp", axis=0, tiled=True).reshape(width, 3, 4, GROUP)
        w_list = [
            lax.dynamic_index_in_dim(gathered, hg, 2, keepdims=False).reshape(width, 3 * GROUP)
        ]

    n_w = 8 if fast else 1
    weights = lax.all_gather(
        jnp.concatenate([shard, w_out], axis=0), "cp", axis=0, tiled=False
    )
    if not fast:
        weights = jnp.concatenate(
            [
                weights[:, at : at + part_rows].reshape(width, width)
                for at in (0, part_rows, 2 * part_rows)
            ],
            axis=0,
        )[None]

    mod_kernel_outs = [
        ((count, GROUP), BF),
        ((count, 2 * GROUP), BF),
        ((count, width), BF),
        ((count, width), BF),
        ((width, 3 * GROUP), BF),
        ((2 * blocks, width), BF),
    ]
    q, kv, h_one, n_one, w_heads, one = call(
        functools.partial(qkv_kernel, blocks, span, fast, len(w_list)),
        mod_kernel_outs,
        [sc, got, mod_one, query_ids[:, None], cosine, sine] + w_list,
        scratch=[((width, 3 * GROUP), F32)],
        name="qkv",
    )
    if not fast:
        kv = lax.all_gather(
            kv, "cp", axis=0, tiled=True,
            axis_index_groups=[[8 * g + i for g in range(groups)] for i in range(8)],
        )
    kvs = gather_sp(kv)
    key_col = key_ids[:, :, None]
    query_row = query_ids[None, :]
    attn, attn_full, lse = call(
        attend_kernel,
        [((count, GROUP), BF), ((count, GROUP), F32), ((8, count), F32)],
        [sc, q] + kvs + [key_col, query_row],
        scratch=[((4 * kv.shape[0], count), F32)],
        name="attend",
    )
    if not fast:
        tail = full_mod.astype(BF)
        rests = [
            lax.dynamic_slice_in_dim(tail, (2 + (s ^ m)) * width, width, 1) for m in range(4)
        ]
    mods, dz = call(
        expand_kernel,
        [((4, 2 * span, width), F32), ((8 * span, width), BF)],
        [sc] + rests + [all_ids[:, None]] + [after(grad_parts[0], attn)]
        + grad_parts[1:],
        name="expand",
    )
    attn_tok = all_to_all(attn.reshape(8, span, GROUP))
    y, x_mid, n_two, inv_two, h_two, w_out_full = call(
        functools.partial(project_kernel, n_w),
        [
            ((2 * span, width), F32),
            ((2 * span, width), F32),
            ((2 * span, width), F32),
            ((2 * span, 1), F32),
            ((2 * span, width), BF),
            ((width, width), BF),
        ],
        [sc, attn_tok, tokens, mods, weights],
        name="project",
    )
    hs = gather_sp(h_two)
    pair = ((2, 2 * span, width), BF)
    tall = ((8 * span, width), BF)
    z_keep, z_send, dh_keep, dh_send, h_all, act, du = call(
        functools.partial(feed_kernel, n_w),
        [pair, pair, pair, pair, tall, tall, tall],
        [sc] + hs + [dz, weights],
        scratch=[((width, width), BF)] * 2,
        name="feed",
    )
    (g_feed,) = call(
        functools.partial(feed_grad_kernel, n_w),
        [((n_w, 2 * width // n_w, width), BF)],
        [sc, h_all, dz, act, du],
        name="feed_grad",
    )
    if fast:
        feed = lax.psum_scatter(g_feed, "cp", scatter_dimension=0, tiled=False)
    else:
        feed = jnp.concatenate(
            [
                lax.psum_scatter(
                    g_feed[0, at : at + width].astype(F32), "cp", scatter_dimension=0, tiled=True
                )
                for at in (0, width)
            ],
            axis=0,
        )

    def reduce_sp(keep, send):
        near = swap(send, "sp", 1, 4)
        both = (keep[1].astype(F32) + near[1].astype(F32)).astype(BF)
        return keep, near, swap(both, "sp", 2, 4)

    def first_sum(keep, near):
        return [(keep[m].astype(F32) + near[m].astype(F32)).astype(BF) for m in range(4)]

    def spread(sums):
        return [sums[0]] + [swap(sums[m], "cp", 2 * m, 8) for m in (1, 2, 3)]

    def total(parts):
        return sum(p.astype(F32) for p in parts)

    dh_parts = reduce_sp(dh_keep, dh_send)
    token_row = token_ids[None, :]
    g_out = ((max(n_w // 2, 1), width // n_w, width), BF)
    wide = ((2 * span, width), F32)
    dx_mid, dh_two, dy, d_attn = call(
        middle_kernel,
        [wide, wide, ((2 * span, width), BF), ((8, span, GROUP), BF)],
        [sc] + list(dh_parts)
        + [mods, n_two, after(inv_two, g_feed), out_grad, w_out_full],
        name="middle",
    )
    s_mid, o_keep, o_send = call(
        functools.partial(middle_grad_kernel, n_w, mod_rows),
        [((3, mod_rows, width), F32), g_out, g_out],
        [sc, dx_mid, dh_two, dy, n_two, y, attn_tok, token_row],
        scratch=[((width, width), BF)],
        name="middle_grad",
    )
    d_heads = all_to_all(d_attn).reshape(count, GROUP)
    if fast:
        o_near = swap(after(o_send, d_heads), "cp", 1, 8)
        d_heads = after(d_heads, s_mid, o_send, o_keep)
    z_parts = reduce_sp(after(z_keep, d_heads), after(z_send, d_heads))
    block_out, s_gate = call(
        functools.partial(block_kernel, mod_rows),
        [(tokens.shape, BF), ((mod_rows, width), F32)],
        [sc] + list(z_parts) + [mods, x_mid, out_grad, token_row],
        name="block",
    )
    part = kv.shape[0]
    dkv = ((part, 2 * GROUP), BF)
    dq, keep0, keep1, send0, send1 = call(
        attend_back_kernel,
        [((count, GROUP), F32), dkv, dkv, dkv, dkv],
        [sc, q] + kvs + [key_col, query_row, attn_full, lse, d_heads],
        scratch=[((HD, count), F32)],
        name="attend_back",
    )
    near0 = swap(send0, "sp", 1, 4)
    near1 = swap(send1, "sp", 1, 4)
    both = (keep1.astype(F32) + near1.astype(F32)).astype(BF)
    far = swap(both, "sp", 2, 4)
    dkv_list = [keep0, near0, far]
    if not fast:
        summed = keep0.astype(F32) + near0.astype(F32) + far.astype(F32)
        summed = lax.psum_scatter(
            summed, "cp", scatter_dimension=0, tiled=True,
            axis_index_groups=[[8 * g + i for g in range(groups)] for i in range(8)],
        ).astype(BF)
        dkv_list = [summed, summed, summed]
    g_shape = ((8, part_rows // 2, 3 * GROUP), BF) if fast else ((1, width, 3 * GROUP), BF)
    m_one, dh_one, dqkv = call(
        functools.partial(qkv_back_kernel, blocks, fast),
        [((8, span, width), BF), ((count, width), BF), ((count, 3 * GROUP), BF)],
        [sc, dq] + dkv_list + [w_heads, one, query_ids[:, None], cosine, sine],
        name="qkv_back",
    )
    m_tok = all_to_all(m_one)
    s_one, q_keep, q_send = call(
        functools.partial(qkv_grad_kernel, blocks, seqs, fast),
        [((2, mod_rows, width), F32), g_shape, g_shape],
        [sc, dqkv, dh_one, h_one, n_one, query_row],
        scratch=[((width, 3 * GROUP), BF)],
        name="qkv_grad",
    )
    (grad_in,) = call(
        last_kernel, [(tokens.shape, F32)], [sc, m_tok, tokens, dx_mid], name="last"
    )

    def reduce_all(x):
        if not fast:
            return lax.psum(x, ("cp", "sp"))
        for axis, k, size in (("cp", 2, 8), ("cp", 4, 8), ("cp", 1, 8), ("sp", 2, 4), ("sp", 1, 4)):
            if axis == "sp" and k == 2:
                x = after(x, m_tok)
            x = x + swap(x, axis, k, size)
        return x

    early = reduce_all(jnp.concatenate([s_mid, s_gate[None]], axis=0))
    late = reduce_all(s_one)
    sums = jnp.concatenate([late, early], axis=0).transpose(1, 0, 2).reshape(mod_rows, 6 * width)
    grad_ada = lax.dot_general(
        cond.astype(F32), sums, (((0,), (0,)), ((), ())), precision=lax.Precision.HIGHEST
    )
    grad_bias = lax.dynamic_slice_in_dim(
        jnp.sum(sums, axis=0), b_ada.shape[0] * r, b_ada.shape[0], 0
    )

    if fast:
        o_near = after(o_near, m_one)
        proj = total(spread(first_sum(o_keep, o_near)))
        near = swap(q_send, "sp", 1, 4)
        sums = (q_keep.astype(F32) + near.astype(F32)).astype(BF).reshape(
            4, 2, part_rows // 2, 3 * GROUP
        )
        ours = lax.dynamic_index_in_dim(sums, seq, 1, keepdims=False)
        theirs = lax.dynamic_index_in_dim(sums, 1 - seq, 1, keepdims=False)
        ours = (ours.astype(F32) + swap(theirs, "cp", 1, 8).astype(F32)).astype(BF)
        found = [
            swap(lax.dynamic_index_in_dim(ours, hg ^ m, 0, keepdims=False), "cp", 2 * m, 8)
            if m
            else lax.dynamic_index_in_dim(ours, hg, 0, keepdims=False)
            for m in range(4)
        ]
        for bit in (1, 2):
            found = [jnp.where((hg & bit) != 0, found[i ^ bit], found[i]) for i in range(4)]
        mine = after(jnp.stack(found), m_tok)
        mine = (mine.astype(F32) + swap(mine, "sp", 2, 4).astype(F32)).astype(BF)
        other = swap(mine, "sp", 1, 4)
        low = jnp.where(s % 2 == 0, mine, other)
        high = jnp.where(s % 2 == 0, other, mine)
        both = jnp.concatenate([low, high], axis=1)
        grad_qkv = (
            both.reshape(4, part_rows, 3, GROUP).transpose(1, 2, 0, 3).reshape(part_rows, 3 * width)
        ).astype(F32)
        for k in (1, 2):
            proj_low = proj.astype(BF)
            proj = proj_low.astype(F32) + swap(proj_low, "sp", k, 4).astype(F32)
        proj_low = proj
    else:
        proj = lax.psum_scatter(o_keep[0].astype(F32), "cp", scatter_dimension=0, tiled=True)
        proj_low = lax.psum(proj, "sp")
        own = lax.psum_scatter(q_keep[0].astype(F32), "sp", scatter_dimension=1, tiled=True)
        placed = lax.dynamic_update_slice(
            jnp.zeros((4, width, 3 * GROUP // 4), F32), own[None], (hg, 0, 0)
        )
        placed = lax.psum_scatter(placed, "cp", scatter_dimension=1, tiled=True)
        whole = lax.all_gather(placed, "sp", axis=2, tiled=True)
        grad_qkv = (
            whole.reshape(4, part_rows, 3, GROUP).transpose(1, 2, 0, 3).reshape(part_rows, 3 * width)
        )
    if fast:
        shares = gather_sp(after(jnp.concatenate([feed, proj_low], axis=0).astype(BF), m_tok))
        grad_up, grad_down, grad_out = call(
            finish_kernel,
            [
                ((part_rows, hidden), F32),
                ((hidden // cp, width), F32),
                ((part_rows, width), F32),
            ],
            [sc] + shares,
            name="finish",
        )
    else:
        shares = lax.all_gather(feed, "sp", axis=0, tiled=False)
        grad_up = (
            shares[:, :part_rows]
            .reshape(4, part_rows, cp, inner)
            .transpose(1, 2, 0, 3)
            .reshape(part_rows, hidden)
        )
        grad_down = shares[:, part_rows:].reshape(hidden // cp, width)
        grad_out = proj_low
    return (
        block_out, grad_in, grad_ada, grad_bias, grad_qkv, grad_out, grad_up, grad_down,
    )


def solution(mesh):
    rows = P("cp", None, "sp", None)
    shard = P("cp", None)
    return jax.shard_map(
        body,
        mesh=mesh,
        in_specs=(
            rows, rows, P(), P(), P(), P(), shard, P("cp"), shard, shard, shard, shard,
        ),
        out_specs=(rows, rows, shard, P("cp"), shard, shard, shard, shard),
        check_vma=False,
    )
```

```python
import functools
import math

import jax
import jax.numpy as jnp
from jax import lax
from jax.experimental import pallas as pl
from jax.experimental.pallas import tpu as pltpu
from jax.sharding import PartitionSpec as P

HD = 64
HEADS = 3
GROUP = 3 * HD
EPS = 1e-06
MASKED = -1e30
BF = jnp.bfloat16
F32 = jnp.float32
VM = pl.BlockSpec(memory_space=pltpu.VMEM)
SM = pl.BlockSpec(memory_space=pltpu.SMEM)


def call(kernel, outs, ins, scratch=(), name=None):
    return pl.pallas_call(
        kernel,
        out_shape=[jax.ShapeDtypeStruct(shape, kind) for shape, kind in outs],
        in_specs=[SM] + [VM] * (len(ins) - 1),
        out_specs=[VM] * len(outs),
        scratch_shapes=[pltpu.VMEM(shape, kind) for shape, kind in scratch],
        compiler_params=pltpu.CompilerParams(vmem_limit_bytes=60 * 1024 * 1024),
        name=name,
    )(*ins)


def dot(a, b):
    return lax.dot_general(a, b, (((1,), (0,)), ((), ())), preferred_element_type=F32)


def dot_nt(a, b):
    return lax.dot_general(a, b, (((1,), (1,)), ((), ())), preferred_element_type=F32)


def dot_tn(a, b):
    return lax.dot_general(a, b, (((0,), (0,)), ((), ())), preferred_element_type=F32)


def normalize(x):
    center = x - jnp.mean(x, axis=-1, keepdims=True)
    inv = lax.rsqrt(jnp.mean(center * center, axis=-1, keepdims=True) + EPS)
    return center * inv, inv


def norm_back(m, n, inv):
    return inv * (
        m - jnp.mean(m, axis=-1, keepdims=True) - n * jnp.mean(m * n, axis=-1, keepdims=True)
    )


def onehot(ids_col, count):
    rows = ids_col.shape[0]
    return jnp.where(
        lax.broadcasted_iota(jnp.int32, (rows, count), 1) == ids_col, 1.0, 0.0
    ).astype(BF)


def onehot_t(ids_row, count):
    cols = ids_row.shape[1]
    return jnp.where(
        lax.broadcasted_iota(jnp.int32, (count, cols), 0) == ids_row, 1.0, 0.0
    ).astype(BF)


def turn(x, cosine, sine):
    lane = lax.broadcasted_iota(jnp.int32, cosine.shape, 1) % HD
    parts = []
    for i in range(x.shape[1] // 128):
        piece = x[:, 128 * i : 128 * (i + 1)]
        swapped = jnp.where(
            lane < HD // 2, pltpu.roll(piece, 128 - HD // 2, 1), pltpu.roll(piece, HD // 2, 1)
        )
        parts.append(piece * cosine + swapped * sine)
    return jnp.concatenate(parts, axis=1)


def turn_back(x, cosine, sine):
    lane = lax.broadcasted_iota(jnp.int32, cosine.shape, 1) % HD
    parts = []
    for i in range(x.shape[1] // 128):
        piece = x[:, 128 * i : 128 * (i + 1)]
        other = piece * sine
        swapped = jnp.where(
            lane < HD // 2, pltpu.roll(other, 128 - HD // 2, 1), pltpu.roll(other, HD // 2, 1)
        )
        parts.append(piece * cosine + swapped)
    return jnp.concatenate(parts, axis=1)


def pack_kernel(
    mod_rows, seqs, sc, tok, cond, w_ada, bias, wq, w_up, w_down, w_proj, send, shard
):
    width = tok.shape[-1]
    s = sc[1]
    slots, _, rows, _ = tok.shape
    span = slots * rows
    blocks = mod_rows // seqs
    first = dot(cond[...], w_ada[:, : 2 * width]) + bias[:, : 2 * width]
    at = pl.multiple_of((2 + s) * width, 128)
    rest = (dot(cond[...], w_ada[:, pl.ds(at, width)]) + bias[:, pl.ds(at, width)]).astype(BF)
    for i in range(8):
        seq, hg = i % 2, i // 2
        for slot in range(slots):
            send[i, slot * rows : (slot + 1) * rows, :] = tok[slot, seq]
        mine = first[seq * blocks : (seq + 1) * blocks]
        send[i, span : span + 2 * blocks, :] = jnp.concatenate(
            [mine[:, :width], mine[:, width:]], axis=0
        ).astype(BF)
        send[i, span + 2 * blocks :, :] = jnp.concatenate(
            [
                wq[:, t * width + hg * GROUP : t * width + (hg + 1) * GROUP]
                for t in (0, 1, 2, 2)
            ],
            axis=1,
        )
    inner = w_down.shape[0] // 4
    n_c = w_up.shape[1] // (4 * inner)
    rows = w_up.shape[0]
    shard[rows : rows + inner, :] = w_down[pl.ds(pl.multiple_of(inner * s, 8), inner), :]
    shard[rows + inner : 2 * rows + inner, :] = w_proj[...]
    shard[2 * rows + inner :, :] = rest
    for own in range(4):

        @pl.when(s == own)
        def _(own=own):
            shard[:rows, :] = jnp.concatenate(
                [
                    w_up[:, (4 * c + own) * inner : (4 * c + own + 1) * inner]
                    for c in range(n_c)
                ],
                axis=1,
            )


def qkv_kernel(blocks, span, fast, n_w, *refs):
    sc, tok, mod_one, ids, cos, sin = refs[:6]
    w_refs = refs[6 : 6 + n_w]
    q_out, kv_out, h_out, n_out, w_out_ref, one_out = refs[6 + n_w : 12 + n_w]
    w_scr = refs[12 + n_w]
    width = tok.shape[-1]
    s = sc[1]
    if fast:
        at = span
        one = jnp.zeros((2 * blocks, width), F32)
        for i in range(8):
            one = one + tok[i, at : at + 2 * blocks, :].astype(F32)
        rows = width // 32
        for m in range(4):
            for i in range(8):
                where = pl.multiple_of(4 * rows * i + rows * (s ^ m), 8)
                w_scr[pl.ds(where, rows), :] = w_refs[m][
                    i * rows : (i + 1) * rows, : 3 * GROUP
                ].astype(F32)
        w = w_scr[...].astype(BF)
    else:
        one = mod_one[...].astype(F32)
        w = w_refs[0][...]
    one = one.astype(BF)
    one_out[...] = one
    w_out_ref[...] = w
    x = jnp.concatenate([tok[i, :span, :] for i in range(8)], axis=0).astype(F32)
    n, _ = normalize(x)
    sel = onehot(ids[...], blocks)
    shift = dot(sel, one[:blocks])
    scale = dot(sel, one[blocks:])
    h = (n * (1.0 + scale) + shift).astype(BF)
    h_out[...] = h
    n_out[...] = n.astype(BF)
    p = dot(h, w)
    qk = turn(p[:, : 2 * GROUP], cos[...], sin[...])
    q_out[...] = (qk[:, :GROUP].astype(BF).astype(F32) * (1.0 / math.sqrt(HD))).astype(BF)
    kv_out[...] = jnp.concatenate([qk[:, GROUP:], p[:, 2 * GROUP :]], axis=1).astype(BF)


def attend_small_kernel(
    sc, q, kv0, kv1, kv2, kv3, kid, qid, o_low, o_full, lse, kv, scores, acc, top, low
):
    for m, part in enumerate((kv0, kv1, kv2, kv3)):
        kv[m] = part[...]
    top[...] = jnp.full(top.shape, MASKED, F32)
    low[...] = jnp.zeros(low.shape, F32)
    acc[...] = jnp.zeros(acc.shape, F32)

    def one(m, _):
        allowed = kid[m] <= qid[...]
        for h in range(HEADS):
            st = dot_nt(kv[m, :, h * HD : (h + 1) * HD], q[:, h * HD : (h + 1) * HD])
            st = jnp.where(allowed, st, MASKED)
            scores[m, h] = st
            top[h] = jnp.maximum(top[h], jnp.max(st, axis=0, keepdims=True))
        return 0

    def two(m, _):
        for h in range(HEADS):
            p = jnp.exp(scores[m, h] - top[h])
            low[h] += jnp.sum(p, axis=0, keepdims=True)
            acc[h] += dot_tn(kv[m, :, GROUP + h * HD : GROUP + (h + 1) * HD], p.astype(BF))
        return 0

    lax.fori_loop(0, 4, one, 0)
    lax.fori_loop(0, 4, two, 0)
    for h in range(HEADS):
        o = (acc[h] / low[h]).T
        o_full[:, h * HD : (h + 1) * HD] = o
        o_low[:, h * HD : (h + 1) * HD] = o.astype(BF)
        lse[h : h + 1, :] = top[h] + jnp.log(low[h])


def attend_large_kernel(sc, q, kv0, kv1, kv2, kv3, kid, qid, o_low, o_full, lse, scores):
    count = q.shape[0]
    part = kv0.shape[0]
    kvs = (kv0, kv1, kv2, kv3)
    step = 512
    for h in range(HEADS):
        qh = q[:, h * HD : (h + 1) * HD]

        def one(g, peak, m=0, h=h, qh=qh):
            rows = pl.ds(pl.multiple_of(g * step, step), step)
            st = dot_nt(kvs[m][rows, h * HD : (h + 1) * HD], qh)
            st = jnp.where(kid[m, rows, :] <= qid[...], st, MASKED)
            scores[pl.ds(pl.multiple_of(m * part + g * step, step), step), :] = st
            return jnp.maximum(peak, jnp.max(st, axis=0, keepdims=True))

        peak = jnp.full((1, count), MASKED, F32)
        for m in range(4):
            peak = lax.fori_loop(0, part // step, functools.partial(one, m=m), peak)

        def two(g, carry, m=0, h=h, peak=peak):
            total, acc = carry
            rows = pl.ds(pl.multiple_of(g * step, step), step)
            where = pl.ds(pl.multiple_of(m * part + g * step, step), step)
            p = jnp.exp(scores[where, :] - peak)
            v = kvs[m][rows, GROUP + h * HD : GROUP + (h + 1) * HD]
            return total + jnp.sum(p, axis=0, keepdims=True), acc + dot_tn(v, p.astype(BF))

        carry = (jnp.zeros((1, count), F32), jnp.zeros((HD, count), F32))
        for m in range(4):
            carry = lax.fori_loop(0, part // step, functools.partial(two, m=m), carry)
        total, acc = carry
        o = (acc / total).T
        o_full[:, h * HD : (h + 1) * HD] = o
        o_low[:, h * HD : (h + 1) * HD] = o.astype(BF)
        lse[h : h + 1, :] = peak + jnp.log(total)


def expand_kernel(sc, rest0, rest1, rest2, rest3, ids, g0, g1, g2, g3, mods, dz):
    s = sc[1]
    parts = [r[...] for r in (rest0, rest1, rest2, rest3)]
    for bit in (1, 2):
        parts = [jnp.where((s & bit) != 0, parts[i ^ bit], parts[i]) for i in range(4)]
    slots, seqs, rows, width = g0.shape
    count = slots * seqs * rows
    rest_low = parts[3]
    for i in range(3):
        mods[i] = dot(onehot(ids[:count, :], rest_low.shape[0]), parts[i])
    gate = dot(onehot(ids[...], rest_low.shape[0]), rest_low)
    mods[3] = gate[:count]
    for m, grad in enumerate((g0, g1, g2, g3)):
        for seq in range(seqs):
            for slot in range(slots):
                at = m * count + (seq * slots + slot) * rows
                g = grad[slot, seq].astype(F32)
                dz[at : at + rows, :] = (g * (1.0 + gate[at : at + rows])).astype(BF)


def project_kernel(n_w, sc, attn, tok, mods, weights, y_out, x_out, n_out, inv_out, h_out, w_out):
    width = tok.shape[-1]
    r = sc[0]
    rows = width // n_w
    for k in range(n_w):
        w_out[rows * k : rows * (k + 1), :] = weights[k, 2 * rows : 3 * rows, :]
    full = jnp.concatenate(
        [
            jnp.concatenate([attn[2 * hg + seq] for hg in range(4)], axis=1)
            for seq in range(2)
        ],
        axis=0,
    )
    y = dot(full, w_out[...])
    y_out[...] = y
    slots, seqs, rows, _ = tok.shape
    x = jnp.concatenate(
        [tok[slot, seq] for seq in range(seqs) for slot in range(slots)], axis=0
    ).astype(F32)
    x1 = x + (1.0 + mods[0]) * y
    x_out[...] = x1
    n, inv = normalize(x1)
    n_out[...] = n
    inv_out[...] = inv
    h_out[...] = (n * (1.0 + mods[2]) + mods[1]).astype(BF)


def feed_kernel(
    n_w, sc, h0, h1, h2, h3, dz_in, weights,
    z_keep, z_send, dh_keep, dh_send, h_all, act_out, du_out, up, down,
):
    width = h0.shape[1]
    rows = width // n_w
    for k in range(n_w):
        up[rows * k : rows * (k + 1), :] = weights[k, :rows, :]
        down[rows * k : rows * (k + 1), :] = weights[k, rows : 2 * rows, :]
    h = jnp.concatenate([h0[...], h1[...], h2[...], h3[...]], axis=0)
    dz = dz_in[...]
    part = h0.shape[0]
    u = dot(h, up[...])
    square = u * u
    inner = 0.7978845608028654 * (u + 0.044715 * square * u)
    t = jnp.tanh(inner)
    act = (0.5 * u * (1.0 + t)).astype(BF)
    slope = 0.5 * (1.0 + t) + 0.5 * u * (1.0 - t * t) * (
        0.7978845608028654 * (1.0 + 3.0 * 0.044715 * square)
    )
    du = (dot_nt(dz, down[...]) * slope).astype(BF)
    dh = dot_nt(du, up[...]).astype(BF)
    for m in range(4):
        (dh_keep, dh_send)[m % 2][m // 2] = dh[m * part : (m + 1) * part]
    z = dot(act, down[...]).astype(BF)
    for m in range(4):
        (z_keep, z_send)[m % 2][m // 2] = z[m * part : (m + 1) * part]
    h_all[...] = h
    act_out[...] = act
    du_out[...] = du


def feed_grad_kernel(n_w, sc, h, dz, act, du, grads):
    rows = h.shape[1] // n_w
    up = dot_tn(h[...], du[...]).astype(BF)
    down = dot_tn(act[...], dz[...]).astype(BF)
    for k in range(n_w):
        grads[k, :rows, :] = up[rows * k : rows * (k + 1)]
        grads[k, rows:, :] = down[rows * k : rows * (k + 1)]


def middle_kernel(
    sc, dh_keep, dh_recv, dh_far, mods, n_in, inv, grad, w, dx_out, dh_out, dy_out, d_out
):
    dh = (
        dh_keep[0].astype(F32) + dh_recv[0].astype(F32) + dh_far[...].astype(F32)
    )
    slots, seqs, rows, width = grad.shape
    g = jnp.concatenate(
        [grad[slot, seq] for seq in range(seqs) for slot in range(slots)], axis=0
    ).astype(F32)
    dx = g + norm_back(dh * (1.0 + mods[2]), n_in[...], inv[...])
    dx_out[...] = dx
    dh_out[...] = dh
    dy = (dx * (1.0 + mods[0])).astype(BF)
    dy_out[...] = dy
    d = dot_nt(dy, w[...]).astype(BF)
    span = slots * rows
    for seq in range(seqs):
        for hg in range(4):
            d_out[2 * hg + seq] = d[seq * span : (seq + 1) * span, hg * GROUP : (hg + 1) * GROUP]


def middle_grad_kernel(
    n_p, rows_total, sc, dx, dh, dy, n_in, y, attn, ids_row, s_out, g_keep, g_send, g_scr
):
    sel = onehot_t(ids_row[...], rows_total)
    s_out[0] = dot(sel, (dx[...] * y[...]).astype(BF))
    s_out[1] = dot(sel, dh[...].astype(BF))
    s_out[2] = dot(sel, (dh[...] * n_in[...]).astype(BF))
    full = jnp.concatenate(
        [
            jnp.concatenate([attn[2 * hg + seq] for hg in range(4)], axis=1)
            for seq in range(2)
        ],
        axis=0,
    )
    g_scr[...] = dot_tn(full, dy[...]).astype(BF)
    if n_p == 1:
        g_keep[0] = g_scr[...]
        g_send[...] = jnp.zeros(g_send.shape, BF)
    else:
        core = sc[1] & 1
        half = g_keep.shape[1]
        for i in range(n_p):
            g_keep[i] = g_scr[pl.ds(pl.multiple_of(2 * half * i + half * core, 16), half), :]
            g_send[i] = g_scr[pl.ds(pl.multiple_of(2 * half * i + half * (1 - core), 16), half), :]


def block_kernel(rows_total, sc, z_keep, z_recv, z_far, mods, x1, grad, ids_row, out, s_out):
    z = z_keep[0].astype(F32) + z_recv[0].astype(F32) + z_far[...].astype(F32)
    slots, seqs, rows, width = grad.shape
    g = jnp.concatenate(
        [grad[slot, seq] for seq in range(seqs) for slot in range(slots)], axis=0
    ).astype(F32)
    s_out[...] = dot(onehot_t(ids_row[...], rows_total), (g * z).astype(BF))
    o = (x1[...] + (1.0 + mods[3]) * z).astype(BF)
    for seq in range(seqs):
        for slot in range(slots):
            at = (seq * slots + slot) * rows
            out[slot, seq] = o[at : at + rows]


def row_sums(x):
    return lax.dot_general(
        jnp.ones((8, x.shape[1]), F32), x, (((1,), (1,)), ((), ())),
        precision=lax.Precision.HIGHEST, preferred_element_type=F32,
    )[:1]


def attend_back_small_kernel(
    sc, q, kv0, kv1, kv2, kv3, kid, qid, o_full, lse, do, dq_out, keep, send, kv, out, acc, delta
):
    for m, part in enumerate((kv0, kv1, kv2, kv3)):
        kv[m] = part[...]
    for h in range(HEADS):
        lanes = slice(h * HD, (h + 1) * HD)
        delta[h] = row_sums(do[:, lanes].astype(F32) * o_full[:, lanes])
    acc[...] = jnp.zeros(acc.shape, F32)

    def piece(m, _):
        allowed = kid[m] <= qid[...]
        for h in range(HEADS):
            lanes = slice(h * HD, (h + 1) * HD)
            others = slice(GROUP + h * HD, GROUP + (h + 1) * HD)
            k = kv[m, :, lanes]
            p = jnp.where(allowed, jnp.exp(dot_nt(k, q[:, lanes]) - lse[h : h + 1, :]), 0.0)
            g = (p * (dot_nt(kv[m, :, others], do[:, lanes]) - delta[h])).astype(BF)
            out[m, :, lanes] = dot(g, q[:, lanes]).astype(BF)
            out[m, :, others] = dot(p.astype(BF), do[:, lanes]).astype(BF)
            acc[h] += dot_tn(k, g)
        return 0

    lax.fori_loop(0, 4, piece, 0)
    for h in range(HEADS):
        dq_out[:, h * HD : (h + 1) * HD] = acc[h].T * (1.0 / math.sqrt(HD))
    for m in range(4):
        (keep, send)[m % 2][m // 2] = out[m]


def attend_back_large_kernel(
    sc, q, kv0, kv1, kv2, kv3, kid, qid, o_full, lse, do, dq_out, keep, send, dqs
):
    part = kv0.shape[0]
    step = 512
    for h in range(HEADS):
        lanes = slice(h * HD, (h + 1) * HD)
        qh = q[:, lanes]
        doh = do[:, lanes]
        delta = row_sums(doh.astype(F32) * o_full[:, lanes])
        top = lse[h : h + 1, :]
        dqs[...] = jnp.zeros(dqs.shape, F32)
        for m, kv in enumerate((kv0, kv1, kv2, kv3)):
            out = (keep, send)[m % 2].at[m // 2]

            def loop(g, c, m=m, kv=kv, out=out, qh=qh, doh=doh, delta=delta, top=top, h=h):
                rows = pl.ds(pl.multiple_of(g * step, step), step)
                k = kv[rows, h * HD : (h + 1) * HD]
                v = kv[rows, GROUP + h * HD : GROUP + (h + 1) * HD]
                p = jnp.where(kid[m, rows, :] <= qid[...], jnp.exp(dot_nt(k, qh) - top), 0.0)
                g2 = (p * (dot_nt(v, doh) - delta)).astype(BF)
                out[rows, h * HD : (h + 1) * HD] = dot(g2, qh).astype(BF)
                out[rows, GROUP + h * HD : GROUP + (h + 1) * HD] = dot(p.astype(BF), doh).astype(BF)
                dqs[...] += dot_tn(k, g2)
                return c

            lax.fori_loop(0, part // step, loop, 0)
        dq_out[:, lanes] = dqs[...].T * (1.0 / math.sqrt(HD))


def qkv_back_kernel(
    blocks, fast, sc, dq, dkv_a, dkv_b, dkv_c, w, one, ids_col, cos, sin, m_out, dh_out, d_out
):
    kv = dkv_a[0].astype(F32)
    if fast:
        kv = kv + dkv_b[0].astype(F32) + dkv_c[...].astype(F32)
    kv = kv.astype(BF).astype(F32)
    q = dq[...].astype(BF).astype(F32)
    qk = turn_back(jnp.concatenate([q, kv[:, :GROUP]], axis=1), cos[...], sin[...])
    d = jnp.concatenate([qk, kv[:, GROUP:]], axis=1).astype(BF)
    d_out[...] = d
    dh = dot_nt(d, w[...])
    dh_out[...] = dh.astype(BF)
    scale = dot(onehot(ids_col[...], blocks), one[blocks:])
    m = (dh * (1.0 + scale)).astype(BF)
    part = m.shape[0] // 8
    for i in range(8):
        m_out[i] = m[i * part : (i + 1) * part]


def qkv_grad_kernel(
    blocks, seqs, fast, sc, d, dh, h, n_in, ids_row, s_out, g_keep, g_send, g_scr
):
    sel = onehot_t(ids_row[...], blocks)
    shift_sum = dot(sel, dh[...])
    scale_sum = dot(sel, (dh[...].astype(F32) * n_in[...].astype(F32)).astype(BF))
    seq = sc[2]
    for b in range(seqs):
        s_out[0, b * blocks : (b + 1) * blocks, :] = jnp.where(seq == b, shift_sum, 0.0)
        s_out[1, b * blocks : (b + 1) * blocks, :] = jnp.where(seq == b, scale_sum, 0.0)
    g_scr[...] = dot_tn(h[...], d[...]).astype(BF)
    if fast:
        c = sc[1] & 1
        half = g_keep.shape[1]
        for i in range(8):
            g_keep[i] = g_scr[pl.ds(pl.multiple_of(2 * half * i + half * c, 16), half), :]
            g_send[i] = g_scr[pl.ds(pl.multiple_of(2 * half * i + half * (1 - c), 16), half), :]
    else:
        g_keep[0] = g_scr[...]
        g_send[...] = jnp.zeros(g_send.shape, BF)


def last_kernel(sc, m_in, tok, dx, out):
    slots, seqs, rows, width = tok.shape
    span = slots * rows
    for seq in range(seqs):
        m = m_in[seq].astype(F32)
        for hg in range(1, 4):
            m = m + m_in[2 * hg + seq].astype(F32)
        x = jnp.concatenate([tok[slot, seq] for slot in range(slots)], axis=0).astype(F32)
        n, inv = normalize(x)
        o = dx[seq * span : (seq + 1) * span, :] + norm_back(m, n, inv)
        for slot in range(slots):
            out[slot, seq] = o[slot * rows : (slot + 1) * rows]


def finish_kernel(sc, p0, p1, p2, p3, proj, proj_other, up, down, outw):
    s = sc[1]
    rows = p0.shape[0] // 2
    width = p0.shape[1]
    parts = [p0, p1, p2, p3]
    half = proj.shape[0]
    outw[pl.ds(pl.multiple_of(half * (s & 1), 8), half), :] = proj[...].astype(F32)
    outw[pl.ds(pl.multiple_of(half * (1 - (s & 1)), 8), half), :] = proj_other[...].astype(F32)
    for m in range(4):
        down[pl.ds(pl.multiple_of(rows * (s ^ m), 8), rows), :] = parts[m][rows : 2 * rows, :].astype(F32)
    ups = [p[:rows, :].astype(F32) for p in parts]
    for bit in (1, 2):
        ups = [jnp.where((s & bit) != 0, ups[i ^ bit], ups[i]) for i in range(4)]
    quarter = up.shape[1] // 4 // (width // rows)
    n_c = up.shape[1] // (4 * quarter)
    for c in range(n_c):
        up[:, 4 * quarter * c : 4 * quarter * (c + 1)] = jnp.concatenate(
            [u[:, quarter * c : quarter * (c + 1)] for u in ups], axis=1
        )


def swap(x, axis, k, size):
    return lax.ppermute(x, axis, [(i, i ^ k) for i in range(size)])


def after(x, *others):
    return lax.optimization_barrier((x,) + others)[0]


def gather_sp(x):
    far = swap(x, "sp", 2, 4)
    return [x, swap(x, "sp", 1, 4), far, swap(far, "sp", 1, 4)]


def body(
    tokens, out_grad, time_table, time_index, span_order, block_ids,
    w_ada, b_ada, w_qkv, w_out, w_up, w_down,
):
    slots, seqs, rows, width = tokens.shape
    cp = lax.axis_size("cp")
    fast = cp == 8
    groups = cp // 8
    r = lax.axis_index("cp")
    s = lax.axis_index("sp")
    j = r % 8
    group = r // 8
    seq = j % 2
    hg = j // 2
    span = slots * rows
    span_rows = 4 * rows
    blocks = time_index.shape[1]
    mod_rows = seqs * blocks
    part_rows = width // cp
    total_slots = slots * cp
    hidden = w_up.shape[1]
    count = 8 * span
    sc = jnp.stack([r, s, seq]).astype(jnp.int32)
    exchange_groups = None if fast else [[8 * g + i for i in range(8)] for g in range(groups)]

    def all_to_all(x):
        return lax.all_to_all(
            x, "cp", split_axis=0, concat_axis=0, tiled=True, axis_index_groups=exchange_groups
        )

    spans = span_order.astype(jnp.int32)
    pick = (spans[:, None] == jnp.arange(total_slots, dtype=jnp.int32)[None, :]).astype(BF)
    slot_ids = jnp.einsum(
        "ns,bst->bnt",
        pick,
        block_ids.reshape(seqs, total_slots, span_rows).astype(BF),
        preferred_element_type=F32,
    ).astype(jnp.int32)
    slot_ids = slot_ids.reshape(seqs, total_slots, 4, rows)
    own_seq = lax.dynamic_index_in_dim(slot_ids, seq, 0, keepdims=False)
    key_ids = jnp.stack(
        [
            lax.dynamic_index_in_dim(own_seq, s ^ m, 1, keepdims=False).reshape(-1)
            for m in range(4)
        ]
    )
    query_ids = lax.dynamic_slice_in_dim(key_ids[0], group * count, count, 0)
    here = lax.dynamic_slice_in_dim(slot_ids, slots * r, slots, 1)
    all_ids = jnp.concatenate(
        [
            (
                lax.dynamic_index_in_dim(here, s ^ m, 2, keepdims=False).reshape(seqs, span)
                + blocks * jnp.arange(seqs, dtype=jnp.int32)[:, None]
            ).reshape(-1)
            for m in range(4)
        ]
    )
    token_ids = all_ids[: seqs * span]
    own_spans = lax.dynamic_slice_in_dim(spans, 8 * slots * group, 8 * slots, 0)
    positions = (
        own_spans[:, None] * span_rows + s * rows + jnp.arange(rows, dtype=jnp.int32)[None, :]
    ).reshape(-1)
    lane = jnp.arange(128, dtype=jnp.int32) % HD
    frequency = jnp.exp(
        -math.log(10000.0) * 2.0 * (lane % (HD // 2)).astype(F32) / HD
    )
    angles = positions.astype(F32)[:, None] * frequency[None, :]
    cosine = jnp.cos(angles)
    sine = jnp.where(lane < HD // 2, -1.0, 1.0)[None, :] * jnp.sin(angles)

    pick_time = (
        time_index.reshape(-1)[:, None] == jnp.arange(time_table.shape[0], dtype=jnp.int32)
    ).astype(F32)
    table_part = lax.dynamic_slice_in_dim(time_table, part_rows * r, part_rows, 1)
    cond = jax.nn.silu(
        jnp.dot(pick_time, table_part, precision=lax.Precision.HIGHEST)
    ).astype(BF)
    bias = lax.dynamic_update_slice(
        jnp.zeros((1, 6 * width), F32), b_ada.astype(F32)[None, :], (0, b_ada.shape[0] * r)
    )

    if fast:
        quarter_rows = part_rows // 4
        wq = lax.dynamic_slice(w_qkv, (quarter_rows * s, 0), (quarter_rows, 3 * width))
        extra = 2 * blocks + quarter_rows
    else:
        wq = w_qkv
        extra = 0
    inner = hidden // cp // 4
    if fast:
        send, shard = call(
            functools.partial(pack_kernel, mod_rows, seqs),
            [((8, span + extra, width), BF), ((2 * part_rows + inner + mod_rows, width), BF)],
            [sc, tokens, cond, w_ada, bias, wq, w_up, w_down, w_out],
            name="pack",
        )
    else:
        send = jnp.broadcast_to(
            tokens.transpose(1, 0, 2, 3).reshape(1, seqs, span, width), (4, seqs, span, width)
        ).reshape(8, span, width)
        up_part = lax.dynamic_index_in_dim(
            w_up.reshape(part_rows, cp, 4, inner), s, 2, keepdims=False
        ).reshape(part_rows, cp * inner)
        down_part = lax.dynamic_slice_in_dim(w_down, inner * s, inner, 0)
        shard = jnp.concatenate([up_part, down_part, w_out], axis=0)
    grad_parts = gather_sp(out_grad)
    got = after(all_to_all(send), *grad_parts)
    if fast:
        w_own = got[:, span + extra - quarter_rows :, :].reshape(8 * quarter_rows, width)
        w_list = gather_sp(w_own)
        mod_one = got
    else:
        full_mod = lax.psum(
            jnp.dot(cond, w_ada, preferred_element_type=F32) + bias, "cp"
        )
        first = lax.dynamic_slice_in_dim(full_mod, seq * blocks, blocks, 0)
        mod_one = jnp.concatenate([first[:, :width], first[:, width : 2 * width]], axis=0)
        gathered = lax.all_gather(w_qkv, "cp", axis=0, tiled=True).reshape(width, 3, 4, GROUP)
        w_list = [
            lax.dynamic_index_in_dim(gathered, hg, 2, keepdims=False).reshape(width, 3 * GROUP)
        ]

    n_w = 8 if fast else 1
    weights = lax.all_gather(shard, "cp", axis=0, tiled=False)
    rests = None
    if fast:
        rest = jnp.sum(weights[:, -mod_rows:, :].astype(F32), axis=0).astype(BF)
    if not fast:
        weights = jnp.concatenate(
            [
                weights[:, at : at + part_rows].reshape(width, width)
                for at in (0, part_rows, 2 * part_rows)
            ],
            axis=0,
        )[None]

    mod_kernel_outs = [
        ((count, GROUP), BF),
        ((count, 2 * GROUP), BF),
        ((count, width), BF),
        ((count, width), BF),
        ((width, 3 * GROUP), BF),
        ((2 * blocks, width), BF),
    ]
    q, kv, h_one, n_one, w_heads, one = call(
        functools.partial(qkv_kernel, blocks, span, fast, len(w_list)),
        mod_kernel_outs,
        [sc, got, mod_one, query_ids[:, None], cosine, sine] + w_list,
        scratch=[((width, 3 * GROUP), F32)],
        name="qkv",
    )
    if not fast:
        kv = lax.all_gather(
            kv, "cp", axis=0, tiled=True,
            axis_index_groups=[[8 * g + i for g in range(groups)] for i in range(8)],
        )
    kvs = gather_sp(kv)
    key_col = key_ids[:, :, None]
    query_row = query_ids[None, :]
    part = kv.shape[0]
    wide_kv = ((4, part, 2 * GROUP), BF)
    attn, attn_full, lse = call(
        attend_small_kernel if fast else attend_large_kernel,
        [((count, GROUP), BF), ((count, GROUP), F32), ((8, count), F32)],
        [sc, q] + kvs + [key_col, query_row],
        scratch=[
            wide_kv,
            ((4, HEADS, part, count), F32),
            ((HEADS, HD, count), F32),
            ((HEADS, 1, count), F32),
            ((HEADS, 1, count), F32),
        ]
        if fast
        else [((4 * part, count), F32)],
        name="attend",
    )
    if fast:
        rests = gather_sp(after(rest, attn))
    else:
        tail = full_mod.astype(BF)
        rests = [
            lax.dynamic_slice_in_dim(tail, (2 + (s ^ m)) * width, width, 1) for m in range(4)
        ]
    mods, dz = call(
        expand_kernel,
        [((4, 2 * span, width), F32), ((8 * span, width), BF)],
        [sc] + rests + [all_ids[:, None]] + [after(grad_parts[0], attn)]
        + grad_parts[1:],
        name="expand",
    )
    attn_tok = all_to_all(attn.reshape(8, span, GROUP))
    y, x_mid, n_two, inv_two, h_two, w_out_full = call(
        functools.partial(project_kernel, n_w),
        [
            ((2 * span, width), F32),
            ((2 * span, width), F32),
            ((2 * span, width), F32),
            ((2 * span, 1), F32),
            ((2 * span, width), BF),
            ((width, width), BF),
        ],
        [sc, attn_tok, tokens, mods, weights],
        name="project",
    )
    hs = gather_sp(h_two)
    pair = ((2, 2 * span, width), BF)
    tall = ((8 * span, width), BF)
    z_keep, z_send, dh_keep, dh_send, h_all, act, du = call(
        functools.partial(feed_kernel, n_w),
        [pair, pair, pair, pair, tall, tall, tall],
        [sc] + hs + [dz, weights],
        scratch=[((width, width), BF)] * 2,
        name="feed",
    )
    def reduce_sp(keep, send):
        near = swap(send, "sp", 1, 4)
        both = (keep[1].astype(F32) + near[1].astype(F32)).astype(BF)
        return (keep, near, swap(both, "sp", 2, 4)), both

    dh_parts, dh_both = reduce_sp(dh_keep, dh_send)
    (g_feed,) = call(
        functools.partial(feed_grad_kernel, n_w),
        [((n_w, 2 * width // n_w, width), BF)],
        [sc, h_all, dz, after(act, dh_both), du],
        name="feed_grad",
    )
    if fast:
        feed = lax.psum_scatter(g_feed, "cp", scatter_dimension=0, tiled=False)
    else:
        feed = jnp.concatenate(
            [
                lax.psum_scatter(
                    g_feed[0, at : at + width].astype(F32), "cp", scatter_dimension=0, tiled=True
                )
                for at in (0, width)
            ],
            axis=0,
        )

    token_row = token_ids[None, :]
    g_out = ((8, part_rows // 2, width), BF) if fast else ((1, width, width), BF)
    wide = ((2 * span, width), F32)
    dx_mid, dh_two, dy, d_attn = call(
        middle_kernel,
        [wide, wide, ((2 * span, width), BF), ((8, span, GROUP), BF)],
        [sc] + list(dh_parts)
        + [mods, n_two, after(inv_two, g_feed), out_grad, w_out_full],
        name="middle",
    )
    s_mid, o_keep, o_send = call(
        functools.partial(middle_grad_kernel, n_w, mod_rows),
        [((3, mod_rows, width), F32), g_out, g_out],
        [sc, dx_mid, dh_two, dy, n_two, y, attn_tok, token_row],
        scratch=[((width, width), BF)],
        name="middle_grad",
    )
    d_heads = all_to_all(d_attn).reshape(count, GROUP)
    if fast:
        o_near = swap(after(o_send, d_heads), "sp", 1, 4)
        d_heads = after(d_heads, s_mid, o_send, o_keep)
    z_parts, _ = reduce_sp(after(z_keep, d_heads), after(z_send, d_heads))
    block_out, s_gate = call(
        functools.partial(block_kernel, mod_rows),
        [(tokens.shape, BF), ((mod_rows, width), F32)],
        [sc] + list(z_parts) + [mods, x_mid, out_grad, token_row],
        name="block",
    )
    dkv = ((2, part, 2 * GROUP), BF)
    dq, kv_keep, kv_send = call(
        attend_back_small_kernel if fast else attend_back_large_kernel,
        [((count, GROUP), F32), dkv, dkv],
        [sc, q] + kvs + [key_col, query_row, attn_full, lse, d_heads],
        scratch=[wide_kv, wide_kv, ((HEADS, HD, count), F32), ((HEADS, 1, count), F32)]
        if fast
        else [((HD, count), F32)],
        name="attend_back",
    )
    dkv_list, _ = reduce_sp(kv_keep, kv_send)
    if not fast:
        summed = sum(x.astype(F32) for x in (dkv_list[0][0], dkv_list[1][0], dkv_list[2]))
        summed = lax.psum_scatter(
            summed, "cp", scatter_dimension=0, tiled=True,
            axis_index_groups=[[8 * g + i for g in range(groups)] for i in range(8)],
        ).astype(BF)
        dkv_list = [summed[None], summed[None], summed]
    g_shape = ((8, part_rows // 2, 3 * GROUP), BF) if fast else ((1, width, 3 * GROUP), BF)
    m_one, dh_one, dqkv = call(
        functools.partial(qkv_back_kernel, blocks, fast),
        [((8, span, width), BF), ((count, width), BF), ((count, 3 * GROUP), BF)],
        [sc, dq] + list(dkv_list) + [w_heads, one, query_ids[:, None], cosine, sine],
        name="qkv_back",
    )
    m_tok = all_to_all(m_one)
    s_one, q_keep, q_send = call(
        functools.partial(qkv_grad_kernel, blocks, seqs, fast),
        [((2, mod_rows, width), F32), g_shape, g_shape],
        [sc, dqkv, dh_one, h_one, n_one, query_row],
        scratch=[((width, 3 * GROUP), BF)],
        name="qkv_grad",
    )
    (grad_in,) = call(
        last_kernel, [(tokens.shape, F32)], [sc, m_tok, tokens, dx_mid], name="last"
    )

    def reduce_all(x, wait=None):
        if not fast:
            return lax.psum(x, ("cp", "sp"))
        for axis, k, size in (("sp", 1, 4), ("sp", 2, 4), ("cp", 1, 8), ("cp", 2, 8), ("cp", 4, 8)):
            if k == 4:
                x = after(x, wait)
            low = x.astype(BF)
            x = low.astype(F32) + swap(low, axis, k, size).astype(F32)
        return x

    sums = reduce_all(jnp.concatenate([s_one, s_mid, s_gate[None]], axis=0), m_tok)
    sums = sums.transpose(1, 0, 2).reshape(mod_rows, 6 * width)
    grad_ada = lax.dot_general(
        cond.astype(F32), sums, (((0,), (0,)), ((), ())), precision=lax.Precision.HIGHEST
    )
    grad_bias = lax.dynamic_slice_in_dim(
        jnp.sum(sums, axis=0), b_ada.shape[0] * r, b_ada.shape[0], 0
    )

    if fast:
        half_width = width // 2
        o_sum = (o_keep.astype(F32) + after(o_near, dq).astype(F32)).astype(BF)
        far = s // 2
        mine = lax.dynamic_slice_in_dim(o_sum, half_width * far, half_width, 2)
        theirs = lax.dynamic_slice_in_dim(o_sum, half_width * (1 - far), half_width, 2)
        o_sum = (mine.astype(F32) + swap(theirs, "sp", 2, 4).astype(F32)).astype(BF)
        o_sum = o_sum.reshape(4, 2, part_rows // 2, half_width)
        mine = lax.dynamic_index_in_dim(o_sum, seq, 1, keepdims=False)
        theirs = lax.dynamic_index_in_dim(o_sum, 1 - seq, 1, keepdims=False)
        o_sum = (mine.astype(F32) + swap(theirs, "cp", 1, 8).astype(F32)).astype(BF)
        proj = sum(
            (
                swap(lax.dynamic_index_in_dim(o_sum, hg ^ m, 0, keepdims=False), "cp", 2 * m, 8)
                if m
                else lax.dynamic_index_in_dim(o_sum, hg, 0, keepdims=False)
            ).astype(F32)
            for m in range(4)
        ).astype(BF)
        other = swap(proj, "sp", 2, 4)
        proj = jnp.concatenate(
            [jnp.where(far == 0, proj, other), jnp.where(far == 0, other, proj)], axis=1
        )
        proj_other = swap(proj, "sp", 1, 4)
        near = swap(q_send, "sp", 1, 4)
        sums = (q_keep.astype(F32) + near.astype(F32)).astype(BF).reshape(
            4, 2, part_rows // 2, 3 * GROUP
        )
        ours = lax.dynamic_index_in_dim(sums, seq, 1, keepdims=False)
        theirs = lax.dynamic_index_in_dim(sums, 1 - seq, 1, keepdims=False)
        ours = (ours.astype(F32) + swap(theirs, "cp", 1, 8).astype(F32)).astype(BF)
        found = [
            swap(lax.dynamic_index_in_dim(ours, hg ^ m, 0, keepdims=False), "cp", 2 * m, 8)
            if m
            else lax.dynamic_index_in_dim(ours, hg, 0, keepdims=False)
            for m in range(4)
        ]
        for bit in (1, 2):
            found = [jnp.where((hg & bit) != 0, found[i ^ bit], found[i]) for i in range(4)]
        mine = after(jnp.stack(found), m_tok)
        mine = (mine.astype(F32) + swap(mine, "sp", 2, 4).astype(F32)).astype(BF)
        other = swap(mine, "sp", 1, 4)
        low = jnp.where(s % 2 == 0, mine, other)
        high = jnp.where(s % 2 == 0, other, mine)
        both = jnp.concatenate([low, high], axis=1)
        grad_qkv = (
            both.reshape(4, part_rows, 3, GROUP).transpose(1, 2, 0, 3).reshape(part_rows, 3 * width)
        ).astype(F32)
    else:
        proj = lax.psum_scatter(o_keep[0].astype(F32), "cp", scatter_dimension=0, tiled=True)
        proj_low = lax.psum(proj, "sp")
        own = lax.psum_scatter(q_keep[0].astype(F32), "sp", scatter_dimension=1, tiled=True)
        placed = lax.dynamic_update_slice(
            jnp.zeros((4, width, 3 * GROUP // 4), F32), own[None], (hg, 0, 0)
        )
        placed = lax.psum_scatter(placed, "cp", scatter_dimension=1, tiled=True)
        whole = lax.all_gather(placed, "sp", axis=2, tiled=True)
        grad_qkv = (
            whole.reshape(4, part_rows, 3, GROUP).transpose(1, 2, 0, 3).reshape(part_rows, 3 * width)
        )
    if fast:
        shares = gather_sp(feed.reshape(2 * part_rows, width))
        grad_up, grad_down, grad_out = call(
            finish_kernel,
            [
                ((part_rows, hidden), F32),
                ((hidden // cp, width), F32),
                ((part_rows, width), F32),
            ],
            [sc] + shares + [proj, proj_other],
            name="finish",
        )
    else:
        shares = lax.all_gather(feed, "sp", axis=0, tiled=False)
        grad_up = (
            shares[:, :part_rows]
            .reshape(4, part_rows, cp, inner)
            .transpose(1, 2, 0, 3)
            .reshape(part_rows, hidden)
        )
        grad_down = shares[:, part_rows:].reshape(hidden // cp, width)
        grad_out = proj_low
    return (
        block_out, grad_in, grad_ada, grad_bias, grad_qkv, grad_out, grad_up, grad_down,
    )


def solution(mesh):
    rows = P("cp", None, "sp", None)
    shard = P("cp", None)
    return jax.shard_map(
        body,
        mesh=mesh,
        in_specs=(
            rows, rows, P(), P(), P(), P(), shard, P("cp"), shard, shard, shard, shard,
        ),
        out_specs=(rows, rows, shard, P("cp"), shard, shard, shard, shard),
        check_vma=False,
    )
```

```python
import functools
import math

import jax
import jax.numpy as jnp
from jax import lax
from jax.experimental import pallas as pl
from jax.experimental.pallas import tpu as pltpu
from jax.sharding import PartitionSpec as P

HD = 64
HEADS = 3
GROUP = 3 * HD
EPS = 1e-06
MASKED = -1e30
BF = jnp.bfloat16
F32 = jnp.float32
VM = pl.BlockSpec(memory_space=pltpu.VMEM)
SM = pl.BlockSpec(memory_space=pltpu.SMEM)


def call(kernel, outs, ins, scratch=(), name=None):
    return pl.pallas_call(
        kernel,
        out_shape=[jax.ShapeDtypeStruct(shape, kind) for shape, kind in outs],
        in_specs=[SM] + [VM] * (len(ins) - 1),
        out_specs=[VM] * len(outs),
        scratch_shapes=[pltpu.VMEM(shape, kind) for shape, kind in scratch],
        compiler_params=pltpu.CompilerParams(vmem_limit_bytes=60 * 1024 * 1024),
        name=name,
    )(*ins)


def dot(a, b):
    return lax.dot_general(a, b, (((1,), (0,)), ((), ())), preferred_element_type=F32)


def dot_nt(a, b):
    return lax.dot_general(a, b, (((1,), (1,)), ((), ())), preferred_element_type=F32)


def dot_tn(a, b):
    return lax.dot_general(a, b, (((0,), (0,)), ((), ())), preferred_element_type=F32)


def normalize(x):
    center = x - jnp.mean(x, axis=-1, keepdims=True)
    inv = lax.rsqrt(jnp.mean(center * center, axis=-1, keepdims=True) + EPS)
    return center * inv, inv


def norm_back(m, n, inv):
    return inv * (
        m - jnp.mean(m, axis=-1, keepdims=True) - n * jnp.mean(m * n, axis=-1, keepdims=True)
    )


def onehot(ids_col, count):
    rows = ids_col.shape[0]
    return jnp.where(
        lax.broadcasted_iota(jnp.int32, (rows, count), 1) == ids_col, 1.0, 0.0
    ).astype(BF)


def onehot_t(ids_row, count):
    cols = ids_row.shape[1]
    return jnp.where(
        lax.broadcasted_iota(jnp.int32, (count, cols), 0) == ids_row, 1.0, 0.0
    ).astype(BF)


def turn(x, cosine, sine):
    lane = lax.broadcasted_iota(jnp.int32, cosine.shape, 1) % HD
    parts = []
    for i in range(x.shape[1] // 128):
        piece = x[:, 128 * i : 128 * (i + 1)]
        swapped = jnp.where(
            lane < HD // 2, pltpu.roll(piece, 128 - HD // 2, 1), pltpu.roll(piece, HD // 2, 1)
        )
        parts.append(piece * cosine + swapped * sine)
    return jnp.concatenate(parts, axis=1)


def turn_back(x, cosine, sine):
    lane = lax.broadcasted_iota(jnp.int32, cosine.shape, 1) % HD
    parts = []
    for i in range(x.shape[1] // 128):
        piece = x[:, 128 * i : 128 * (i + 1)]
        other = piece * sine
        swapped = jnp.where(
            lane < HD // 2, pltpu.roll(other, 128 - HD // 2, 1), pltpu.roll(other, HD // 2, 1)
        )
        parts.append(piece * cosine + swapped)
    return jnp.concatenate(parts, axis=1)


def pack_kernel(
    mod_rows, seqs, sc, tok, cond, w_ada, bias, wq, w_up, w_down, send, shard
):
    width = tok.shape[-1]
    s = sc[1]
    slots, _, rows, _ = tok.shape
    span = slots * rows
    blocks = mod_rows // seqs
    first = dot(cond[...], w_ada[:, : 2 * width]) + bias[:, : 2 * width]
    at = pl.multiple_of((2 + s) * width, 128)
    rest = (dot(cond[...], w_ada[:, pl.ds(at, width)]) + bias[:, pl.ds(at, width)]).astype(BF)
    for i in range(8):
        seq, hg = i % 2, i // 2
        for slot in range(slots):
            send[i, slot * rows : (slot + 1) * rows, :] = tok[slot, seq]
        mine = first[seq * blocks : (seq + 1) * blocks]
        send[i, span : span + 2 * blocks, :] = jnp.concatenate(
            [mine[:, :width], mine[:, width:]], axis=0
        ).astype(BF)
        send[i, span + 2 * blocks : span + 2 * blocks + mod_rows, :] = rest
        send[i, span + 2 * blocks + mod_rows :, :] = jnp.concatenate(
            [
                wq[:, t * width + hg * GROUP : t * width + (hg + 1) * GROUP]
                for t in (0, 1, 2, 2)
            ],
            axis=1,
        )
    inner = w_down.shape[0] // 4
    n_c = w_up.shape[1] // (4 * inner)
    rows = w_up.shape[0]
    shard[rows : rows + inner, :] = w_down[pl.ds(pl.multiple_of(inner * s, 8), inner), :]
    for own in range(4):

        @pl.when(s == own)
        def _(own=own):
            shard[:rows, :] = jnp.concatenate(
                [
                    w_up[:, (4 * c + own) * inner : (4 * c + own + 1) * inner]
                    for c in range(n_c)
                ],
                axis=1,
            )


def qkv_kernel(blocks, span, fast, n_w, *refs):
    sc, tok, mod_one, ids, cos, sin = refs[:6]
    w_refs = refs[6 : 6 + n_w]
    q_out, kv_out, h_out, n_out, w_out_ref, one_out = refs[6 + n_w : 12 + n_w]
    w_scr = refs[12 + n_w]
    width = tok.shape[-1]
    s = sc[1]
    if fast:
        at = span
        one = jnp.zeros((2 * blocks, width), F32)
        for i in range(8):
            one = one + tok[i, at : at + 2 * blocks, :].astype(F32)
        rows = width // 32
        for m in range(4):
            for i in range(8):
                where = pl.multiple_of(4 * rows * i + rows * (s ^ m), 8)
                w_scr[pl.ds(where, rows), :] = w_refs[m][
                    i * rows : (i + 1) * rows, : 3 * GROUP
                ].astype(F32)
        w = w_scr[...].astype(BF)
    else:
        one = mod_one[...].astype(F32)
        w = w_refs[0][...]
    one = one.astype(BF)
    one_out[...] = one
    w_out_ref[...] = w
    x = jnp.concatenate([tok[i, :span, :] for i in range(8)], axis=0).astype(F32)
    n, _ = normalize(x)
    sel = onehot(ids[...], blocks)
    shift = dot(sel, one[:blocks])
    scale = dot(sel, one[blocks:])
    h = (n * (1.0 + scale) + shift).astype(BF)
    h_out[...] = h
    n_out[...] = n.astype(BF)
    p = dot(h, w)
    qk = turn(p[:, : 2 * GROUP], cos[...], sin[...])
    q_out[...] = (qk[:, :GROUP].astype(BF).astype(F32) * (1.0 / math.sqrt(HD))).astype(BF)
    kv_out[...] = jnp.concatenate([qk[:, GROUP:], p[:, 2 * GROUP :]], axis=1).astype(BF)


def attend_small_kernel(
    sc, q, kv0, kv1, kv2, kv3, kid, qid, o_low, o_full, lse, kv, scores, acc, top, low
):
    for m, part in enumerate((kv0, kv1, kv2, kv3)):
        kv[m] = part[...]
    top[...] = jnp.full(top.shape, MASKED, F32)
    low[...] = jnp.zeros(low.shape, F32)
    acc[...] = jnp.zeros(acc.shape, F32)

    def one(m, _):
        allowed = kid[m] <= qid[...]
        for h in range(HEADS):
            st = dot_nt(kv[m, :, h * HD : (h + 1) * HD], q[:, h * HD : (h + 1) * HD])
            st = jnp.where(allowed, st, MASKED)
            scores[m, h] = st
            top[h] = jnp.maximum(top[h], jnp.max(st, axis=0, keepdims=True))
        return 0

    def two(m, _):
        for h in range(HEADS):
            p = jnp.exp(scores[m, h] - top[h])
            low[h] += jnp.sum(p, axis=0, keepdims=True)
            acc[h] += dot_tn(kv[m, :, GROUP + h * HD : GROUP + (h + 1) * HD], p.astype(BF))
        return 0

    lax.fori_loop(0, 4, one, 0)
    lax.fori_loop(0, 4, two, 0)
    for h in range(HEADS):
        o = (acc[h] / low[h]).T
        o_full[:, h * HD : (h + 1) * HD] = o
        o_low[:, h * HD : (h + 1) * HD] = o.astype(BF)
        lse[h : h + 1, :] = top[h] + jnp.log(low[h])


def attend_large_kernel(sc, q, kv0, kv1, kv2, kv3, kid, qid, o_low, o_full, lse, scores):
    count = q.shape[0]
    part = kv0.shape[0]
    kvs = (kv0, kv1, kv2, kv3)
    step = 512
    for h in range(HEADS):
        qh = q[:, h * HD : (h + 1) * HD]

        def one(g, peak, m=0, h=h, qh=qh):
            rows = pl.ds(pl.multiple_of(g * step, step), step)
            st = dot_nt(kvs[m][rows, h * HD : (h + 1) * HD], qh)
            st = jnp.where(kid[m, rows, :] <= qid[...], st, MASKED)
            scores[pl.ds(pl.multiple_of(m * part + g * step, step), step), :] = st
            return jnp.maximum(peak, jnp.max(st, axis=0, keepdims=True))

        peak = jnp.full((1, count), MASKED, F32)
        for m in range(4):
            peak = lax.fori_loop(0, part // step, functools.partial(one, m=m), peak)

        def two(g, carry, m=0, h=h, peak=peak):
            total, acc = carry
            rows = pl.ds(pl.multiple_of(g * step, step), step)
            where = pl.ds(pl.multiple_of(m * part + g * step, step), step)
            p = jnp.exp(scores[where, :] - peak)
            v = kvs[m][rows, GROUP + h * HD : GROUP + (h + 1) * HD]
            return total + jnp.sum(p, axis=0, keepdims=True), acc + dot_tn(v, p.astype(BF))

        carry = (jnp.zeros((1, count), F32), jnp.zeros((HD, count), F32))
        for m in range(4):
            carry = lax.fori_loop(0, part // step, functools.partial(two, m=m), carry)
        total, acc = carry
        o = (acc / total).T
        o_full[:, h * HD : (h + 1) * HD] = o
        o_low[:, h * HD : (h + 1) * HD] = o.astype(BF)
        lse[h : h + 1, :] = peak + jnp.log(total)


def expand_kernel(sc, rest0, rest1, rest2, rest3, ids, g0, g1, g2, g3, mods, dz):
    s = sc[1]
    parts = [r[...] for r in (rest0, rest1, rest2, rest3)]
    for bit in (1, 2):
        parts = [jnp.where((s & bit) != 0, parts[i ^ bit], parts[i]) for i in range(4)]
    slots, seqs, rows, width = g0.shape
    count = slots * seqs * rows
    rest_low = parts[3]
    for i in range(3):
        mods[i] = dot(onehot(ids[:count, :], rest_low.shape[0]), parts[i])
    gate = dot(onehot(ids[...], rest_low.shape[0]), rest_low)
    mods[3] = gate[:count]
    for m, grad in enumerate((g0, g1, g2, g3)):
        for seq in range(seqs):
            for slot in range(slots):
                at = m * count + (seq * slots + slot) * rows
                g = grad[slot, seq].astype(F32)
                dz[at : at + rows, :] = (g * (1.0 + gate[at : at + rows])).astype(BF)


def project_kernel(n_w, sc, attn, tok, mods, weights, y_out, x_out, n_out, inv_out, h_out, w_out):
    width = tok.shape[-1]
    r = sc[0]
    if n_w == 1:
        w_out[...] = weights[0, 0]
    else:
        half = weights.shape[2]
        for k in range(n_w):
            for c in range(2):
                at = pl.multiple_of(2 * half * k + half * ((sc[1] & 1) ^ c), 16)
                w_out[pl.ds(at, half), :] = weights[c, k]
    full = jnp.concatenate(
        [
            jnp.concatenate([attn[2 * hg + seq] for hg in range(4)], axis=1)
            for seq in range(2)
        ],
        axis=0,
    )
    y = dot(full, w_out[...])
    y_out[...] = y
    slots, seqs, rows, _ = tok.shape
    x = jnp.concatenate(
        [tok[slot, seq] for seq in range(seqs) for slot in range(slots)], axis=0
    ).astype(F32)
    x1 = x + (1.0 + mods[0]) * y
    x_out[...] = x1
    n, inv = normalize(x1)
    n_out[...] = n
    inv_out[...] = inv
    h_out[...] = (n * (1.0 + mods[2]) + mods[1]).astype(BF)


def feed_kernel(
    n_w, sc, h0, h1, h2, h3, dz_in, weights,
    z_keep, z_send, dh_keep, dh_send, h_all, act_out, du_out, up, down,
):
    width = h0.shape[1]
    rows = width // n_w
    for k in range(n_w):
        up[rows * k : rows * (k + 1), :] = weights[k, :rows, :]
        down[rows * k : rows * (k + 1), :] = weights[k, rows : 2 * rows, :]
    h = jnp.concatenate([h0[...], h1[...], h2[...], h3[...]], axis=0)
    dz = dz_in[...]
    part = h0.shape[0]
    u = dot(h, up[...])
    square = u * u
    inner = 0.7978845608028654 * (u + 0.044715 * square * u)
    t = jnp.tanh(inner)
    act = (0.5 * u * (1.0 + t)).astype(BF)
    slope = 0.5 * (1.0 + t) + 0.5 * u * (1.0 - t * t) * (
        0.7978845608028654 * (1.0 + 3.0 * 0.044715 * square)
    )
    du = (dot_nt(dz, down[...]) * slope).astype(BF)
    dh = dot_nt(du, up[...]).astype(BF)
    for m in range(4):
        (dh_keep, dh_send)[m % 2][m // 2] = dh[m * part : (m + 1) * part]
    z = dot(act, down[...]).astype(BF)
    for m in range(4):
        (z_keep, z_send)[m % 2][m // 2] = z[m * part : (m + 1) * part]
    h_all[...] = h
    act_out[...] = act
    du_out[...] = du


def feed_grad_kernel(n_w, sc, h, dz, act, du, grads):
    rows = h.shape[1] // n_w
    up = dot_tn(h[...], du[...]).astype(BF)
    down = dot_tn(act[...], dz[...]).astype(BF)
    for k in range(n_w):
        grads[k, :rows, :] = up[rows * k : rows * (k + 1)]
        grads[k, rows:, :] = down[rows * k : rows * (k + 1)]


def middle_kernel(
    sc, dh_keep, dh_recv, dh_far, mods, n_in, inv, grad, w, dx_out, dh_out, dy_out, d_out
):
    dh = (
        dh_keep[0].astype(F32) + dh_recv[0].astype(F32) + dh_far[...].astype(F32)
    )
    slots, seqs, rows, width = grad.shape
    g = jnp.concatenate(
        [grad[slot, seq] for seq in range(seqs) for slot in range(slots)], axis=0
    ).astype(F32)
    dx = g + norm_back(dh * (1.0 + mods[2]), n_in[...], inv[...])
    dx_out[...] = dx
    dh_out[...] = dh
    dy = (dx * (1.0 + mods[0])).astype(BF)
    dy_out[...] = dy
    d = dot_nt(dy, w[...]).astype(BF)
    span = slots * rows
    for seq in range(seqs):
        for hg in range(4):
            d_out[2 * hg + seq] = d[seq * span : (seq + 1) * span, hg * GROUP : (hg + 1) * GROUP]


def middle_grad_kernel(
    n_p, rows_total, sc, dx, dh, dy, n_in, y, attn, ids_row, s_out, g_keep, g_send, g_scr
):
    sel = onehot_t(ids_row[...], rows_total)
    s_out[0] = dot(sel, (dx[...] * y[...]).astype(BF))
    s_out[1] = dot(sel, dh[...].astype(BF))
    s_out[2] = dot(sel, (dh[...] * n_in[...]).astype(BF))
    full = jnp.concatenate(
        [
            jnp.concatenate([attn[2 * hg + seq] for hg in range(4)], axis=1)
            for seq in range(2)
        ],
        axis=0,
    )
    g_scr[...] = dot_tn(full, dy[...]).astype(BF)
    if n_p == 1:
        g_keep[0] = g_scr[...]
        g_send[...] = jnp.zeros(g_send.shape, BF)
    else:
        core = sc[1] & 1
        half = g_keep.shape[1]
        for i in range(n_p):
            g_keep[i] = g_scr[pl.ds(pl.multiple_of(2 * half * i + half * core, 16), half), :]
            g_send[i] = g_scr[pl.ds(pl.multiple_of(2 * half * i + half * (1 - core), 16), half), :]


def block_kernel(rows_total, sc, z_keep, z_recv, z_far, mods, x1, grad, ids_row, out, s_out):
    z = z_keep[0].astype(F32) + z_recv[0].astype(F32) + z_far[...].astype(F32)
    slots, seqs, rows, width = grad.shape
    g = jnp.concatenate(
        [grad[slot, seq] for seq in range(seqs) for slot in range(slots)], axis=0
    ).astype(F32)
    s_out[...] = dot(onehot_t(ids_row[...], rows_total), (g * z).astype(BF))
    o = (x1[...] + (1.0 + mods[3]) * z).astype(BF)
    for seq in range(seqs):
        for slot in range(slots):
            at = (seq * slots + slot) * rows
            out[slot, seq] = o[at : at + rows]


def row_sums(x):
    return lax.dot_general(
        jnp.ones((8, x.shape[1]), F32), x, (((1,), (1,)), ((), ())),
        precision=lax.Precision.HIGHEST, preferred_element_type=F32,
    )[:1]


def attend_back_small_kernel(
    sc, q, kv0, kv1, kv2, kv3, kid, qid, o_full, lse, do, dq_out, keep, send, kv, out, acc, delta
):
    for m, part in enumerate((kv0, kv1, kv2, kv3)):
        kv[m] = part[...]
    for h in range(HEADS):
        lanes = slice(h * HD, (h + 1) * HD)
        delta[h] = row_sums(do[:, lanes].astype(F32) * o_full[:, lanes])
    acc[...] = jnp.zeros(acc.shape, F32)

    def piece(m, _):
        allowed = kid[m] <= qid[...]
        for h in range(HEADS):
            lanes = slice(h * HD, (h + 1) * HD)
            others = slice(GROUP + h * HD, GROUP + (h + 1) * HD)
            k = kv[m, :, lanes]
            p = jnp.where(allowed, jnp.exp(dot_nt(k, q[:, lanes]) - lse[h : h + 1, :]), 0.0)
            g = (p * (dot_nt(kv[m, :, others], do[:, lanes]) - delta[h])).astype(BF)
            out[m, :, lanes] = dot(g, q[:, lanes]).astype(BF)
            out[m, :, others] = dot(p.astype(BF), do[:, lanes]).astype(BF)
            acc[h] += dot_tn(k, g)
        return 0

    lax.fori_loop(0, 4, piece, 0)
    for h in range(HEADS):
        dq_out[:, h * HD : (h + 1) * HD] = acc[h].T * (1.0 / math.sqrt(HD))
    for m in range(4):
        (keep, send)[m % 2][m // 2] = out[m]


def attend_back_large_kernel(
    sc, q, kv0, kv1, kv2, kv3, kid, qid, o_full, lse, do, dq_out, keep, send, dqs
):
    part = kv0.shape[0]
    step = 512
    for h in range(HEADS):
        lanes = slice(h * HD, (h + 1) * HD)
        qh = q[:, lanes]
        doh = do[:, lanes]
        delta = row_sums(doh.astype(F32) * o_full[:, lanes])
        top = lse[h : h + 1, :]
        dqs[...] = jnp.zeros(dqs.shape, F32)
        for m, kv in enumerate((kv0, kv1, kv2, kv3)):
            out = (keep, send)[m % 2].at[m // 2]

            def loop(g, c, m=m, kv=kv, out=out, qh=qh, doh=doh, delta=delta, top=top, h=h):
                rows = pl.ds(pl.multiple_of(g * step, step), step)
                k = kv[rows, h * HD : (h + 1) * HD]
                v = kv[rows, GROUP + h * HD : GROUP + (h + 1) * HD]
                p = jnp.where(kid[m, rows, :] <= qid[...], jnp.exp(dot_nt(k, qh) - top), 0.0)
                g2 = (p * (dot_nt(v, doh) - delta)).astype(BF)
                out[rows, h * HD : (h + 1) * HD] = dot(g2, qh).astype(BF)
                out[rows, GROUP + h * HD : GROUP + (h + 1) * HD] = dot(p.astype(BF), doh).astype(BF)
                dqs[...] += dot_tn(k, g2)
                return c

            lax.fori_loop(0, part // step, loop, 0)
        dq_out[:, lanes] = dqs[...].T * (1.0 / math.sqrt(HD))


def qkv_back_kernel(
    blocks, fast, sc, dq, dkv_a, dkv_b, dkv_c, w, one, ids_col, cos, sin, m_out, dh_out, d_out
):
    kv = dkv_a[0].astype(F32)
    if fast:
        kv = kv + dkv_b[0].astype(F32) + dkv_c[...].astype(F32)
    kv = kv.astype(BF).astype(F32)
    q = dq[...].astype(BF).astype(F32)
    qk = turn_back(jnp.concatenate([q, kv[:, :GROUP]], axis=1), cos[...], sin[...])
    d = jnp.concatenate([qk, kv[:, GROUP:]], axis=1).astype(BF)
    d_out[...] = d
    dh = dot_nt(d, w[...])
    dh_out[...] = dh.astype(BF)
    scale = dot(onehot(ids_col[...], blocks), one[blocks:])
    m = (dh * (1.0 + scale)).astype(BF)
    part = m.shape[0] // 8
    for i in range(8):
        m_out[i] = m[i * part : (i + 1) * part]


def qkv_grad_kernel(
    blocks, seqs, fast, sc, d, dh, h, n_in, ids_row, s_out, g_keep, g_send, g_scr
):
    sel = onehot_t(ids_row[...], blocks)
    shift_sum = dot(sel, dh[...])
    scale_sum = dot(sel, (dh[...].astype(F32) * n_in[...].astype(F32)).astype(BF))
    seq = sc[2]
    for b in range(seqs):
        s_out[0, b * blocks : (b + 1) * blocks, :] = jnp.where(seq == b, shift_sum, 0.0)
        s_out[1, b * blocks : (b + 1) * blocks, :] = jnp.where(seq == b, scale_sum, 0.0)
    g_scr[:, : d.shape[1]] = dot_tn(h[...], d[...]).astype(BF)
    if fast:
        g_scr[:, d.shape[1] :] = jnp.zeros((g_scr.shape[0], g_scr.shape[1] - d.shape[1]), BF)
        c = sc[1] & 1
        half = g_keep.shape[1]
        for i in range(8):
            g_keep[i] = g_scr[pl.ds(pl.multiple_of(2 * half * i + half * c, 16), half), :]
            g_send[i] = g_scr[pl.ds(pl.multiple_of(2 * half * i + half * (1 - c), 16), half), :]
    else:
        g_keep[0] = g_scr[...]
        g_send[...] = jnp.zeros(g_send.shape, BF)


def last_kernel(sc, m_in, tok, dx, out):
    slots, seqs, rows, width = tok.shape
    span = slots * rows
    for seq in range(seqs):
        m = m_in[seq].astype(F32)
        for hg in range(1, 4):
            m = m + m_in[2 * hg + seq].astype(F32)
        x = jnp.concatenate([tok[slot, seq] for slot in range(slots)], axis=0).astype(F32)
        n, inv = normalize(x)
        o = dx[seq * span : (seq + 1) * span, :] + norm_back(m, n, inv)
        for slot in range(slots):
            out[slot, seq] = o[slot * rows : (slot + 1) * rows]


def finish_kernel(sc, p0, p1, p2, p3, up, down):
    s = sc[1]
    rows = p0.shape[0] // 2
    width = p0.shape[1]
    parts = [p0, p1, p2, p3]
    for m in range(4):
        down[pl.ds(pl.multiple_of(rows * (s ^ m), 8), rows), :] = parts[m][rows : 2 * rows, :].astype(F32)
    ups = [p[:rows, :].astype(F32) for p in parts]
    for bit in (1, 2):
        ups = [jnp.where((s & bit) != 0, ups[i ^ bit], ups[i]) for i in range(4)]
    quarter = up.shape[1] // 4 // (width // rows)
    n_c = up.shape[1] // (4 * quarter)
    for c in range(n_c):
        up[:, 4 * quarter * c : 4 * quarter * (c + 1)] = jnp.concatenate(
            [u[:, quarter * c : quarter * (c + 1)] for u in ups], axis=1
        )


def finish_qkv_kernel(sc, own, other, out, proj):
    s = sc[1]
    hg = sc[0] // 2
    half = own.shape[2]
    for c, part in enumerate((own, other)):
        where = pl.ds(pl.multiple_of(half * ((s & 1) ^ c), 8), half)
        swapped = (s & 2) != 0
        low = [jnp.where(swapped, part[1, m].astype(F32), part[0, m].astype(F32)) for m in range(4)]
        high = [jnp.where(swapped, part[0, m].astype(F32), part[1, m].astype(F32)) for m in range(4)]
        low_out, high_out = part[0, 4].astype(F32), part[1, 4].astype(F32)
        proj[where, :] = jnp.concatenate(
            [jnp.where(swapped, high_out, low_out), jnp.where(swapped, low_out, high_out)], axis=1
        )
        for bit in (1, 2):
            flip = (hg & bit) != 0
            low = [jnp.where(flip, low[i ^ bit], low[i]) for i in range(4)]
            high = [jnp.where(flip, high[i ^ bit], high[i]) for i in range(4)]
        out[where, :] = jnp.concatenate(
            [x[:, :GROUP] for x in low]
            + [x[:, GROUP : 2 * GROUP] for x in low]
            + [x[:, :GROUP] for x in high],
            axis=1,
        )


def swap(x, axis, k, size):
    return lax.ppermute(x, axis, [(i, i ^ k) for i in range(size)])


def after(x, *others):
    return lax.optimization_barrier((x,) + others)[0]


def gather_sp(x):
    far = swap(x, "sp", 2, 4)
    return [x, swap(x, "sp", 1, 4), far, swap(far, "sp", 1, 4)]


def body(
    tokens, out_grad, time_table, time_index, span_order, block_ids,
    w_ada, b_ada, w_qkv, w_out, w_up, w_down,
):
    slots, seqs, rows, width = tokens.shape
    cp = lax.axis_size("cp")
    fast = cp == 8
    groups = cp // 8
    r = lax.axis_index("cp")
    s = lax.axis_index("sp")
    j = r % 8
    group = r // 8
    seq = j % 2
    hg = j // 2
    span = slots * rows
    span_rows = 4 * rows
    blocks = time_index.shape[1]
    mod_rows = seqs * blocks
    part_rows = width // cp
    total_slots = slots * cp
    hidden = w_up.shape[1]
    count = 8 * span
    sc = jnp.stack([r, s, seq]).astype(jnp.int32)
    exchange_groups = None if fast else [[8 * g + i for i in range(8)] for g in range(groups)]

    def all_to_all(x):
        return lax.all_to_all(
            x, "cp", split_axis=0, concat_axis=0, tiled=True, axis_index_groups=exchange_groups
        )

    spans = span_order.astype(jnp.int32)
    pick = (spans[:, None] == jnp.arange(total_slots, dtype=jnp.int32)[None, :]).astype(BF)
    slot_ids = jnp.einsum(
        "ns,bst->bnt",
        pick,
        block_ids.reshape(seqs, total_slots, span_rows).astype(BF),
        preferred_element_type=F32,
    ).astype(jnp.int32)
    slot_ids = slot_ids.reshape(seqs, total_slots, 4, rows)
    own_seq = lax.dynamic_index_in_dim(slot_ids, seq, 0, keepdims=False)
    key_ids = jnp.stack(
        [
            lax.dynamic_index_in_dim(own_seq, s ^ m, 1, keepdims=False).reshape(-1)
            for m in range(4)
        ]
    )
    query_ids = lax.dynamic_slice_in_dim(key_ids[0], group * count, count, 0)
    here = lax.dynamic_slice_in_dim(slot_ids, slots * r, slots, 1)
    all_ids = jnp.concatenate(
        [
            (
                lax.dynamic_index_in_dim(here, s ^ m, 2, keepdims=False).reshape(seqs, span)
                + blocks * jnp.arange(seqs, dtype=jnp.int32)[:, None]
            ).reshape(-1)
            for m in range(4)
        ]
    )
    token_ids = all_ids[: seqs * span]
    own_spans = lax.dynamic_slice_in_dim(spans, 8 * slots * group, 8 * slots, 0)
    positions = (
        own_spans[:, None] * span_rows + s * rows + jnp.arange(rows, dtype=jnp.int32)[None, :]
    ).reshape(-1)
    lane = jnp.arange(128, dtype=jnp.int32) % HD
    frequency = jnp.exp(
        -math.log(10000.0) * 2.0 * (lane % (HD // 2)).astype(F32) / HD
    )
    angles = positions.astype(F32)[:, None] * frequency[None, :]
    cosine = jnp.cos(angles)
    sine = jnp.where(lane < HD // 2, -1.0, 1.0)[None, :] * jnp.sin(angles)

    pick_time = (
        time_index.reshape(-1)[:, None] == jnp.arange(time_table.shape[0], dtype=jnp.int32)
    ).astype(F32)
    table_part = lax.dynamic_slice_in_dim(time_table, part_rows * r, part_rows, 1)
    cond = jax.nn.silu(
        jnp.dot(pick_time, table_part, precision=lax.Precision.HIGHEST)
    ).astype(BF)
    bias = lax.dynamic_update_slice(
        jnp.zeros((1, 6 * width), F32), b_ada.astype(F32)[None, :], (0, b_ada.shape[0] * r)
    )

    if fast:
        quarter_rows = part_rows // 4
        wq = lax.dynamic_slice(w_qkv, (quarter_rows * s, 0), (quarter_rows, 3 * width))
        extra = 2 * blocks + mod_rows + quarter_rows
    else:
        wq = w_qkv
        extra = 0
    inner = hidden // cp // 4
    if fast:
        send, shard = call(
            functools.partial(pack_kernel, mod_rows, seqs),
            [((8, span + extra, width), BF), ((part_rows + inner, width), BF)],
            [sc, tokens, cond, w_ada, bias, wq, w_up, w_down],
            name="pack",
        )
    else:
        send = jnp.broadcast_to(
            tokens.transpose(1, 0, 2, 3).reshape(1, seqs, span, width), (4, seqs, span, width)
        ).reshape(8, span, width)
        up_part = lax.dynamic_index_in_dim(
            w_up.reshape(part_rows, cp, 4, inner), s, 2, keepdims=False
        ).reshape(part_rows, cp * inner)
        down_part = lax.dynamic_slice_in_dim(w_down, inner * s, inner, 0)
        shard = jnp.concatenate([up_part, down_part], axis=0)
    grad_parts = gather_sp(out_grad)
    got = after(all_to_all(send), *grad_parts)
    if fast:
        w_own = got[:, span + extra - quarter_rows :, :].reshape(8 * quarter_rows, width)
        rest = got[:, span + 2 * blocks : span + 2 * blocks + mod_rows, :].astype(F32)
        w_list = gather_sp(
            jnp.concatenate([w_own, jnp.sum(rest, axis=0).astype(BF)], axis=0)
        )
        rests = [w[8 * quarter_rows :] for w in w_list]
        mod_one = got
    else:
        full_mod = lax.psum(
            jnp.dot(cond, w_ada, preferred_element_type=F32) + bias, "cp"
        )
        first = lax.dynamic_slice_in_dim(full_mod, seq * blocks, blocks, 0)
        mod_one = jnp.concatenate([first[:, :width], first[:, width : 2 * width]], axis=0)
        gathered = lax.all_gather(w_qkv, "cp", axis=0, tiled=True).reshape(width, 3, 4, GROUP)
        w_list = [
            lax.dynamic_index_in_dim(gathered, hg, 2, keepdims=False).reshape(width, 3 * GROUP)
        ]

    n_w = 8 if fast else 1
    weights = lax.all_gather(after(shard, got) if fast else shard, "cp", axis=0, tiled=False)
    if fast:
        half = part_rows // 2
        w_own = lax.dynamic_slice_in_dim(w_out, half * (s % 2), half, 0)
        w_proj = all_to_all(jnp.broadcast_to(after(w_own, got)[None], (8, half, width)))
    else:
        w_proj = lax.all_gather(w_out, "cp", axis=0, tiled=True)[None, None]
        weights = jnp.concatenate(
            [
                weights[:, at : at + part_rows].reshape(width, width)
                for at in (0, part_rows)
            ],
            axis=0,
        )[None]

    mod_kernel_outs = [
        ((count, GROUP), BF),
        ((count, 2 * GROUP), BF),
        ((count, width), BF),
        ((count, width), BF),
        ((width, 3 * GROUP), BF),
        ((2 * blocks, width), BF),
    ]
    q, kv, h_one, n_one, w_heads, one = call(
        functools.partial(qkv_kernel, blocks, span, fast, len(w_list)),
        mod_kernel_outs,
        [sc, got, mod_one, query_ids[:, None], cosine, sine] + w_list,
        scratch=[((width, 3 * GROUP), F32)],
        name="qkv",
    )
    if not fast:
        kv = lax.all_gather(
            kv, "cp", axis=0, tiled=True,
            axis_index_groups=[[8 * g + i for g in range(groups)] for i in range(8)],
        )
    kvs = gather_sp(kv)
    if fast:
        kvs[0] = after(kvs[0], w_proj)
        w_proj = jnp.stack([w_proj, swap(w_proj, "sp", 1, 4)])
    key_col = key_ids[:, :, None]
    query_row = query_ids[None, :]
    part = kv.shape[0]
    wide_kv = ((4, part, 2 * GROUP), BF)
    attn, attn_full, lse = call(
        attend_small_kernel if fast else attend_large_kernel,
        [((count, GROUP), BF), ((count, GROUP), F32), ((8, count), F32)],
        [sc, q] + kvs + [key_col, query_row],
        scratch=[
            wide_kv,
            ((4, HEADS, part, count), F32),
            ((HEADS, HD, count), F32),
            ((HEADS, 1, count), F32),
            ((HEADS, 1, count), F32),
        ]
        if fast
        else [((4 * part, count), F32)],
        name="attend",
    )
    if not fast:
        tail = full_mod.astype(BF)
        rests = [
            lax.dynamic_slice_in_dim(tail, (2 + (s ^ m)) * width, width, 1) for m in range(4)
        ]
    mods, dz = call(
        expand_kernel,
        [((4, 2 * span, width), F32), ((8 * span, width), BF)],
        [sc] + rests + [all_ids[:, None]] + [after(grad_parts[0], attn)]
        + grad_parts[1:],
        name="expand",
    )
    attn_tok = all_to_all(attn.reshape(8, span, GROUP))
    y, x_mid, n_two, inv_two, h_two, w_out_full = call(
        functools.partial(project_kernel, n_w),
        [
            ((2 * span, width), F32),
            ((2 * span, width), F32),
            ((2 * span, width), F32),
            ((2 * span, 1), F32),
            ((2 * span, width), BF),
            ((width, width), BF),
        ],
        [sc, attn_tok, tokens, mods, w_proj],
        name="project",
    )
    hs = gather_sp(h_two)
    pair = ((2, 2 * span, width), BF)
    tall = ((8 * span, width), BF)
    z_keep, z_send, dh_keep, dh_send, h_all, act, du = call(
        functools.partial(feed_kernel, n_w),
        [pair, pair, pair, pair, tall, tall, tall],
        [sc] + hs + [dz, weights],
        scratch=[((width, width), BF)] * 2,
        name="feed",
    )
    def reduce_sp(keep, send, *wait):
        near = swap(send, "sp", 1, 4)
        if wait:
            near = after(near, *wait)
        both = (keep[1].astype(F32) + near[1].astype(F32)).astype(BF)
        return (keep, near, swap(both, "sp", 2, 4)), both

    dh_parts, dh_both = reduce_sp(dh_keep, dh_send)
    token_row = token_ids[None, :]
    g_out = ((8, part_rows // 2, width), BF) if fast else ((1, width, width), BF)
    wide = ((2 * span, width), F32)
    dx_mid, dh_two, dy, d_attn = call(
        middle_kernel,
        [wide, wide, ((2 * span, width), BF), ((8, span, GROUP), BF)],
        [sc] + list(dh_parts)
        + [mods, n_two, inv_two, out_grad, w_out_full],
        name="middle",
    )
    half_width = width // 2
    far = s // 2

    def split_far(mine, theirs):
        part = (mine.astype(F32) + theirs.astype(F32)).astype(BF)
        return (
            lax.dynamic_slice_in_dim(part, half_width * far, half_width, 2),
            lax.dynamic_slice_in_dim(part, half_width * (1 - far), half_width, 2),
        )

    def split_y(mine, theirs):
        part = (mine.astype(F32) + theirs.astype(F32)).astype(BF)
        part = part.reshape((4, 2) + part.shape[1:])
        return (
            lax.dynamic_index_in_dim(part, seq, 1, keepdims=False),
            lax.dynamic_index_in_dim(part, 1 - seq, 1, keepdims=False),
        )

    d_heads = all_to_all(d_attn).reshape(count, GROUP)
    if fast:
        pass
    (g_feed,) = call(
        functools.partial(feed_grad_kernel, n_w),
        [((n_w, 2 * width // n_w, width), BF)],
        [sc, h_all, dz, after(act, d_heads), du],
        name="feed_grad",
    )
    if fast:
        feed = lax.psum_scatter(g_feed, "cp", scatter_dimension=0, tiled=False)
    else:
        feed = jnp.concatenate(
            [
                lax.psum_scatter(
                    g_feed[0, at : at + width].astype(F32), "cp", scatter_dimension=0, tiled=True
                )
                for at in (0, width)
            ],
            axis=0,
        )

    if fast:
        d_heads = after(d_heads, g_feed)
    dkv = ((2, part, 2 * GROUP), BF)
    dq, kv_keep, kv_send = call(
        attend_back_small_kernel if fast else attend_back_large_kernel,
        [((count, GROUP), F32), dkv, dkv],
        [sc, q] + kvs + [key_col, query_row, attn_full, lse, d_heads],
        scratch=[wide_kv, wide_kv, ((HEADS, HD, count), F32), ((HEADS, 1, count), F32)]
        if fast
        else [((HD, count), F32)],
        name="attend_back",
    )
    s_mid, o_keep, o_send = call(
        functools.partial(middle_grad_kernel, n_w, mod_rows),
        [((3, mod_rows, width), F32), g_out, g_out],
        [sc, dx_mid, dh_two, dy, n_two, after(y, dq), attn_tok, token_row],
        scratch=[((width, width), BF)],
        name="middle_grad",
    )
    if fast:
        o_near = swap(o_send, "sp", 1, 4)
    dkv_list, _ = reduce_sp(kv_keep, kv_send)
    if not fast:
        summed = sum(x.astype(F32) for x in (dkv_list[0][0], dkv_list[1][0], dkv_list[2]))
        summed = lax.psum_scatter(
            summed, "cp", scatter_dimension=0, tiled=True,
            axis_index_groups=[[8 * g + i for g in range(groups)] for i in range(8)],
        ).astype(BF)
        dkv_list = [summed[None], summed[None], summed]
    g_shape = ((8, part_rows // 2, width), BF) if fast else ((1, width, 3 * GROUP), BF)
    m_one, dh_one, dqkv = call(
        functools.partial(qkv_back_kernel, blocks, fast),
        [((8, span, width), BF), ((count, width), BF), ((count, 3 * GROUP), BF)],
        [sc, dq] + list(dkv_list) + [w_heads, one, query_ids[:, None], cosine, sine],
        name="qkv_back",
    )
    m_tok = all_to_all(m_one)
    z_parts, _ = reduce_sp(z_keep, after(z_send, dh_both), m_one)
    block_out, s_gate = call(
        functools.partial(block_kernel, mod_rows),
        [(tokens.shape, BF), ((mod_rows, width), F32)],
        [sc] + list(z_parts) + [mods, after(x_mid, m_one), out_grad, token_row],
        name="block",
    )
    s_one, q_keep, q_send = call(
        functools.partial(qkv_grad_kernel, blocks, seqs, fast),
        [((2, mod_rows, width), F32), g_shape, g_shape],
        [sc, dqkv, dh_one, h_one, n_one, query_row],
        scratch=[((width, width if fast else 3 * GROUP), BF)],
        name="qkv_grad",
    )
    shares = gather_sp(feed.reshape(2 * part_rows, width)) if fast else []
    (grad_in,) = call(
        last_kernel,
        [(tokens.shape, F32)],
        [sc, m_tok, tokens, dx_mid],
        name="last",
    )

    def reduce_all(x, wait=None):
        if not fast:
            return lax.psum(x, ("cp", "sp"))
        for axis, k, size in (("sp", 1, 4), ("sp", 2, 4), ("cp", 1, 8), ("cp", 2, 8), ("cp", 4, 8)):
            if axis == "cp" and k == 2:
                x = after(x, wait)
            low = x.astype(BF)
            x = low.astype(F32) + swap(low, axis, k, size).astype(F32)
        return x

    sums = reduce_all(jnp.concatenate([s_one, s_mid, s_gate[None]], axis=0), m_tok)
    sums = sums.transpose(1, 0, 2).reshape(mod_rows, 6 * width)
    grad_ada = lax.dot_general(
        cond.astype(F32), sums, (((0,), (0,)), ((), ())), precision=lax.Precision.HIGHEST
    )
    grad_bias = lax.dynamic_slice_in_dim(
        jnp.sum(sums, axis=0), b_ada.shape[0] * r, b_ada.shape[0], 0
    )

    if fast:
        o_mine, o_theirs = split_y(o_keep, after(o_near, dq))
        o_mine, o_theirs = split_far(o_mine, after(swap(o_theirs, "cp", 1, 8), m_one))
        mine, theirs = split_far(q_keep, swap(q_send, "sp", 1, 4))
        got_far = swap(jnp.concatenate([theirs, o_theirs], axis=0), "sp", 2, 4)
        mine, theirs = split_y(mine, after(got_far, feed)[:8])
        mine = (mine.astype(F32) + swap(theirs, "cp", 1, 8).astype(F32)).astype(BF)
        o_mine = (o_mine.astype(F32) + got_far[8:].astype(F32)).astype(BF)
        pick = [
            jnp.stack([lax.dynamic_index_in_dim(x, hg ^ m, 0, keepdims=False) for x in (mine, o_mine)])
            for m in range(4)
        ]
        parts = [pick[0]] + [swap(pick[m], "cp", 2 * m, 8) for m in (1, 2, 3)]
        proj = sum(p[1].astype(F32) for p in parts).astype(BF)
        found = after(jnp.stack([p[0] for p in parts] + [proj]), m_tok)
        found = jnp.stack([found, swap(found, "sp", 2, 4)])
        found = [found, swap(found, "sp", 1, 4)]
        grad_qkv, grad_out = call(
            finish_qkv_kernel,
            [((part_rows, 3 * width), F32), ((part_rows, width), F32)],
            [sc] + found,
            name="finish_qkv",
        )
    else:
        proj = lax.psum_scatter(o_keep[0].astype(F32), "cp", scatter_dimension=0, tiled=True)
        proj_low = lax.psum(proj, "sp")
        own = lax.psum_scatter(q_keep[0].astype(F32), "sp", scatter_dimension=1, tiled=True)
        placed = lax.dynamic_update_slice(
            jnp.zeros((4, width, 3 * GROUP // 4), F32), own[None], (hg, 0, 0)
        )
        placed = lax.psum_scatter(placed, "cp", scatter_dimension=1, tiled=True)
        whole = lax.all_gather(placed, "sp", axis=2, tiled=True)
        grad_qkv = (
            whole.reshape(4, part_rows, 3, GROUP).transpose(1, 2, 0, 3).reshape(part_rows, 3 * width)
        )
    if fast:
        grad_up, grad_down = call(
            finish_kernel,
            [
                ((part_rows, hidden), F32),
                ((hidden // cp, width), F32),
            ],
            [sc] + shares,
            name="finish",
        )
    else:
        shares = lax.all_gather(feed, "sp", axis=0, tiled=False)
        grad_up = (
            shares[:, :part_rows]
            .reshape(4, part_rows, cp, inner)
            .transpose(1, 2, 0, 3)
            .reshape(part_rows, hidden)
        )
        grad_down = shares[:, part_rows:].reshape(hidden // cp, width)
        grad_out = proj_low
    return (
        block_out, grad_in, grad_ada, grad_bias, grad_qkv, grad_out, grad_up, grad_down,
    )


def solution(mesh):
    rows = P("cp", None, "sp", None)
    shard = P("cp", None)
    return jax.shard_map(
        body,
        mesh=mesh,
        in_specs=(
            rows, rows, P(), P(), P(), P(), shard, P("cp"), shard, shard, shard, shard,
        ),
        out_specs=(rows, rows, shard, P("cp"), shard, shard, shard, shard),
        check_vma=False,
    )
```

```python
import functools
import math

import jax
import jax.numpy as jnp
from jax import lax
from jax.experimental import pallas as pl
from jax.experimental.pallas import tpu as pltpu
from jax.sharding import PartitionSpec as P

HD = 64
HEADS = 3
GROUP = 3 * HD
EPS = 1e-06
MASKED = -1e30
BF = jnp.bfloat16
F32 = jnp.float32
VM = pl.BlockSpec(memory_space=pltpu.VMEM)
SM = pl.BlockSpec(memory_space=pltpu.SMEM)


def call(kernel, outs, ins, scratch=(), name=None):
    return pl.pallas_call(
        kernel,
        out_shape=[jax.ShapeDtypeStruct(shape, kind) for shape, kind in outs],
        in_specs=[SM] + [VM] * (len(ins) - 1),
        out_specs=[VM] * len(outs),
        scratch_shapes=[pltpu.VMEM(shape, kind) for shape, kind in scratch],
        compiler_params=pltpu.CompilerParams(vmem_limit_bytes=60 * 1024 * 1024),
        name=name,
    )(*ins)


def dot(a, b):
    return lax.dot_general(a, b, (((1,), (0,)), ((), ())), preferred_element_type=F32)


def dot_nt(a, b):
    return lax.dot_general(a, b, (((1,), (1,)), ((), ())), preferred_element_type=F32)


def dot_tn(a, b):
    return lax.dot_general(a, b, (((0,), (0,)), ((), ())), preferred_element_type=F32)


def normalize(x):
    center = x - jnp.mean(x, axis=-1, keepdims=True)
    inv = lax.rsqrt(jnp.mean(center * center, axis=-1, keepdims=True) + EPS)
    return center * inv, inv


def norm_back(m, n, inv):
    return inv * (
        m - jnp.mean(m, axis=-1, keepdims=True) - n * jnp.mean(m * n, axis=-1, keepdims=True)
    )


def onehot(ids_col, count):
    rows = ids_col.shape[0]
    return jnp.where(
        lax.broadcasted_iota(jnp.int32, (rows, count), 1) == ids_col, 1.0, 0.0
    ).astype(BF)


def onehot_t(ids_row, count):
    cols = ids_row.shape[1]
    return jnp.where(
        lax.broadcasted_iota(jnp.int32, (count, cols), 0) == ids_row, 1.0, 0.0
    ).astype(BF)


def turn(x, cosine, sine):
    lane = lax.broadcasted_iota(jnp.int32, cosine.shape, 1) % HD
    parts = []
    for i in range(x.shape[1] // 128):
        piece = x[:, 128 * i : 128 * (i + 1)]
        swapped = jnp.where(
            lane < HD // 2, pltpu.roll(piece, 128 - HD // 2, 1), pltpu.roll(piece, HD // 2, 1)
        )
        parts.append(piece * cosine + swapped * sine)
    return jnp.concatenate(parts, axis=1)


def turn_back(x, cosine, sine):
    lane = lax.broadcasted_iota(jnp.int32, cosine.shape, 1) % HD
    parts = []
    for i in range(x.shape[1] // 128):
        piece = x[:, 128 * i : 128 * (i + 1)]
        other = piece * sine
        swapped = jnp.where(
            lane < HD // 2, pltpu.roll(other, 128 - HD // 2, 1), pltpu.roll(other, HD // 2, 1)
        )
        parts.append(piece * cosine + swapped)
    return jnp.concatenate(parts, axis=1)


def pack_kernel(
    mod_rows, seqs, sc, tok, cond, w_ada, bias, wq, w_up, w_down, send, shard
):
    width = tok.shape[-1]
    s = sc[1]
    slots, _, rows, _ = tok.shape
    span = slots * rows
    blocks = mod_rows // seqs
    count = wq.shape[0] // 4
    quarter = wq[:count, :]
    for own in range(1, 4):
        quarter = jnp.where(s == own, wq[own * count : (own + 1) * count, :], quarter)
    first = dot(cond[...], w_ada[:, : 2 * width]) + bias[:, : 2 * width]
    at = pl.multiple_of((2 + s) * width, 128)
    rest = (dot(cond[...], w_ada[:, pl.ds(at, width)]) + bias[:, pl.ds(at, width)]).astype(BF)
    for i in range(8):
        seq, hg = i % 2, i // 2
        for slot in range(slots):
            send[i, slot * rows : (slot + 1) * rows, :] = tok[slot, seq]
        mine = first[seq * blocks : (seq + 1) * blocks]
        send[i, span : span + 2 * blocks, :] = jnp.concatenate(
            [mine[:, :width], mine[:, width:]], axis=0
        ).astype(BF)
        send[i, span + 2 * blocks : span + 2 * blocks + mod_rows, :] = rest
        send[i, span + 2 * blocks + mod_rows :, :] = jnp.concatenate(
            [
                quarter[:, t * width + hg * GROUP : t * width + (hg + 1) * GROUP]
                for t in (0, 1, 2, 2)
            ],
            axis=1,
        )
    inner = w_down.shape[0] // 4
    n_c = w_up.shape[1] // (4 * inner)
    rows = w_up.shape[0]
    shard[rows : rows + inner, :] = w_down[pl.ds(pl.multiple_of(inner * s, 8), inner), :]
    for own in range(4):

        @pl.when(s == own)
        def _(own=own):
            shard[:rows, :] = jnp.concatenate(
                [
                    w_up[:, (4 * c + own) * inner : (4 * c + own + 1) * inner]
                    for c in range(n_c)
                ],
                axis=1,
            )


def qkv_kernel(blocks, span, fast, n_w, *refs):
    sc, tok, mod_one, ids, cos, sin = refs[:6]
    w_refs = refs[6 : 6 + n_w]
    q_out, kv_out, h_out, n_out, w_out_ref, one_out = refs[6 + n_w : 12 + n_w]
    w_scr = refs[12 + n_w]
    width = tok.shape[-1]
    s = sc[1]
    if fast:
        at = span
        one = jnp.zeros((2 * blocks, width), F32)
        for i in range(8):
            one = one + tok[i, at : at + 2 * blocks, :].astype(F32)
        rows = width // 32
        for m in range(4):
            for i in range(8):
                where = pl.multiple_of(4 * rows * i + rows * (s ^ m), 8)
                w_scr[pl.ds(where, rows), :] = w_refs[m][
                    i * rows : (i + 1) * rows, : 3 * GROUP
                ].astype(F32)
        w = w_scr[...].astype(BF)
    else:
        one = mod_one[...].astype(F32)
        w = w_refs[0][...]
    one = one.astype(BF)
    one_out[...] = one
    w_out_ref[...] = w
    x = jnp.concatenate([tok[i, :span, :] for i in range(8)], axis=0).astype(F32)
    n, _ = normalize(x)
    sel = onehot(ids[...], blocks)
    shift = dot(sel, one[:blocks])
    scale = dot(sel, one[blocks:])
    h = (n * (1.0 + scale) + shift).astype(BF)
    h_out[...] = h
    n_out[...] = n.astype(BF)
    p = dot(h, w)
    qk = turn(p[:, : 2 * GROUP], cos[...], sin[...])
    q_out[...] = (qk[:, :GROUP].astype(BF).astype(F32) * (1.0 / math.sqrt(HD))).astype(BF)
    kv_out[...] = jnp.concatenate([qk[:, GROUP:], p[:, 2 * GROUP :]], axis=1).astype(BF)


def attend_small_kernel(
    sc, q, kv0, kv1, kv2, kv3, kid, qid, o_low, o_full, lse, kv, scores, acc, top, low
):
    for m, part in enumerate((kv0, kv1, kv2, kv3)):
        kv[m] = part[...]
    top[...] = jnp.full(top.shape, MASKED, F32)
    low[...] = jnp.zeros(low.shape, F32)
    acc[...] = jnp.zeros(acc.shape, F32)

    def one(m, _):
        allowed = kid[m] <= qid[...]
        for h in range(HEADS):
            st = dot_nt(kv[m, :, h * HD : (h + 1) * HD], q[:, h * HD : (h + 1) * HD])
            st = jnp.where(allowed, st, MASKED)
            scores[m, h] = st
            top[h] = jnp.maximum(top[h], jnp.max(st, axis=0, keepdims=True))
        return 0

    def two(m, _):
        for h in range(HEADS):
            p = jnp.exp(scores[m, h] - top[h])
            low[h] += jnp.sum(p, axis=0, keepdims=True)
            acc[h] += dot_tn(kv[m, :, GROUP + h * HD : GROUP + (h + 1) * HD], p.astype(BF))
        return 0

    lax.fori_loop(0, 4, one, 0, unroll=2)
    lax.fori_loop(0, 4, two, 0, unroll=2)
    for h in range(HEADS):
        o = (acc[h] / low[h]).T
        o_full[:, h * HD : (h + 1) * HD] = o
        o_low[:, h * HD : (h + 1) * HD] = o.astype(BF)
        lse[h : h + 1, :] = top[h] + jnp.log(low[h])


def attend_large_kernel(sc, q, kv0, kv1, kv2, kv3, kid, qid, o_low, o_full, lse, scores):
    count = q.shape[0]
    part = kv0.shape[0]
    kvs = (kv0, kv1, kv2, kv3)
    step = 512
    for h in range(HEADS):
        qh = q[:, h * HD : (h + 1) * HD]

        def one(g, peak, m=0, h=h, qh=qh):
            rows = pl.ds(pl.multiple_of(g * step, step), step)
            st = dot_nt(kvs[m][rows, h * HD : (h + 1) * HD], qh)
            st = jnp.where(kid[m, rows, :] <= qid[...], st, MASKED)
            scores[pl.ds(pl.multiple_of(m * part + g * step, step), step), :] = st
            return jnp.maximum(peak, jnp.max(st, axis=0, keepdims=True))

        peak = jnp.full((1, count), MASKED, F32)
        for m in range(4):
            peak = lax.fori_loop(0, part // step, functools.partial(one, m=m), peak)

        def two(g, carry, m=0, h=h, peak=peak):
            total, acc = carry
            rows = pl.ds(pl.multiple_of(g * step, step), step)
            where = pl.ds(pl.multiple_of(m * part + g * step, step), step)
            p = jnp.exp(scores[where, :] - peak)
            v = kvs[m][rows, GROUP + h * HD : GROUP + (h + 1) * HD]
            return total + jnp.sum(p, axis=0, keepdims=True), acc + dot_tn(v, p.astype(BF))

        carry = (jnp.zeros((1, count), F32), jnp.zeros((HD, count), F32))
        for m in range(4):
            carry = lax.fori_loop(0, part // step, functools.partial(two, m=m), carry)
        total, acc = carry
        o = (acc / total).T
        o_full[:, h * HD : (h + 1) * HD] = o
        o_low[:, h * HD : (h + 1) * HD] = o.astype(BF)
        lse[h : h + 1, :] = peak + jnp.log(total)


def expand_kernel(sc, rest0, rest1, rest2, rest3, ids, g0, g1, g2, g3, mods, dz):
    s = sc[1]
    parts = [r[...] for r in (rest0, rest1, rest2, rest3)]
    for bit in (1, 2):
        parts = [jnp.where((s & bit) != 0, parts[i ^ bit], parts[i]) for i in range(4)]
    slots, seqs, rows, width = g0.shape
    count = slots * seqs * rows
    rest_low = parts[3]
    for i in range(3):
        mods[i] = dot(onehot(ids[:count, :], rest_low.shape[0]), parts[i])
    gate = dot(onehot(ids[...], rest_low.shape[0]), rest_low)
    mods[3] = gate[:count]
    for m, grad in enumerate((g0, g1, g2, g3)):
        for seq in range(seqs):
            for slot in range(slots):
                at = m * count + (seq * slots + slot) * rows
                g = grad[slot, seq].astype(F32)
                dz[at : at + rows, :] = (g * (1.0 + gate[at : at + rows])).astype(BF)


def project_kernel(n_w, sc, attn, tok, mods, weights, y_out, x_out, n_out, inv_out, h_out, w_out):
    width = tok.shape[-1]
    r = sc[0]
    if n_w == 1:
        w_out[...] = weights[0, 0]
    else:
        half = weights.shape[2]
        for k in range(n_w):
            for c in range(2):
                at = pl.multiple_of(2 * half * k + half * ((sc[1] & 1) ^ c), 16)
                w_out[pl.ds(at, half), :] = weights[c, k]
    full = jnp.concatenate(
        [
            jnp.concatenate([attn[2 * hg + seq] for hg in range(4)], axis=1)
            for seq in range(2)
        ],
        axis=0,
    )
    y = dot(full, w_out[...])
    y_out[...] = y
    slots, seqs, rows, _ = tok.shape
    x = jnp.concatenate(
        [tok[slot, seq] for seq in range(seqs) for slot in range(slots)], axis=0
    ).astype(F32)
    x1 = x + (1.0 + mods[0]) * y
    x_out[...] = x1
    n, inv = normalize(x1)
    n_out[...] = n
    inv_out[...] = inv
    h_out[...] = (n * (1.0 + mods[2]) + mods[1]).astype(BF)


def feed_kernel(
    n_w, sc, h0, h1, h2, h3, dz_in, weights,
    z_keep, z_send, dh_keep, dh_send, h_all, act_out, du_out, up, down,
):
    width = h0.shape[1]
    rows = width // n_w
    for k in range(n_w):
        up[rows * k : rows * (k + 1), :] = weights[k, :rows, :]
        down[rows * k : rows * (k + 1), :] = weights[k, rows : 2 * rows, :]
    h = jnp.concatenate([h0[...], h1[...], h2[...], h3[...]], axis=0)
    dz = dz_in[...]
    part = h0.shape[0]
    u = dot(h, up[...])
    square = u * u
    inner = 0.7978845608028654 * (u + 0.044715 * square * u)
    t = jnp.tanh(inner)
    act = (0.5 * u * (1.0 + t)).astype(BF)
    slope = 0.5 * (1.0 + t) + 0.5 * u * (1.0 - t * t) * (
        0.7978845608028654 * (1.0 + 3.0 * 0.044715 * square)
    )
    du = (dot_nt(dz, down[...]) * slope).astype(BF)
    dh = dot_nt(du, up[...]).astype(BF)
    for m in range(4):
        (dh_keep, dh_send)[m % 2][m // 2] = dh[m * part : (m + 1) * part]
    z = dot(act, down[...]).astype(BF)
    for m in range(4):
        (z_keep, z_send)[m % 2][m // 2] = z[m * part : (m + 1) * part]
    h_all[...] = h
    act_out[...] = act
    du_out[...] = du


def feed_grad_kernel(n_w, sc, h, dz, act, du, grads):
    rows = h.shape[1] // n_w
    up = dot_tn(h[...], du[...]).astype(BF)
    down = dot_tn(act[...], dz[...]).astype(BF)
    for k in range(n_w):
        grads[k, :rows, :] = up[rows * k : rows * (k + 1)]
        grads[k, rows:, :] = down[rows * k : rows * (k + 1)]


def middle_kernel(
    sc, dh_keep, dh_recv, dh_far, mods, n_in, inv, grad, w, dx_out, dh_out, dy_out, d_out
):
    dh = (
        dh_keep[0].astype(F32) + dh_recv[0].astype(F32) + dh_far[...].astype(F32)
    )
    slots, seqs, rows, width = grad.shape
    g = jnp.concatenate(
        [grad[slot, seq] for seq in range(seqs) for slot in range(slots)], axis=0
    ).astype(F32)
    dx = g + norm_back(dh * (1.0 + mods[2]), n_in[...], inv[...])
    dx_out[...] = dx
    dh_out[...] = dh
    dy = (dx * (1.0 + mods[0])).astype(BF)
    dy_out[...] = dy
    d = dot_nt(dy, w[...]).astype(BF)
    span = slots * rows
    for seq in range(seqs):
        for hg in range(4):
            d_out[2 * hg + seq] = d[seq * span : (seq + 1) * span, hg * GROUP : (hg + 1) * GROUP]


def middle_grad_kernel(
    n_p, rows_total, sc, dx, dh, dy, n_in, y, attn, ids_row, s_out, g_keep, g_send, g_scr
):
    sel = onehot_t(ids_row[...], rows_total)
    s_out[0] = dot(sel, (dx[...] * y[...]).astype(BF))
    s_out[1] = dot(sel, dh[...].astype(BF))
    s_out[2] = dot(sel, (dh[...] * n_in[...]).astype(BF))
    full = jnp.concatenate(
        [
            jnp.concatenate([attn[2 * hg + seq] for hg in range(4)], axis=1)
            for seq in range(2)
        ],
        axis=0,
    )
    g_scr[...] = dot_tn(full, dy[...]).astype(BF)
    if n_p == 1:
        g_keep[0] = g_scr[...]
        g_send[...] = jnp.zeros(g_send.shape, BF)
    else:
        core = sc[1] & 1
        half = g_keep.shape[1]
        for i in range(n_p):
            g_keep[i] = g_scr[pl.ds(pl.multiple_of(2 * half * i + half * core, 16), half), :]
            g_send[i] = g_scr[pl.ds(pl.multiple_of(2 * half * i + half * (1 - core), 16), half), :]


def block_kernel(rows_total, sc, z_keep, z_recv, z_far, mods, x1, grad, ids_row, out, s_out):
    z = z_keep[0].astype(F32) + z_recv[0].astype(F32) + z_far[...].astype(F32)
    slots, seqs, rows, width = grad.shape
    g = jnp.concatenate(
        [grad[slot, seq] for seq in range(seqs) for slot in range(slots)], axis=0
    ).astype(F32)
    s_out[...] = dot(onehot_t(ids_row[...], rows_total), (g * z).astype(BF))
    o = (x1[...] + (1.0 + mods[3]) * z).astype(BF)
    for seq in range(seqs):
        for slot in range(slots):
            at = (seq * slots + slot) * rows
            out[slot, seq] = o[at : at + rows]


def row_sums(x):
    return lax.dot_general(
        jnp.ones((8, x.shape[1]), F32), x, (((1,), (1,)), ((), ())),
        precision=lax.Precision.HIGHEST, preferred_element_type=F32,
    )[:1]


def attend_back_small_kernel(
    sc, q, kv0, kv1, kv2, kv3, kid, qid, o_full, lse, do, dq_out, keep, send, kv, out, acc, delta
):
    for m, part in enumerate((kv0, kv1, kv2, kv3)):
        kv[m] = part[...]
    for h in range(HEADS):
        lanes = slice(h * HD, (h + 1) * HD)
        delta[h] = row_sums(do[:, lanes].astype(F32) * o_full[:, lanes])
    acc[...] = jnp.zeros(acc.shape, F32)

    def piece(m, _):
        allowed = kid[m] <= qid[...]
        for h in range(HEADS):
            lanes = slice(h * HD, (h + 1) * HD)
            others = slice(GROUP + h * HD, GROUP + (h + 1) * HD)
            k = kv[m, :, lanes]
            p = jnp.where(allowed, jnp.exp(dot_nt(k, q[:, lanes]) - lse[h : h + 1, :]), 0.0)
            g = (p * (dot_nt(kv[m, :, others], do[:, lanes]) - delta[h])).astype(BF)
            out[m, :, lanes] = dot(g, q[:, lanes]).astype(BF)
            out[m, :, others] = dot(p.astype(BF), do[:, lanes]).astype(BF)
            acc[h] += dot_tn(k, g)
        return 0

    lax.fori_loop(0, 4, piece, 0, unroll=2)
    for h in range(HEADS):
        dq_out[:, h * HD : (h + 1) * HD] = acc[h].T * (1.0 / math.sqrt(HD))
    for m in range(4):
        (keep, send)[m % 2][m // 2] = out[m]


def attend_back_large_kernel(
    sc, q, kv0, kv1, kv2, kv3, kid, qid, o_full, lse, do, dq_out, keep, send, dqs
):
    part = kv0.shape[0]
    step = 512
    for h in range(HEADS):
        lanes = slice(h * HD, (h + 1) * HD)
        qh = q[:, lanes]
        doh = do[:, lanes]
        delta = row_sums(doh.astype(F32) * o_full[:, lanes])
        top = lse[h : h + 1, :]
        dqs[...] = jnp.zeros(dqs.shape, F32)
        for m, kv in enumerate((kv0, kv1, kv2, kv3)):
            out = (keep, send)[m % 2].at[m // 2]

            def loop(g, c, m=m, kv=kv, out=out, qh=qh, doh=doh, delta=delta, top=top, h=h):
                rows = pl.ds(pl.multiple_of(g * step, step), step)
                k = kv[rows, h * HD : (h + 1) * HD]
                v = kv[rows, GROUP + h * HD : GROUP + (h + 1) * HD]
                p = jnp.where(kid[m, rows, :] <= qid[...], jnp.exp(dot_nt(k, qh) - top), 0.0)
                g2 = (p * (dot_nt(v, doh) - delta)).astype(BF)
                out[rows, h * HD : (h + 1) * HD] = dot(g2, qh).astype(BF)
                out[rows, GROUP + h * HD : GROUP + (h + 1) * HD] = dot(p.astype(BF), doh).astype(BF)
                dqs[...] += dot_tn(k, g2)
                return c

            lax.fori_loop(0, part // step, loop, 0)
        dq_out[:, lanes] = dqs[...].T * (1.0 / math.sqrt(HD))


def qkv_back_kernel(
    blocks, fast, sc, dq, dkv_a, dkv_b, dkv_c, w, one, ids_col, cos, sin, m_out, dh_out, d_out
):
    kv = dkv_a[0].astype(F32)
    if fast:
        kv = kv + dkv_b[0].astype(F32) + dkv_c[...].astype(F32)
    kv = kv.astype(BF).astype(F32)
    q = dq[...].astype(BF).astype(F32)
    qk = turn_back(jnp.concatenate([q, kv[:, :GROUP]], axis=1), cos[...], sin[...])
    d = jnp.concatenate([qk, kv[:, GROUP:]], axis=1).astype(BF)
    d_out[...] = d
    dh = dot_nt(d, w[...])
    dh_out[...] = dh.astype(BF)
    scale = dot(onehot(ids_col[...], blocks), one[blocks:])
    m = (dh * (1.0 + scale)).astype(BF)
    part = m.shape[0] // 8
    for i in range(8):
        m_out[i] = m[i * part : (i + 1) * part]


def qkv_grad_kernel(
    blocks, seqs, fast, sc, d, dh, h, n_in, ids_row, s_out, g_keep, g_send, g_scr
):
    sel = onehot_t(ids_row[...], blocks)
    shift_sum = dot(sel, dh[...])
    scale_sum = dot(sel, (dh[...].astype(F32) * n_in[...].astype(F32)).astype(BF))
    seq = sc[2]
    for b in range(seqs):
        s_out[0, b * blocks : (b + 1) * blocks, :] = jnp.where(seq == b, shift_sum, 0.0)
        s_out[1, b * blocks : (b + 1) * blocks, :] = jnp.where(seq == b, scale_sum, 0.0)
    g_scr[:, : d.shape[1]] = dot_tn(h[...], d[...]).astype(BF)
    if fast:
        g_scr[:, d.shape[1] :] = jnp.zeros((g_scr.shape[0], g_scr.shape[1] - d.shape[1]), BF)
        c = sc[1] & 1
        half = g_keep.shape[1]
        for i in range(8):
            g_keep[i] = g_scr[pl.ds(pl.multiple_of(2 * half * i + half * c, 16), half), :]
            g_send[i] = g_scr[pl.ds(pl.multiple_of(2 * half * i + half * (1 - c), 16), half), :]
    else:
        g_keep[0] = g_scr[...]
        g_send[...] = jnp.zeros(g_send.shape, BF)


def last_kernel(sc, m_in, tok, dx, out):
    slots, seqs, rows, width = tok.shape
    span = slots * rows
    for seq in range(seqs):
        m = m_in[seq].astype(F32)
        for hg in range(1, 4):
            m = m + m_in[2 * hg + seq].astype(F32)
        x = jnp.concatenate([tok[slot, seq] for slot in range(slots)], axis=0).astype(F32)
        n, inv = normalize(x)
        o = dx[seq * span : (seq + 1) * span, :] + norm_back(m, n, inv)
        for slot in range(slots):
            out[slot, seq] = o[slot * rows : (slot + 1) * rows]


def finish_kernel(sc, p0, p1, p2, p3, up, down):
    s = sc[1]
    rows = p0.shape[0] // 2
    width = p0.shape[1]
    parts = [p0, p1, p2, p3]
    for m in range(4):
        down[pl.ds(pl.multiple_of(rows * (s ^ m), 8), rows), :] = parts[m][rows : 2 * rows, :].astype(F32)
    ups = [p[:rows, :].astype(F32) for p in parts]
    for bit in (1, 2):
        ups = [jnp.where((s & bit) != 0, ups[i ^ bit], ups[i]) for i in range(4)]
    quarter = up.shape[1] // 4 // (width // rows)
    n_c = up.shape[1] // (4 * quarter)
    for c in range(n_c):
        up[:, 4 * quarter * c : 4 * quarter * (c + 1)] = jnp.concatenate(
            [u[:, quarter * c : quarter * (c + 1)] for u in ups], axis=1
        )


def finish_qkv_kernel(sc, own, other, out, proj):
    s = sc[1]
    hg = sc[0] // 2
    half = own.shape[2]
    for c, part in enumerate((own, other)):
        where = pl.ds(pl.multiple_of(half * ((s & 1) ^ c), 8), half)
        swapped = (s & 2) != 0
        low = [jnp.where(swapped, part[1, m].astype(F32), part[0, m].astype(F32)) for m in range(4)]
        high = [jnp.where(swapped, part[0, m].astype(F32), part[1, m].astype(F32)) for m in range(4)]
        low_out, high_out = part[0, 4].astype(F32), part[1, 4].astype(F32)
        proj[where, :] = jnp.concatenate(
            [jnp.where(swapped, high_out, low_out), jnp.where(swapped, low_out, high_out)], axis=1
        )
        for bit in (1, 2):
            flip = (hg & bit) != 0
            low = [jnp.where(flip, low[i ^ bit], low[i]) for i in range(4)]
            high = [jnp.where(flip, high[i ^ bit], high[i]) for i in range(4)]
        out[where, :] = jnp.concatenate(
            [x[:, :GROUP] for x in low]
            + [x[:, GROUP : 2 * GROUP] for x in low]
            + [x[:, :GROUP] for x in high],
            axis=1,
        )


def swap(x, axis, k, size):
    return lax.ppermute(x, axis, [(i, i ^ k) for i in range(size)])


def after(x, *others):
    return lax.optimization_barrier((x,) + others)[0]


def gather_sp(x, ready=None):
    far = swap(x, "sp", 2, 4)
    if ready is not None:
        far = after(far, ready)
    return [x, swap(x, "sp", 1, 4), far, swap(far, "sp", 1, 4)]


def body(
    tokens, out_grad, time_table, time_index, span_order, block_ids,
    w_ada, b_ada, w_qkv, w_out, w_up, w_down,
):
    slots, seqs, rows, width = tokens.shape
    cp = lax.axis_size("cp")
    fast = cp == 8
    groups = cp // 8
    r = lax.axis_index("cp")
    s = lax.axis_index("sp")
    j = r % 8
    group = r // 8
    seq = j % 2
    hg = j // 2
    span = slots * rows
    span_rows = 4 * rows
    blocks = time_index.shape[1]
    mod_rows = seqs * blocks
    part_rows = width // cp
    total_slots = slots * cp
    hidden = w_up.shape[1]
    count = 8 * span
    sc = jnp.stack([r, s, seq]).astype(jnp.int32)
    exchange_groups = None if fast else [[8 * g + i for i in range(8)] for g in range(groups)]

    def all_to_all(x):
        return lax.all_to_all(
            x, "cp", split_axis=0, concat_axis=0, tiled=True, axis_index_groups=exchange_groups
        )

    spans = span_order.astype(jnp.int32)
    pick = (spans[:, None] == jnp.arange(total_slots, dtype=jnp.int32)[None, :]).astype(BF)
    slot_ids = jnp.einsum(
        "ns,bst->bnt",
        pick,
        block_ids.reshape(seqs, total_slots, span_rows).astype(BF),
        preferred_element_type=F32,
    ).astype(jnp.int32)
    slot_ids = slot_ids.reshape(seqs, total_slots, 4, rows)
    own_seq = lax.dynamic_index_in_dim(slot_ids, seq, 0, keepdims=False)
    key_ids = jnp.stack(
        [
            lax.dynamic_index_in_dim(own_seq, s ^ m, 1, keepdims=False).reshape(-1)
            for m in range(4)
        ]
    )
    query_ids = lax.dynamic_slice_in_dim(key_ids[0], group * count, count, 0)
    here = lax.dynamic_slice_in_dim(slot_ids, slots * r, slots, 1)
    all_ids = jnp.concatenate(
        [
            (
                lax.dynamic_index_in_dim(here, s ^ m, 2, keepdims=False).reshape(seqs, span)
                + blocks * jnp.arange(seqs, dtype=jnp.int32)[:, None]
            ).reshape(-1)
            for m in range(4)
        ]
    )
    token_ids = all_ids[: seqs * span]
    own_spans = lax.dynamic_slice_in_dim(spans, 8 * slots * group, 8 * slots, 0)
    positions = (
        own_spans[:, None] * span_rows + s * rows + jnp.arange(rows, dtype=jnp.int32)[None, :]
    ).reshape(-1)
    lane = jnp.arange(128, dtype=jnp.int32) % HD
    frequency = jnp.exp(
        -math.log(10000.0) * 2.0 * (lane % (HD // 2)).astype(F32) / HD
    )
    angles = positions.astype(F32)[:, None] * frequency[None, :]
    cosine = jnp.cos(angles)
    sine = jnp.where(lane < HD // 2, -1.0, 1.0)[None, :] * jnp.sin(angles)

    pick_time = (
        time_index.reshape(-1)[:, None] == jnp.arange(time_table.shape[0], dtype=jnp.int32)
    ).astype(F32)
    table_part = lax.dynamic_slice_in_dim(time_table, part_rows * r, part_rows, 1)
    cond = jax.nn.silu(
        jnp.dot(pick_time, table_part, precision=lax.Precision.HIGHEST)
    ).astype(BF)
    bias = lax.dynamic_update_slice(
        jnp.zeros((1, 6 * width), F32), b_ada.astype(F32)[None, :], (0, b_ada.shape[0] * r)
    )

    if fast:
        quarter_rows = part_rows // 4
        wq = w_qkv
        extra = 2 * blocks + mod_rows + quarter_rows
    else:
        wq = w_qkv
        extra = 0
    inner = hidden // cp // 4
    if fast:
        send, shard = call(
            functools.partial(pack_kernel, mod_rows, seqs),
            [((8, span + extra, width), BF), ((part_rows + inner, width), BF)],
            [sc, tokens, cond, w_ada, bias, wq, w_up, w_down],
            name="pack",
        )
    else:
        send = jnp.broadcast_to(
            tokens.transpose(1, 0, 2, 3).reshape(1, seqs, span, width), (4, seqs, span, width)
        ).reshape(8, span, width)
        up_part = lax.dynamic_index_in_dim(
            w_up.reshape(part_rows, cp, 4, inner), s, 2, keepdims=False
        ).reshape(part_rows, cp * inner)
        down_part = lax.dynamic_slice_in_dim(w_down, inner * s, inner, 0)
        shard = jnp.concatenate([up_part, down_part], axis=0)
    grad_parts = gather_sp(out_grad)
    got = after(all_to_all(send), *grad_parts)
    if fast:
        w_own = got[:, span + extra - quarter_rows :, :].reshape(8 * quarter_rows, width)
        rest = got[:, span + 2 * blocks : span + 2 * blocks + mod_rows, :].astype(F32)
        w_list = gather_sp(
            jnp.concatenate([w_own, jnp.sum(rest, axis=0).astype(BF)], axis=0)
        )
        rests = [w[8 * quarter_rows :] for w in w_list]
        mod_one = got
    else:
        full_mod = lax.psum(
            jnp.dot(cond, w_ada, preferred_element_type=F32) + bias, "cp"
        )
        first = lax.dynamic_slice_in_dim(full_mod, seq * blocks, blocks, 0)
        mod_one = jnp.concatenate([first[:, :width], first[:, width : 2 * width]], axis=0)
        gathered = lax.all_gather(w_qkv, "cp", axis=0, tiled=True).reshape(width, 3, 4, GROUP)
        w_list = [
            lax.dynamic_index_in_dim(gathered, hg, 2, keepdims=False).reshape(width, 3 * GROUP)
        ]

    n_w = 8 if fast else 1
    weights = lax.all_gather(after(shard, got) if fast else shard, "cp", axis=0, tiled=False)
    if fast:
        half = part_rows // 2
        w_own = lax.dynamic_slice_in_dim(w_out, half * (s % 2), half, 0)
        w_proj = all_to_all(jnp.broadcast_to(after(w_own, got)[None], (8, half, width)))
    else:
        w_proj = lax.all_gather(w_out, "cp", axis=0, tiled=True)[None, None]
        weights = jnp.concatenate(
            [
                weights[:, at : at + part_rows].reshape(width, width)
                for at in (0, part_rows)
            ],
            axis=0,
        )[None]

    mod_kernel_outs = [
        ((count, GROUP), BF),
        ((count, 2 * GROUP), BF),
        ((count, width), BF),
        ((count, width), BF),
        ((width, 3 * GROUP), BF),
        ((2 * blocks, width), BF),
    ]
    q, kv, h_one, n_one, w_heads, one = call(
        functools.partial(qkv_kernel, blocks, span, fast, len(w_list)),
        mod_kernel_outs,
        [sc, got, mod_one, query_ids[:, None], cosine, sine] + w_list,
        scratch=[((width, 3 * GROUP), F32)],
        name="qkv",
    )
    if not fast:
        kv = lax.all_gather(
            kv, "cp", axis=0, tiled=True,
            axis_index_groups=[[8 * g + i for g in range(groups)] for i in range(8)],
        )
    key_col = key_ids[:, :, None]
    kvs = gather_sp(kv, key_col)
    if fast:
        kvs[0] = after(kvs[0], w_proj)
        w_proj = jnp.stack([w_proj, swap(w_proj, "sp", 1, 4)])
    query_row = query_ids[None, :]
    part = kv.shape[0]
    wide_kv = ((4, part, 2 * GROUP), BF)
    attn, attn_full, lse = call(
        attend_small_kernel if fast else attend_large_kernel,
        [((count, GROUP), BF), ((count, GROUP), F32), ((8, count), F32)],
        [sc, q] + kvs + [key_col, query_row],
        scratch=[
            wide_kv,
            ((4, HEADS, part, count), F32),
            ((HEADS, HD, count), F32),
            ((HEADS, 1, count), F32),
            ((HEADS, 1, count), F32),
        ]
        if fast
        else [((4 * part, count), F32)],
        name="attend",
    )
    if not fast:
        tail = full_mod.astype(BF)
        rests = [
            lax.dynamic_slice_in_dim(tail, (2 + (s ^ m)) * width, width, 1) for m in range(4)
        ]
    mods, dz = call(
        expand_kernel,
        [((4, 2 * span, width), F32), ((8 * span, width), BF)],
        [sc] + rests + [all_ids[:, None]] + [after(grad_parts[0], attn)]
        + grad_parts[1:],
        name="expand",
    )
    attn_tok = all_to_all(attn.reshape(8, span, GROUP))
    y, x_mid, n_two, inv_two, h_two, w_out_full = call(
        functools.partial(project_kernel, n_w),
        [
            ((2 * span, width), F32),
            ((2 * span, width), F32),
            ((2 * span, width), F32),
            ((2 * span, 1), F32),
            ((2 * span, width), BF),
            ((width, width), BF),
        ],
        [sc, attn_tok, tokens, mods, w_proj],
        name="project",
    )
    hs = gather_sp(h_two)
    pair = ((2, 2 * span, width), BF)
    tall = ((8 * span, width), BF)
    z_keep, z_send, dh_keep, dh_send, h_all, act, du = call(
        functools.partial(feed_kernel, n_w),
        [pair, pair, pair, pair, tall, tall, tall],
        [sc] + hs + [dz, weights],
        scratch=[((width, width), BF)] * 2,
        name="feed",
    )
    def reduce_sp(keep, send, *wait):
        near = swap(send, "sp", 1, 4)
        if wait:
            near = after(near, *wait)
        both = (keep[1].astype(F32) + near[1].astype(F32)).astype(BF)
        return (keep, near, swap(both, "sp", 2, 4)), both

    dh_parts, dh_both = reduce_sp(dh_keep, dh_send)
    token_row = token_ids[None, :]
    g_out = ((8, part_rows // 2, width), BF) if fast else ((1, width, width), BF)
    wide = ((2 * span, width), F32)
    dx_mid, dh_two, dy, d_attn = call(
        middle_kernel,
        [wide, wide, ((2 * span, width), BF), ((8, span, GROUP), BF)],
        [sc] + list(dh_parts)
        + [mods, n_two, inv_two, out_grad, w_out_full],
        name="middle",
    )
    half_width = width // 2
    far = s // 2

    def split_far(mine, theirs):
        part = (mine.astype(F32) + theirs.astype(F32)).astype(BF)
        return (
            lax.dynamic_slice_in_dim(part, half_width * far, half_width, 2),
            lax.dynamic_slice_in_dim(part, half_width * (1 - far), half_width, 2),
        )

    def split_y(mine, theirs):
        part = (mine.astype(F32) + theirs.astype(F32)).astype(BF)
        part = part.reshape((4, 2) + part.shape[1:])
        return (
            lax.dynamic_index_in_dim(part, seq, 1, keepdims=False),
            lax.dynamic_index_in_dim(part, 1 - seq, 1, keepdims=False),
        )

    d_heads = all_to_all(d_attn).reshape(count, GROUP)
    if fast:
        pass
    (g_feed,) = call(
        functools.partial(feed_grad_kernel, n_w),
        [((n_w, 2 * width // n_w, width), BF)],
        [sc, h_all, dz, after(act, d_heads), du],
        name="feed_grad",
    )
    if fast:
        feed = lax.psum_scatter(g_feed, "cp", scatter_dimension=0, tiled=False)
    else:
        feed = jnp.concatenate(
            [
                lax.psum_scatter(
                    g_feed[0, at : at + width].astype(F32), "cp", scatter_dimension=0, tiled=True
                )
                for at in (0, width)
            ],
            axis=0,
        )

    if fast:
        d_heads = after(d_heads, g_feed)
    dkv = ((2, part, 2 * GROUP), BF)
    dq, kv_keep, kv_send = call(
        attend_back_small_kernel if fast else attend_back_large_kernel,
        [((count, GROUP), F32), dkv, dkv],
        [sc, q] + kvs + [key_col, query_row, attn_full, lse, d_heads],
        scratch=[wide_kv, wide_kv, ((HEADS, HD, count), F32), ((HEADS, 1, count), F32)]
        if fast
        else [((HD, count), F32)],
        name="attend_back",
    )
    s_mid, o_keep, o_send = call(
        functools.partial(middle_grad_kernel, n_w, mod_rows),
        [((3, mod_rows, width), F32), g_out, g_out],
        [sc, dx_mid, dh_two, dy, n_two, after(y, dq), attn_tok, token_row],
        scratch=[((width, width), BF)],
        name="middle_grad",
    )
    if fast:
        o_near = swap(o_send, "sp", 1, 4)
    dkv_list, _ = reduce_sp(kv_keep, kv_send)
    if not fast:
        summed = sum(x.astype(F32) for x in (dkv_list[0][0], dkv_list[1][0], dkv_list[2]))
        summed = lax.psum_scatter(
            summed, "cp", scatter_dimension=0, tiled=True,
            axis_index_groups=[[8 * g + i for g in range(groups)] for i in range(8)],
        ).astype(BF)
        dkv_list = [summed[None], summed[None], summed]
    g_shape = ((8, part_rows // 2, width), BF) if fast else ((1, width, 3 * GROUP), BF)
    m_one, dh_one, dqkv = call(
        functools.partial(qkv_back_kernel, blocks, fast),
        [((8, span, width), BF), ((count, width), BF), ((count, 3 * GROUP), BF)],
        [sc, dq] + list(dkv_list) + [w_heads, one, query_ids[:, None], cosine, sine],
        name="qkv_back",
    )
    m_tok = all_to_all(m_one)
    z_parts, _ = reduce_sp(z_keep, after(z_send, dh_both), m_one)
    block_out, s_gate = call(
        functools.partial(block_kernel, mod_rows),
        [(tokens.shape, BF), ((mod_rows, width), F32)],
        [sc] + list(z_parts) + [mods, after(x_mid, m_one), out_grad, token_row],
        name="block",
    )
    s_one, q_keep, q_send = call(
        functools.partial(qkv_grad_kernel, blocks, seqs, fast),
        [((2, mod_rows, width), F32), g_shape, g_shape],
        [sc, dqkv, dh_one, h_one, n_one, query_row],
        scratch=[((width, width if fast else 3 * GROUP), BF)],
        name="qkv_grad",
    )
    shares = gather_sp(feed.reshape(2 * part_rows, width)) if fast else []
    (grad_in,) = call(
        last_kernel,
        [(tokens.shape, F32)],
        [sc, m_tok, tokens, dx_mid],
        name="last",
    )

    def reduce_all(x, wait=None):
        if not fast:
            return lax.psum(x, ("cp", "sp"))
        for axis, k, size in (("sp", 1, 4), ("sp", 2, 4), ("cp", 1, 8), ("cp", 2, 8), ("cp", 4, 8)):
            if axis == "cp" and k == 2:
                x = after(x, wait)
            low = x.astype(BF)
            x = low.astype(F32) + swap(low, axis, k, size).astype(F32)
        return x

    sums = reduce_all(jnp.concatenate([s_one, s_mid, s_gate[None]], axis=0), m_tok)
    sums = sums.transpose(1, 0, 2).reshape(mod_rows, 6 * width)
    grad_ada = lax.dot_general(
        cond.astype(F32), sums, (((0,), (0,)), ((), ())), precision=lax.Precision.HIGHEST
    )
    grad_bias = lax.dynamic_slice_in_dim(
        jnp.sum(sums, axis=0), b_ada.shape[0] * r, b_ada.shape[0], 0
    )

    if fast:
        o_mine, o_theirs = split_y(o_keep, after(o_near, dq))
        o_mine, o_theirs = split_far(o_mine, after(swap(o_theirs, "cp", 1, 8), m_one))
        mine, theirs = split_far(q_keep, swap(q_send, "sp", 1, 4))
        got_far = swap(jnp.concatenate([theirs, o_theirs], axis=0), "sp", 2, 4)
        mine, theirs = split_y(mine, after(got_far, feed)[:8])
        mine = (mine.astype(F32) + swap(theirs, "cp", 1, 8).astype(F32)).astype(BF)
        o_mine = (o_mine.astype(F32) + got_far[8:].astype(F32)).astype(BF)
        pick = [
            jnp.stack([lax.dynamic_index_in_dim(x, hg ^ m, 0, keepdims=False) for x in (mine, o_mine)])
            for m in range(4)
        ]
        parts = [pick[0]] + [swap(pick[m], "cp", 2 * m, 8) for m in (1, 2, 3)]
        proj = sum(p[1].astype(F32) for p in parts).astype(BF)
        found = after(jnp.stack([p[0] for p in parts] + [proj]), m_tok)
        found = jnp.stack([found, swap(found, "sp", 2, 4)])
        found = [found, swap(found, "sp", 1, 4)]
        grad_qkv, grad_out = call(
            finish_qkv_kernel,
            [((part_rows, 3 * width), F32), ((part_rows, width), F32)],
            [sc] + found,
            name="finish_qkv",
        )
    else:
        proj = lax.psum_scatter(o_keep[0].astype(F32), "cp", scatter_dimension=0, tiled=True)
        proj_low = lax.psum(proj, "sp")
        own = lax.psum_scatter(q_keep[0].astype(F32), "sp", scatter_dimension=1, tiled=True)
        placed = lax.dynamic_update_slice(
            jnp.zeros((4, width, 3 * GROUP // 4), F32), own[None], (hg, 0, 0)
        )
        placed = lax.psum_scatter(placed, "cp", scatter_dimension=1, tiled=True)
        whole = lax.all_gather(placed, "sp", axis=2, tiled=True)
        grad_qkv = (
            whole.reshape(4, part_rows, 3, GROUP).transpose(1, 2, 0, 3).reshape(part_rows, 3 * width)
        )
    if fast:
        grad_up, grad_down = call(
            finish_kernel,
            [
                ((part_rows, hidden), F32),
                ((hidden // cp, width), F32),
            ],
            [sc] + shares,
            name="finish",
        )
    else:
        shares = lax.all_gather(feed, "sp", axis=0, tiled=False)
        grad_up = (
            shares[:, :part_rows]
            .reshape(4, part_rows, cp, inner)
            .transpose(1, 2, 0, 3)
            .reshape(part_rows, hidden)
        )
        grad_down = shares[:, part_rows:].reshape(hidden // cp, width)
        grad_out = proj_low
    return (
        block_out, grad_in, grad_ada, grad_bias, grad_qkv, grad_out, grad_up, grad_down,
    )


def solution(mesh):
    rows = P("cp", None, "sp", None)
    shard = P("cp", None)
    return jax.shard_map(
        body,
        mesh=mesh,
        in_specs=(
            rows, rows, P(), P(), P(), P(), shard, P("cp"), shard, shard, shard, shard,
        ),
        out_specs=(rows, rows, shard, P("cp"), shard, shard, shard, shard),
        check_vma=False,
    )
```

```python
import functools
import math

import jax
import jax.numpy as jnp
from jax import lax
from jax.experimental import pallas as pl
from jax.experimental.pallas import tpu as pltpu
from jax.sharding import PartitionSpec as P

HD = 64
HEADS = 3
GROUP = 3 * HD
EPS = 1e-06
MASKED = -1e30
BF = jnp.bfloat16
F32 = jnp.float32
VM = pl.BlockSpec(memory_space=pltpu.VMEM)
SM = pl.BlockSpec(memory_space=pltpu.SMEM)


def call(kernel, outs, ins, scratch=(), name=None):
    return pl.pallas_call(
        kernel,
        out_shape=[jax.ShapeDtypeStruct(shape, kind) for shape, kind in outs],
        in_specs=[SM] + [VM] * (len(ins) - 1),
        out_specs=[VM] * len(outs),
        scratch_shapes=[pltpu.VMEM(shape, kind) for shape, kind in scratch],
        compiler_params=pltpu.CompilerParams(vmem_limit_bytes=60 * 1024 * 1024),
        name=name,
    )(*ins)


def dot(a, b):
    return lax.dot_general(a, b, (((1,), (0,)), ((), ())), preferred_element_type=F32)


def dot_nt(a, b):
    return lax.dot_general(a, b, (((1,), (1,)), ((), ())), preferred_element_type=F32)


def dot_tn(a, b):
    return lax.dot_general(a, b, (((0,), (0,)), ((), ())), preferred_element_type=F32)


def normalize(x):
    center = x - jnp.mean(x, axis=-1, keepdims=True)
    inv = lax.rsqrt(jnp.mean(center * center, axis=-1, keepdims=True) + EPS)
    return center * inv, inv


def norm_back(m, n, inv):
    return inv * (
        m - jnp.mean(m, axis=-1, keepdims=True) - n * jnp.mean(m * n, axis=-1, keepdims=True)
    )


def onehot(ids_col, count):
    rows = ids_col.shape[0]
    return jnp.where(
        lax.broadcasted_iota(jnp.int32, (rows, count), 1) == ids_col, 1.0, 0.0
    ).astype(BF)


def onehot_t(ids_row, count):
    cols = ids_row.shape[1]
    return jnp.where(
        lax.broadcasted_iota(jnp.int32, (count, cols), 0) == ids_row, 1.0, 0.0
    ).astype(BF)


def turn(x, cosine, sine):
    lane = lax.broadcasted_iota(jnp.int32, cosine.shape, 1) % HD
    parts = []
    for i in range(x.shape[1] // 128):
        piece = x[:, 128 * i : 128 * (i + 1)]
        swapped = jnp.where(
            lane < HD // 2, pltpu.roll(piece, 128 - HD // 2, 1), pltpu.roll(piece, HD // 2, 1)
        )
        parts.append(piece * cosine + swapped * sine)
    return jnp.concatenate(parts, axis=1)


def turn_back(x, cosine, sine):
    lane = lax.broadcasted_iota(jnp.int32, cosine.shape, 1) % HD
    parts = []
    for i in range(x.shape[1] // 128):
        piece = x[:, 128 * i : 128 * (i + 1)]
        other = piece * sine
        swapped = jnp.where(
            lane < HD // 2, pltpu.roll(other, 128 - HD // 2, 1), pltpu.roll(other, HD // 2, 1)
        )
        parts.append(piece * cosine + swapped)
    return jnp.concatenate(parts, axis=1)


def pack_kernel(
    mod_rows, seqs, sc, tok, cond, w_ada, bias, wq, w_up, w_down, send, shard
):
    width = tok.shape[-1]
    s = sc[1]
    slots, _, rows, _ = tok.shape
    span = slots * rows
    blocks = mod_rows // seqs
    count = wq.shape[0] // 4
    quarter = wq[:count, :]
    for own in range(1, 4):
        quarter = jnp.where(s == own, wq[own * count : (own + 1) * count, :], quarter)
    first = dot(cond[...], w_ada[:, : 2 * width]) + bias[:, : 2 * width]
    at = pl.multiple_of((2 + s) * width, 128)
    rest = (dot(cond[...], w_ada[:, pl.ds(at, width)]) + bias[:, pl.ds(at, width)]).astype(BF)
    for i in range(8):
        seq, hg = i % 2, i // 2
        for slot in range(slots):
            send[i, slot * rows : (slot + 1) * rows, :] = tok[slot, seq]
        mine = first[seq * blocks : (seq + 1) * blocks]
        send[i, span : span + 2 * blocks, :] = jnp.concatenate(
            [mine[:, :width], mine[:, width:]], axis=0
        ).astype(BF)
        send[i, span + 2 * blocks : span + 2 * blocks + mod_rows, :] = rest
        send[i, span + 2 * blocks + mod_rows :, :] = jnp.concatenate(
            [
                quarter[:, t * width + hg * GROUP : t * width + (hg + 1) * GROUP]
                for t in (0, 1, 2, 2)
            ],
            axis=1,
        )
    inner = w_down.shape[0] // 4
    n_c = w_up.shape[1] // (4 * inner)
    rows = w_up.shape[0]
    shard[rows : rows + inner, :] = w_down[pl.ds(pl.multiple_of(inner * s, 8), inner), :]
    for own in range(4):

        @pl.when(s == own)
        def _(own=own):
            shard[:rows, :] = jnp.concatenate(
                [
                    w_up[:, (4 * c + own) * inner : (4 * c + own + 1) * inner]
                    for c in range(n_c)
                ],
                axis=1,
            )


def qkv_kernel(blocks, span, fast, n_w, *refs):
    sc, tok, mod_one, ids, cos, sin = refs[:6]
    w_refs = refs[6 : 6 + n_w]
    q_out, kv_out, h_out, n_out, w_out_ref, one_out = refs[6 + n_w : 12 + n_w]
    w_scr = refs[12 + n_w]
    width = tok.shape[-1]
    s = sc[1]
    if fast:
        at = span
        one = jnp.zeros((2 * blocks, width), F32)
        for i in range(8):
            one = one + tok[i, at : at + 2 * blocks, :].astype(F32)
        rows = width // 32
        for m in range(4):
            for i in range(8):
                where = pl.multiple_of(4 * rows * i + rows * (s ^ m), 8)
                w_scr[pl.ds(where, rows), :] = w_refs[m][
                    i * rows : (i + 1) * rows, : 3 * GROUP
                ].astype(F32)
        w = w_scr[...].astype(BF)
    else:
        one = mod_one[...].astype(F32)
        w = w_refs[0][...]
    one = one.astype(BF)
    one_out[...] = one
    w_out_ref[...] = w
    x = jnp.concatenate([tok[i, :span, :] for i in range(8)], axis=0).astype(F32)
    n, _ = normalize(x)
    sel = onehot(ids[...], blocks)
    shift = dot(sel, one[:blocks])
    scale = dot(sel, one[blocks:])
    h = (n * (1.0 + scale) + shift).astype(BF)
    h_out[...] = h
    n_out[...] = n.astype(BF)
    p = dot(h, w)
    qk = turn(p[:, : 2 * GROUP], cos[...], sin[...])
    q_out[...] = (qk[:, :GROUP].astype(BF).astype(F32) * (1.0 / math.sqrt(HD))).astype(BF)
    kv_out[...] = jnp.concatenate([qk[:, GROUP:], p[:, 2 * GROUP :]], axis=1).astype(BF)


def attend_small_kernel(
    sc, q, kv0, kv1, kv2, kv3, kid, qid, o_low, o_full, lse, kv, scores, acc, top, low
):
    for m, part in enumerate((kv0, kv1, kv2, kv3)):
        kv[m] = part[...]
    top[...] = jnp.full(top.shape, MASKED, F32)
    low[...] = jnp.zeros(low.shape, F32)
    acc[...] = jnp.zeros(acc.shape, F32)

    def one(m, _):
        allowed = kid[m] <= qid[...]
        for h in range(HEADS):
            st = dot_nt(kv[m, :, h * HD : (h + 1) * HD], q[:, h * HD : (h + 1) * HD])
            st = jnp.where(allowed, st, MASKED)
            scores[m, h] = st
            top[h] = jnp.maximum(top[h], jnp.max(st, axis=0, keepdims=True))
        return 0

    def two(m, _):
        for h in range(HEADS):
            p = jnp.exp(scores[m, h] - top[h])
            low[h] += jnp.sum(p, axis=0, keepdims=True)
            acc[h] += dot_tn(kv[m, :, GROUP + h * HD : GROUP + (h + 1) * HD], p.astype(BF))
        return 0

    lax.fori_loop(0, 4, one, 0, unroll=2)
    lax.fori_loop(0, 4, two, 0, unroll=2)
    for h in range(HEADS):
        o = (acc[h] / low[h]).T
        o_full[:, h * HD : (h + 1) * HD] = o
        o_low[:, h * HD : (h + 1) * HD] = o.astype(BF)
        lse[h : h + 1, :] = top[h] + jnp.log(low[h])


def attend_large_kernel(sc, q, kv0, kv1, kv2, kv3, kid, qid, o_low, o_full, lse, scores):
    count = q.shape[0]
    part = kv0.shape[0]
    kvs = (kv0, kv1, kv2, kv3)
    step = 512
    for h in range(HEADS):
        qh = q[:, h * HD : (h + 1) * HD]

        def one(g, peak, m=0, h=h, qh=qh):
            rows = pl.ds(pl.multiple_of(g * step, step), step)
            st = dot_nt(kvs[m][rows, h * HD : (h + 1) * HD], qh)
            st = jnp.where(kid[m, rows, :] <= qid[...], st, MASKED)
            scores[pl.ds(pl.multiple_of(m * part + g * step, step), step), :] = st
            return jnp.maximum(peak, jnp.max(st, axis=0, keepdims=True))

        peak = jnp.full((1, count), MASKED, F32)
        for m in range(4):
            peak = lax.fori_loop(0, part // step, functools.partial(one, m=m), peak)

        def two(g, carry, m=0, h=h, peak=peak):
            total, acc = carry
            rows = pl.ds(pl.multiple_of(g * step, step), step)
            where = pl.ds(pl.multiple_of(m * part + g * step, step), step)
            p = jnp.exp(scores[where, :] - peak)
            v = kvs[m][rows, GROUP + h * HD : GROUP + (h + 1) * HD]
            return total + jnp.sum(p, axis=0, keepdims=True), acc + dot_tn(v, p.astype(BF))

        carry = (jnp.zeros((1, count), F32), jnp.zeros((HD, count), F32))
        for m in range(4):
            carry = lax.fori_loop(0, part // step, functools.partial(two, m=m), carry)
        total, acc = carry
        o = (acc / total).T
        o_full[:, h * HD : (h + 1) * HD] = o
        o_low[:, h * HD : (h + 1) * HD] = o.astype(BF)
        lse[h : h + 1, :] = peak + jnp.log(total)


def expand_kernel(sc, rest0, rest1, rest2, rest3, ids, g0, g1, g2, g3, mods, dz):
    s = sc[1]
    parts = [r[...] for r in (rest0, rest1, rest2, rest3)]
    for bit in (1, 2):
        parts = [jnp.where((s & bit) != 0, parts[i ^ bit], parts[i]) for i in range(4)]
    slots, seqs, rows, width = g0.shape
    count = slots * seqs * rows
    rest_low = parts[3]
    for i in range(3):
        mods[i] = dot(onehot(ids[:count, :], rest_low.shape[0]), parts[i])
    gate = dot(onehot(ids[...], rest_low.shape[0]), rest_low)
    mods[3] = gate[:count]
    for m, grad in enumerate((g0, g1, g2, g3)):
        for seq in range(seqs):
            for slot in range(slots):
                at = m * count + (seq * slots + slot) * rows
                g = grad[slot, seq].astype(F32)
                dz[at : at + rows, :] = (g * (1.0 + gate[at : at + rows])).astype(BF)


def project_kernel(n_w, sc, attn, tok, mods, weights, y_out, x_out, n_out, inv_out, h_out, w_out):
    width = tok.shape[-1]
    r = sc[0]
    if n_w == 1:
        w_out[...] = weights[0, 0]
    else:
        half = weights.shape[2]
        for k in range(n_w):
            for c in range(2):
                at = pl.multiple_of(2 * half * k + half * ((sc[1] & 1) ^ c), 16)
                w_out[pl.ds(at, half), :] = weights[c, k]
    full = jnp.concatenate(
        [
            jnp.concatenate([attn[2 * hg + seq] for hg in range(4)], axis=1)
            for seq in range(2)
        ],
        axis=0,
    )
    y = dot(full, w_out[...])
    y_out[...] = y
    slots, seqs, rows, _ = tok.shape
    x = jnp.concatenate(
        [tok[slot, seq] for seq in range(seqs) for slot in range(slots)], axis=0
    ).astype(F32)
    x1 = x + (1.0 + mods[0]) * y
    x_out[...] = x1
    n, inv = normalize(x1)
    n_out[...] = n
    inv_out[...] = inv
    h_out[...] = (n * (1.0 + mods[2]) + mods[1]).astype(BF)


def feed_kernel(
    n_w, sc, h0, h1, h2, h3, dz_in, weights,
    z_keep, z_send, dh_keep, dh_send, h_all, act_out, du_out, up, down,
):
    width = h0.shape[1]
    rows = width // n_w
    for k in range(n_w):
        up[rows * k : rows * (k + 1), :] = weights[k, :rows, :]
        down[rows * k : rows * (k + 1), :] = weights[k, rows : 2 * rows, :]
    h = jnp.concatenate([h0[...], h1[...], h2[...], h3[...]], axis=0)
    dz = dz_in[...]
    part = h0.shape[0]
    u = dot(h, up[...])
    square = u * u
    inner = 0.7978845608028654 * (u + 0.044715 * square * u)
    t = jnp.tanh(inner)
    act = (0.5 * u * (1.0 + t)).astype(BF)
    slope = 0.5 * (1.0 + t) + 0.5 * u * (1.0 - t * t) * (
        0.7978845608028654 * (1.0 + 3.0 * 0.044715 * square)
    )
    du = (dot_nt(dz, down[...]) * slope).astype(BF)
    dh = dot_nt(du, up[...]).astype(BF)
    for m in range(4):
        (dh_keep, dh_send)[m % 2][m // 2] = dh[m * part : (m + 1) * part]
    z = dot(act, down[...]).astype(BF)
    for m in range(4):
        (z_keep, z_send)[m % 2][m // 2] = z[m * part : (m + 1) * part]
    h_all[...] = h
    act_out[...] = act
    du_out[...] = du


def feed_grad_kernel(n_w, sc, h, dz, act, du, grads):
    rows = h.shape[1] // n_w
    up = dot_tn(h[...], du[...]).astype(BF)
    down = dot_tn(act[...], dz[...]).astype(BF)
    for k in range(n_w):
        grads[k, :rows, :] = up[rows * k : rows * (k + 1)]
        grads[k, rows:, :] = down[rows * k : rows * (k + 1)]


def middle_kernel(
    sc, dh_keep, dh_recv, dh_far, mods, n_in, inv, grad, w, dx_out, dh_out, dy_out, d_out
):
    dh = (
        dh_keep[0].astype(F32) + dh_recv[0].astype(F32) + dh_far[...].astype(F32)
    )
    slots, seqs, rows, width = grad.shape
    g = jnp.concatenate(
        [grad[slot, seq] for seq in range(seqs) for slot in range(slots)], axis=0
    ).astype(F32)
    dx = g + norm_back(dh * (1.0 + mods[2]), n_in[...], inv[...])
    dx_out[...] = dx
    dh_out[...] = dh
    dy = (dx * (1.0 + mods[0])).astype(BF)
    dy_out[...] = dy
    d = dot_nt(dy, w[...]).astype(BF)
    span = slots * rows
    for seq in range(seqs):
        for hg in range(4):
            d_out[2 * hg + seq] = d[seq * span : (seq + 1) * span, hg * GROUP : (hg + 1) * GROUP]


def middle_grad_kernel(
    n_p, rows_total, sc, dx, dh, dy, n_in, y, attn, ids_row, s_out, g_keep, g_send, g_scr
):
    sel = onehot_t(ids_row[...], rows_total)
    s_out[0] = dot(sel, (dx[...] * y[...]).astype(BF))
    s_out[1] = dot(sel, dh[...].astype(BF))
    s_out[2] = dot(sel, (dh[...] * n_in[...]).astype(BF))
    full = jnp.concatenate(
        [
            jnp.concatenate([attn[2 * hg + seq] for hg in range(4)], axis=1)
            for seq in range(2)
        ],
        axis=0,
    )
    g_scr[...] = dot_tn(full, dy[...]).astype(BF)
    if n_p == 1:
        g_keep[0] = g_scr[...]
        g_send[...] = jnp.zeros(g_send.shape, BF)
    else:
        core = sc[1] & 1
        half = g_keep.shape[1]
        for i in range(n_p):
            g_keep[i] = g_scr[pl.ds(pl.multiple_of(2 * half * i + half * core, 16), half), :]
            g_send[i] = g_scr[pl.ds(pl.multiple_of(2 * half * i + half * (1 - core), 16), half), :]


def block_kernel(rows_total, sc, z_keep, z_recv, z_far, mods, x1, grad, ids_row, out, s_out):
    z = z_keep[0].astype(F32) + z_recv[0].astype(F32) + z_far[...].astype(F32)
    slots, seqs, rows, width = grad.shape
    g = jnp.concatenate(
        [grad[slot, seq] for seq in range(seqs) for slot in range(slots)], axis=0
    ).astype(F32)
    s_out[...] = dot(onehot_t(ids_row[...], rows_total), (g * z).astype(BF))
    o = (x1[...] + (1.0 + mods[3]) * z).astype(BF)
    for seq in range(seqs):
        for slot in range(slots):
            at = (seq * slots + slot) * rows
            out[slot, seq] = o[at : at + rows]


def row_sums(x):
    return lax.dot_general(
        jnp.ones((8, x.shape[1]), F32), x, (((1,), (1,)), ((), ())),
        precision=lax.Precision.HIGHEST, preferred_element_type=F32,
    )[:1]


def attend_back_small_kernel(
    sc, q, kv0, kv1, kv2, kv3, kid, qid, o_full, lse, do, dq_out, keep, send, kv, out, acc, delta
):
    for m, part in enumerate((kv0, kv1, kv2, kv3)):
        kv[m] = part[...]
    for h in range(HEADS):
        lanes = slice(h * HD, (h + 1) * HD)
        delta[h] = row_sums(do[:, lanes].astype(F32) * o_full[:, lanes])
    acc[...] = jnp.zeros(acc.shape, F32)

    def piece(m, _):
        allowed = kid[m] <= qid[...]
        for h in range(HEADS):
            lanes = slice(h * HD, (h + 1) * HD)
            others = slice(GROUP + h * HD, GROUP + (h + 1) * HD)
            k = kv[m, :, lanes]
            p = jnp.where(allowed, jnp.exp(dot_nt(k, q[:, lanes]) - lse[h : h + 1, :]), 0.0)
            g = (p * (dot_nt(kv[m, :, others], do[:, lanes]) - delta[h])).astype(BF)
            out[m, :, lanes] = dot(g, q[:, lanes]).astype(BF)
            out[m, :, others] = dot(p.astype(BF), do[:, lanes]).astype(BF)
            acc[h] += dot_tn(k, g)
        return 0

    lax.fori_loop(0, 4, piece, 0, unroll=2)
    for h in range(HEADS):
        dq_out[:, h * HD : (h + 1) * HD] = acc[h].T * (1.0 / math.sqrt(HD))
    for m in range(4):
        (keep, send)[m % 2][m // 2] = out[m]


def attend_back_large_kernel(
    sc, q, kv0, kv1, kv2, kv3, kid, qid, o_full, lse, do, dq_out, keep, send, dqs
):
    part = kv0.shape[0]
    step = 512
    for h in range(HEADS):
        lanes = slice(h * HD, (h + 1) * HD)
        qh = q[:, lanes]
        doh = do[:, lanes]
        delta = row_sums(doh.astype(F32) * o_full[:, lanes])
        top = lse[h : h + 1, :]
        dqs[...] = jnp.zeros(dqs.shape, F32)
        for m, kv in enumerate((kv0, kv1, kv2, kv3)):
            out = (keep, send)[m % 2].at[m // 2]

            def loop(g, c, m=m, kv=kv, out=out, qh=qh, doh=doh, delta=delta, top=top, h=h):
                rows = pl.ds(pl.multiple_of(g * step, step), step)
                k = kv[rows, h * HD : (h + 1) * HD]
                v = kv[rows, GROUP + h * HD : GROUP + (h + 1) * HD]
                p = jnp.where(kid[m, rows, :] <= qid[...], jnp.exp(dot_nt(k, qh) - top), 0.0)
                g2 = (p * (dot_nt(v, doh) - delta)).astype(BF)
                out[rows, h * HD : (h + 1) * HD] = dot(g2, qh).astype(BF)
                out[rows, GROUP + h * HD : GROUP + (h + 1) * HD] = dot(p.astype(BF), doh).astype(BF)
                dqs[...] += dot_tn(k, g2)
                return c

            lax.fori_loop(0, part // step, loop, 0)
        dq_out[:, lanes] = dqs[...].T * (1.0 / math.sqrt(HD))


def qkv_back_kernel(
    blocks, fast, sc, dq, dkv_a, dkv_b, dkv_c, w, one, ids_col, cos, sin, m_out, dh_out, d_out
):
    kv = dkv_a[0].astype(F32)
    if fast:
        kv = kv + dkv_b[0].astype(F32) + dkv_c[...].astype(F32)
    kv = kv.astype(BF).astype(F32)
    q = dq[...].astype(BF).astype(F32)
    qk = turn_back(jnp.concatenate([q, kv[:, :GROUP]], axis=1), cos[...], sin[...])
    d = jnp.concatenate([qk, kv[:, GROUP:]], axis=1).astype(BF)
    d_out[...] = d
    dh = dot_nt(d, w[...])
    dh_out[...] = dh.astype(BF)
    scale = dot(onehot(ids_col[...], blocks), one[blocks:])
    m = (dh * (1.0 + scale)).astype(BF)
    part = m.shape[0] // 8
    for i in range(8):
        m_out[i] = m[i * part : (i + 1) * part]


def qkv_grad_kernel(
    blocks, seqs, fast, sc, d, dh, h, n_in, ids_row, s_out, g_keep, g_send, g_scr
):
    sel = onehot_t(ids_row[...], blocks)
    shift_sum = dot(sel, dh[...])
    scale_sum = dot(sel, (dh[...].astype(F32) * n_in[...].astype(F32)).astype(BF))
    seq = sc[2]
    for b in range(seqs):
        s_out[0, b * blocks : (b + 1) * blocks, :] = jnp.where(seq == b, shift_sum, 0.0)
        s_out[1, b * blocks : (b + 1) * blocks, :] = jnp.where(seq == b, scale_sum, 0.0)
    g_scr[:, : d.shape[1]] = dot_tn(h[...], d[...]).astype(BF)
    if fast:
        g_scr[:, d.shape[1] :] = jnp.zeros((g_scr.shape[0], g_scr.shape[1] - d.shape[1]), BF)
        c = sc[1] & 1
        half = g_keep.shape[1]
        for i in range(8):
            g_keep[i] = g_scr[pl.ds(pl.multiple_of(2 * half * i + half * c, 16), half), :]
            g_send[i] = g_scr[pl.ds(pl.multiple_of(2 * half * i + half * (1 - c), 16), half), :]
    else:
        g_keep[0] = g_scr[...]
        g_send[...] = jnp.zeros(g_send.shape, BF)


def last_kernel(sc, m_in, tok, dx, out):
    slots, seqs, rows, width = tok.shape
    span = slots * rows
    for seq in range(seqs):
        m = m_in[seq].astype(F32)
        for hg in range(1, 4):
            m = m + m_in[2 * hg + seq].astype(F32)
        x = jnp.concatenate([tok[slot, seq] for slot in range(slots)], axis=0).astype(F32)
        n, inv = normalize(x)
        o = dx[seq * span : (seq + 1) * span, :] + norm_back(m, n, inv)
        for slot in range(slots):
            out[slot, seq] = o[slot * rows : (slot + 1) * rows]


def finish_kernel(sc, p0, p1, p2, p3, up, down):
    s = sc[1]
    rows = p0.shape[0] // 2
    width = p0.shape[1]
    parts = [p0, p1, p2, p3]
    for m in range(4):
        down[pl.ds(pl.multiple_of(rows * (s ^ m), 8), rows), :] = parts[m][rows : 2 * rows, :].astype(F32)
    ups = [p[:rows, :].astype(F32) for p in parts]
    for bit in (1, 2):
        ups = [jnp.where((s & bit) != 0, ups[i ^ bit], ups[i]) for i in range(4)]
    quarter = up.shape[1] // 4 // (width // rows)
    n_c = up.shape[1] // (4 * quarter)
    for c in range(n_c):
        up[:, 4 * quarter * c : 4 * quarter * (c + 1)] = jnp.concatenate(
            [u[:, quarter * c : quarter * (c + 1)] for u in ups], axis=1
        )


def finish_qkv_kernel(sc, own, other, out, proj):
    s = sc[1]
    hg = sc[0] // 2
    half = own.shape[2]
    for c, part in enumerate((own, other)):
        where = pl.ds(pl.multiple_of(half * ((s & 1) ^ c), 8), half)
        swapped = (s & 2) != 0
        low = [jnp.where(swapped, part[1, m].astype(F32), part[0, m].astype(F32)) for m in range(4)]
        high = [jnp.where(swapped, part[0, m].astype(F32), part[1, m].astype(F32)) for m in range(4)]
        low_out, high_out = part[0, 4].astype(F32), part[1, 4].astype(F32)
        proj[where, :] = jnp.concatenate(
            [jnp.where(swapped, high_out, low_out), jnp.where(swapped, low_out, high_out)], axis=1
        )
        for bit in (1, 2):
            flip = (hg & bit) != 0
            low = [jnp.where(flip, low[i ^ bit], low[i]) for i in range(4)]
            high = [jnp.where(flip, high[i ^ bit], high[i]) for i in range(4)]
        out[where, :] = jnp.concatenate(
            [x[:, :GROUP] for x in low]
            + [x[:, GROUP : 2 * GROUP] for x in low]
            + [x[:, :GROUP] for x in high],
            axis=1,
        )


def swap(x, axis, k, size):
    return lax.ppermute(x, axis, [(i, i ^ k) for i in range(size)])


def after(x, *others):
    return lax.optimization_barrier((x,) + others)[0]


def gather_sp(x, ready=None):
    far = swap(x, "sp", 2, 4)
    if ready is not None:
        far = after(far, ready)
    return [x, swap(x, "sp", 1, 4), far, swap(far, "sp", 1, 4)]


def body(
    tokens, out_grad, time_table, time_index, span_order, block_ids,
    w_ada, b_ada, w_qkv, w_out, w_up, w_down,
):
    slots, seqs, rows, width = tokens.shape
    cp = lax.axis_size("cp")
    fast = cp == 8
    groups = cp // 8
    r = lax.axis_index("cp")
    s = lax.axis_index("sp")
    j = r % 8
    group = r // 8
    seq = j % 2
    hg = j // 2
    span = slots * rows
    span_rows = 4 * rows
    blocks = time_index.shape[1]
    mod_rows = seqs * blocks
    part_rows = width // cp
    total_slots = slots * cp
    hidden = w_up.shape[1]
    count = 8 * span
    sc = jnp.stack([r, s, seq]).astype(jnp.int32)
    exchange_groups = None if fast else [[8 * g + i for i in range(8)] for g in range(groups)]

    def all_to_all(x):
        return lax.all_to_all(
            x, "cp", split_axis=0, concat_axis=0, tiled=True, axis_index_groups=exchange_groups
        )

    spans = span_order.astype(jnp.int32)
    pick = (spans[:, None] == jnp.arange(total_slots, dtype=jnp.int32)[None, :]).astype(BF)
    slot_ids = jnp.einsum(
        "ns,bst->bnt",
        pick,
        block_ids.reshape(seqs, total_slots, span_rows).astype(BF),
        preferred_element_type=F32,
    ).astype(jnp.int32)
    slot_ids = slot_ids.reshape(seqs, total_slots, 4, rows)
    own_seq = lax.dynamic_index_in_dim(slot_ids, seq, 0, keepdims=False)
    key_ids = jnp.stack(
        [
            lax.dynamic_index_in_dim(own_seq, s ^ m, 1, keepdims=False).reshape(-1)
            for m in range(4)
        ]
    )
    query_ids = lax.dynamic_slice_in_dim(key_ids[0], group * count, count, 0)
    here = lax.dynamic_slice_in_dim(slot_ids, slots * r, slots, 1)
    all_ids = jnp.concatenate(
        [
            (
                lax.dynamic_index_in_dim(here, s ^ m, 2, keepdims=False).reshape(seqs, span)
                + blocks * jnp.arange(seqs, dtype=jnp.int32)[:, None]
            ).reshape(-1)
            for m in range(4)
        ]
    )
    token_ids = all_ids[: seqs * span]
    own_spans = lax.dynamic_slice_in_dim(spans, 8 * slots * group, 8 * slots, 0)
    positions = (
        own_spans[:, None] * span_rows + s * rows + jnp.arange(rows, dtype=jnp.int32)[None, :]
    ).reshape(-1)
    lane = jnp.arange(128, dtype=jnp.int32) % HD
    frequency = jnp.exp(
        -math.log(10000.0) * 2.0 * (lane % (HD // 2)).astype(F32) / HD
    )
    angles = positions.astype(F32)[:, None] * frequency[None, :]
    cosine = jnp.cos(angles)
    sine = jnp.where(lane < HD // 2, -1.0, 1.0)[None, :] * jnp.sin(angles)

    pick_time = (
        time_index.reshape(-1)[:, None] == jnp.arange(time_table.shape[0], dtype=jnp.int32)
    ).astype(F32)
    table_part = lax.dynamic_slice_in_dim(time_table, part_rows * r, part_rows, 1)
    cond = jax.nn.silu(
        jnp.dot(pick_time, table_part, precision=lax.Precision.HIGHEST)
    ).astype(BF)
    owner = jnp.arange(6 * width, dtype=jnp.int32) // b_ada.shape[0]
    bias = jnp.where(owner == r, jnp.tile(b_ada.astype(F32), cp), 0.0)[None, :]

    if fast:
        quarter_rows = part_rows // 4
        wq = w_qkv
        extra = 2 * blocks + mod_rows + quarter_rows
    else:
        wq = w_qkv
        extra = 0
    inner = hidden // cp // 4
    if fast:
        send, shard = call(
            functools.partial(pack_kernel, mod_rows, seqs),
            [((8, span + extra, width), BF), ((part_rows + inner, width), BF)],
            [sc, tokens, cond, w_ada, bias, wq, w_up, w_down],
            name="pack",
        )
    else:
        send = jnp.broadcast_to(
            tokens.transpose(1, 0, 2, 3).reshape(1, seqs, span, width), (4, seqs, span, width)
        ).reshape(8, span, width)
        up_part = lax.dynamic_index_in_dim(
            w_up.reshape(part_rows, cp, 4, inner), s, 2, keepdims=False
        ).reshape(part_rows, cp * inner)
        down_part = lax.dynamic_slice_in_dim(w_down, inner * s, inner, 0)
        shard = jnp.concatenate([up_part, down_part], axis=0)
    grad_parts = gather_sp(out_grad)
    got = after(all_to_all(send), *grad_parts)
    if fast:
        w_own = got[:, span + extra - quarter_rows :, :].reshape(8 * quarter_rows, width)
        rest = got[:, span + 2 * blocks : span + 2 * blocks + mod_rows, :].astype(F32)
        w_list = gather_sp(
            jnp.concatenate([w_own, jnp.sum(rest, axis=0).astype(BF)], axis=0)
        )
        rests = [w[8 * quarter_rows :] for w in w_list]
        mod_one = got
    else:
        full_mod = lax.psum(
            jnp.dot(cond, w_ada, preferred_element_type=F32) + bias, "cp"
        )
        first = lax.dynamic_slice_in_dim(full_mod, seq * blocks, blocks, 0)
        mod_one = jnp.concatenate([first[:, :width], first[:, width : 2 * width]], axis=0)
        gathered = lax.all_gather(w_qkv, "cp", axis=0, tiled=True).reshape(width, 3, 4, GROUP)
        w_list = [
            lax.dynamic_index_in_dim(gathered, hg, 2, keepdims=False).reshape(width, 3 * GROUP)
        ]

    n_w = 8 if fast else 1
    weights = lax.all_gather(after(shard, got) if fast else shard, "cp", axis=0, tiled=False)
    if fast:
        half = part_rows // 2
        w_own = lax.dynamic_slice_in_dim(w_out, half * (s % 2), half, 0)
        w_proj = all_to_all(jnp.broadcast_to(after(w_own, got)[None], (8, half, width)))
    else:
        w_proj = lax.all_gather(w_out, "cp", axis=0, tiled=True)[None, None]
        weights = jnp.concatenate(
            [
                weights[:, at : at + part_rows].reshape(width, width)
                for at in (0, part_rows)
            ],
            axis=0,
        )[None]

    mod_kernel_outs = [
        ((count, GROUP), BF),
        ((count, 2 * GROUP), BF),
        ((count, width), BF),
        ((count, width), BF),
        ((width, 3 * GROUP), BF),
        ((2 * blocks, width), BF),
    ]
    q, kv, h_one, n_one, w_heads, one = call(
        functools.partial(qkv_kernel, blocks, span, fast, len(w_list)),
        mod_kernel_outs,
        [sc, got, mod_one, query_ids[:, None], cosine, sine] + w_list,
        scratch=[((width, 3 * GROUP), F32)],
        name="qkv",
    )
    if not fast:
        kv = lax.all_gather(
            kv, "cp", axis=0, tiled=True,
            axis_index_groups=[[8 * g + i for g in range(groups)] for i in range(8)],
        )
    key_col = key_ids[:, :, None]
    kvs = gather_sp(kv, key_col)
    if fast:
        w_proj = jnp.stack([w_proj, swap(w_proj, "sp", 1, 4)])
    query_row = query_ids[None, :]
    part = kv.shape[0]
    wide_kv = ((4, part, 2 * GROUP), BF)
    attn, attn_full, lse = call(
        attend_small_kernel if fast else attend_large_kernel,
        [((count, GROUP), BF), ((count, GROUP), F32), ((8, count), F32)],
        [sc, q] + kvs + [key_col, query_row],
        scratch=[
            wide_kv,
            ((4, HEADS, part, count), F32),
            ((HEADS, HD, count), F32),
            ((HEADS, 1, count), F32),
            ((HEADS, 1, count), F32),
        ]
        if fast
        else [((4 * part, count), F32)],
        name="attend",
    )
    if not fast:
        tail = full_mod.astype(BF)
        rests = [
            lax.dynamic_slice_in_dim(tail, (2 + (s ^ m)) * width, width, 1) for m in range(4)
        ]
    mods, dz = call(
        expand_kernel,
        [((4, 2 * span, width), F32), ((8 * span, width), BF)],
        [sc] + rests + [all_ids[:, None]] + [after(grad_parts[0], attn)]
        + grad_parts[1:],
        name="expand",
    )
    attn_tok = all_to_all(attn.reshape(8, span, GROUP))
    y, x_mid, n_two, inv_two, h_two, w_out_full = call(
        functools.partial(project_kernel, n_w),
        [
            ((2 * span, width), F32),
            ((2 * span, width), F32),
            ((2 * span, width), F32),
            ((2 * span, 1), F32),
            ((2 * span, width), BF),
            ((width, width), BF),
        ],
        [sc, attn_tok, tokens, mods, w_proj],
        name="project",
    )
    hs = gather_sp(h_two)
    pair = ((2, 2 * span, width), BF)
    tall = ((8 * span, width), BF)
    z_keep, z_send, dh_keep, dh_send, h_all, act, du = call(
        functools.partial(feed_kernel, n_w),
        [pair, pair, pair, pair, tall, tall, tall],
        [sc] + hs + [dz, weights],
        scratch=[((width, width), BF)] * 2,
        name="feed",
    )
    def reduce_sp(keep, send, *wait):
        near = swap(send, "sp", 1, 4)
        if wait:
            near = after(near, *wait)
        both = (keep[1].astype(F32) + near[1].astype(F32)).astype(BF)
        return (keep, near, swap(both, "sp", 2, 4)), both

    dh_parts, dh_both = reduce_sp(dh_keep, dh_send)
    token_row = token_ids[None, :]
    g_out = ((8, part_rows // 2, width), BF) if fast else ((1, width, width), BF)
    wide = ((2 * span, width), F32)
    dx_mid, dh_two, dy, d_attn = call(
        middle_kernel,
        [wide, wide, ((2 * span, width), BF), ((8, span, GROUP), BF)],
        [sc] + list(dh_parts)
        + [mods, n_two, inv_two, out_grad, w_out_full],
        name="middle",
    )
    half_width = width // 2
    far = s // 2

    def split_far(mine, theirs):
        part = (mine.astype(F32) + theirs.astype(F32)).astype(BF)
        return (
            lax.dynamic_slice_in_dim(part, half_width * far, half_width, 2),
            lax.dynamic_slice_in_dim(part, half_width * (1 - far), half_width, 2),
        )

    def split_y(mine, theirs):
        part = (mine.astype(F32) + theirs.astype(F32)).astype(BF)
        part = part.reshape((4, 2) + part.shape[1:])
        return (
            lax.dynamic_index_in_dim(part, seq, 1, keepdims=False),
            lax.dynamic_index_in_dim(part, 1 - seq, 1, keepdims=False),
        )

    d_heads = all_to_all(d_attn).reshape(count, GROUP)
    if fast:
        pass
    (g_feed,) = call(
        functools.partial(feed_grad_kernel, n_w),
        [((n_w, 2 * width // n_w, width), BF)],
        [sc, h_all, dz, after(act, d_heads), du],
        name="feed_grad",
    )
    if fast:
        feed = lax.psum_scatter(g_feed, "cp", scatter_dimension=0, tiled=False)
    else:
        feed = jnp.concatenate(
            [
                lax.psum_scatter(
                    g_feed[0, at : at + width].astype(F32), "cp", scatter_dimension=0, tiled=True
                )
                for at in (0, width)
            ],
            axis=0,
        )

    if fast:
        d_heads = after(d_heads, g_feed)
    dkv = ((2, part, 2 * GROUP), BF)
    dq, kv_keep, kv_send = call(
        attend_back_small_kernel if fast else attend_back_large_kernel,
        [((count, GROUP), F32), dkv, dkv],
        [sc, q] + kvs + [key_col, query_row, attn_full, lse, d_heads],
        scratch=[wide_kv, wide_kv, ((HEADS, HD, count), F32), ((HEADS, 1, count), F32)]
        if fast
        else [((HD, count), F32)],
        name="attend_back",
    )
    s_mid, o_keep, o_send = call(
        functools.partial(middle_grad_kernel, n_w, mod_rows),
        [((3, mod_rows, width), F32), g_out, g_out],
        [sc, dx_mid, dh_two, dy, n_two, after(y, dq), attn_tok, token_row],
        scratch=[((width, width), BF)],
        name="middle_grad",
    )
    if fast:
        o_near = swap(o_send, "sp", 1, 4)
    dkv_list, _ = reduce_sp(kv_keep, kv_send)
    if not fast:
        summed = sum(x.astype(F32) for x in (dkv_list[0][0], dkv_list[1][0], dkv_list[2]))
        summed = lax.psum_scatter(
            summed, "cp", scatter_dimension=0, tiled=True,
            axis_index_groups=[[8 * g + i for g in range(groups)] for i in range(8)],
        ).astype(BF)
        dkv_list = [summed[None], summed[None], summed]
    g_shape = ((8, part_rows // 2, width), BF) if fast else ((1, width, 3 * GROUP), BF)
    m_one, dh_one, dqkv = call(
        functools.partial(qkv_back_kernel, blocks, fast),
        [((8, span, width), BF), ((count, width), BF), ((count, 3 * GROUP), BF)],
        [sc, dq] + list(dkv_list) + [w_heads, one, query_ids[:, None], cosine, sine],
        name="qkv_back",
    )
    m_tok = all_to_all(m_one)
    z_parts, _ = reduce_sp(z_keep, after(z_send, dh_both), m_one)
    block_out, s_gate = call(
        functools.partial(block_kernel, mod_rows),
        [(tokens.shape, BF), ((mod_rows, width), F32)],
        [sc] + list(z_parts) + [mods, after(x_mid, m_one), out_grad, token_row],
        name="block",
    )
    s_one, q_keep, q_send = call(
        functools.partial(qkv_grad_kernel, blocks, seqs, fast),
        [((2, mod_rows, width), F32), g_shape, g_shape],
        [sc, dqkv, dh_one, h_one, n_one, query_row],
        scratch=[((width, width if fast else 3 * GROUP), BF)],
        name="qkv_grad",
    )
    shares = gather_sp(feed.reshape(2 * part_rows, width)) if fast else []
    (grad_in,) = call(
        last_kernel,
        [(tokens.shape, F32)],
        [sc, m_tok, tokens, dx_mid],
        name="last",
    )

    def reduce_all(x, wait=None):
        if not fast:
            return lax.psum(x, ("cp", "sp"))
        for axis, k, size in (("sp", 1, 4), ("sp", 2, 4), ("cp", 1, 8), ("cp", 2, 8), ("cp", 4, 8)):
            if axis == "cp" and k == 2:
                x = after(x, wait)
            low = x.astype(BF)
            x = low.astype(F32) + swap(low, axis, k, size).astype(F32)
        return x

    sums = reduce_all(jnp.concatenate([s_one, s_mid, s_gate[None]], axis=0), m_tok)
    sums = sums.transpose(1, 0, 2).reshape(mod_rows, 6 * width)
    grad_ada = lax.dot_general(
        cond.astype(F32), sums, (((0,), (0,)), ((), ())), precision=lax.Precision.HIGHEST
    )
    grad_bias = lax.dynamic_slice_in_dim(
        jnp.sum(sums, axis=0), b_ada.shape[0] * r, b_ada.shape[0], 0
    )

    if fast:
        o_mine, o_theirs = split_y(o_keep, after(o_near, dq))
        o_mine, o_theirs = split_far(o_mine, after(swap(o_theirs, "cp", 1, 8), m_one))
        mine, theirs = split_far(q_keep, swap(q_send, "sp", 1, 4))
        got_far = swap(jnp.concatenate([theirs, o_theirs], axis=0), "sp", 2, 4)
        mine, theirs = split_y(mine, after(got_far, feed)[:8])
        mine = (mine.astype(F32) + swap(theirs, "cp", 1, 8).astype(F32)).astype(BF)
        o_mine = (o_mine.astype(F32) + got_far[8:].astype(F32)).astype(BF)
        pick = [
            jnp.stack([lax.dynamic_index_in_dim(x, hg ^ m, 0, keepdims=False) for x in (mine, o_mine)])
            for m in range(4)
        ]
        parts = [pick[0]] + [swap(pick[m], "cp", 2 * m, 8) for m in (1, 2, 3)]
        proj = sum(p[1].astype(F32) for p in parts).astype(BF)
        found = after(jnp.stack([p[0] for p in parts] + [proj]), m_tok)
        found = jnp.stack([found, swap(found, "sp", 2, 4)])
        found = [found, swap(found, "sp", 1, 4)]
        grad_qkv, grad_out = call(
            finish_qkv_kernel,
            [((part_rows, 3 * width), F32), ((part_rows, width), F32)],
            [sc] + found,
            name="finish_qkv",
        )
    else:
        proj = lax.psum_scatter(o_keep[0].astype(F32), "cp", scatter_dimension=0, tiled=True)
        proj_low = lax.psum(proj, "sp")
        own = lax.psum_scatter(q_keep[0].astype(F32), "sp", scatter_dimension=1, tiled=True)
        placed = lax.dynamic_update_slice(
            jnp.zeros((4, width, 3 * GROUP // 4), F32), own[None], (hg, 0, 0)
        )
        placed = lax.psum_scatter(placed, "cp", scatter_dimension=1, tiled=True)
        whole = lax.all_gather(placed, "sp", axis=2, tiled=True)
        grad_qkv = (
            whole.reshape(4, part_rows, 3, GROUP).transpose(1, 2, 0, 3).reshape(part_rows, 3 * width)
        )
    if fast:
        grad_up, grad_down = call(
            finish_kernel,
            [
                ((part_rows, hidden), F32),
                ((hidden // cp, width), F32),
            ],
            [sc] + shares,
            name="finish",
        )
    else:
        shares = lax.all_gather(feed, "sp", axis=0, tiled=False)
        grad_up = (
            shares[:, :part_rows]
            .reshape(4, part_rows, cp, inner)
            .transpose(1, 2, 0, 3)
            .reshape(part_rows, hidden)
        )
        grad_down = shares[:, part_rows:].reshape(hidden // cp, width)
        grad_out = proj_low
    return (
        block_out, grad_in, grad_ada, grad_bias, grad_qkv, grad_out, grad_up, grad_down,
    )


def solution(mesh):
    rows = P("cp", None, "sp", None)
    shard = P("cp", None)
    return jax.shard_map(
        body,
        mesh=mesh,
        in_specs=(
            rows, rows, P(), P(), P(), P(), shard, P("cp"), shard, shard, shard, shard,
        ),
        out_specs=(rows, rows, shard, P("cp"), shard, shard, shard, shard),
        check_vma=False,
    )
```
